128 devices in a mesh: expert: 16 (over x, y), head: 8 (over z, core).
Axes of the slice: x: 4, y: 4, z: 4, core: 2. Of those that a mesh axis runs over, the one named last changes fastest.
Arguments:
- table_cells: bfloat16 [8192, 2, 2048], P(('expert', 'head')), may hold values from -8 to 8
- w_query: bfloat16 [2048, 2048], P(None, 'head')
- w_key: bfloat16 [2048, 2048], P(None, 'head')
- w_value: bfloat16 [2048, 2048], P(None, 'head'), may hold values from -0.125 to 0.125
- w_out: bfloat16 [2048, 2048], P('head'), may hold values from -0.125 to 0.125
- norm_gain: bfloat16 [2048], replicated, may hold values from 0.099609375 to 1.8984375
- w_gate: bfloat16 [128, 704, 2048], P(('expert', 'head')), may hold values from -0.125 to 0.125
- w_up: bfloat16 [128, 704, 2048], P(('expert', 'head')), may hold values from -0.125 to 0.125
- w_down: bfloat16 [128, 704, 2048], P(('expert', 'head')), may hold values from -0.15625 to 0.15625
- lengths: int32 [2], replicated, may hold values from 2048 to 8192, as said below
- expert_of_cell: int32 [8192, 2], P(('expert', 'head')), may hold values from 0 to 63, as said below
- slot_of_cell: int32 [8192, 2], P(('expert', 'head')), may hold values from 0 to 3, as said below
Outputs:
- updated_cells: bfloat16 [8192, 2, 2048], P(('expert', 'head'))
The draws below stay inside these ranges and needn't reach their ends.
Inputs may be any that keep to these rules, and one draw needn't show every extreme that they name: `lengths`: one table in every draw has all 8192 cells. `expert_of_cell`: within the 128 cells of one device (aligned blocks in row-major order), no expert has more than 4 cells, and in every draw one expert has exactly 4 cells in every device's block. `slot_of_cell`: cells of one device with the same expert have distinct slots.
All inputs are finite; a program needn't handle non-finite values.
Results may differ from the reference program's by a relative error of at most 0.014.
Values may be sent and summed in bfloat16 or wider, within the bound.
A program may use at most 128 MiB of HBM per device.

```python
import math
import jax
import jax.numpy as jnp
from jax import lax

D = 2048
HEADS = 16
DH = 128
FF = 1408
CELLS_DEV = 64
SEQS = 2
BLOCKS = 128
EXPERTS = 64
CAP = 4
HALF = 704
LENGTH = 8192
N_HEAD = 8


def draw_table_cells(key, part):
    base_key = jax.random.fold_in(key, 3)
    first_key = jax.random.fold_in(base_key, 0)
    shape = (LENGTH, SEQS, D)
    drawn = jnp.clip(jax.random.normal(first_key, shape, jnp.float32), -6.0, 6.0)
    return drawn.astype(jnp.bfloat16)


def attention_pair(key):
    base_key = jax.random.fold_in(key, 11)
    first_key, second_key = jax.random.split(base_key)
    shape = (D, HEADS * DH)
    spread = 1.6 / math.sqrt(D)
    first = jax.random.normal(first_key, shape, jnp.float32) * spread
    second = jax.random.normal(second_key, shape, jnp.float32) * spread
    return (first, second)


def draw_w_query(key, part):
    return attention_pair(key)[0].astype(jnp.bfloat16)


def draw_w_key(key, part):
    return attention_pair(key)[1].astype(jnp.bfloat16)


def draw_lengths(key, part):
    base_key = jax.random.fold_in(key, 5)
    first_key, second_key = jax.random.split(base_key)
    drawn_lengths = jax.random.randint(first_key, (SEQS,), LENGTH // 4, LENGTH + 1)
    full_table = jax.random.randint(second_key, (), 0, SEQS)
    return jnp.where(jnp.arange(SEQS, dtype=jnp.int32) == full_table, LENGTH, drawn_lengths).astype(jnp.int32)


def routing(key):
    base_key = jax.random.fold_in(key, 23)
    hot_key, block_key = jax.random.split(base_key)
    hot_expert = jax.random.randint(hot_key, (), 0, EXPERTS)
    block_keys = jax.random.split(block_key, BLOCKS)
    cell_index = jnp.arange(EXPERTS * CAP, dtype=jnp.int32).reshape(EXPERTS, CAP)

    def one_block(single_key):
        level_key, jitter_key, order_key = jax.random.split(single_key, 3)
        levels = jax.random.randint(level_key, (EXPERTS,), 0, 4)
        levels = jnp.where(jnp.arange(EXPERTS, dtype=jnp.int32) == hot_expert, 8, levels)
        jitter = jax.random.randint(jitter_key, (EXPERTS, CAP), 0, 1024)
        ranking = ((levels[:, None] * 1024 + jitter) * (EXPERTS * CAP) + cell_index).reshape(-1)
        chosen = lax.top_k(ranking, CELLS_DEV * SEQS)[1]
        chosen = chosen[jax.random.permutation(order_key, CELLS_DEV * SEQS)]
        return (chosen // CAP, chosen % CAP)
    experts_drawn, slots_drawn = jax.vmap(one_block)(block_keys)
    return (experts_drawn.reshape(LENGTH, SEQS).astype(jnp.int32), slots_drawn.reshape(LENGTH, SEQS).astype(jnp.int32))


def draw_expert_of_cell(key, part):
    return routing(key)[0]


def draw_slot_of_cell(key, part):
    return routing(key)[1]


def steps_of(rng, dims, shards, low, top_value):
    level = 1.0
    for dim, shards_of in shards:
        heights = jax.random.uniform(jax.random.fold_in(jax.random.fold_in(rng, 6), dim), (shards_of,), jnp.float32, low / len(shards), top_value / len(shards))
        level = level * jnp.repeat(jnp.exp(heights), dims[dim] // shards_of).reshape((-1,) + (1,) * (len(dims) - 1 - dim))
    return level


def centred(rng, dims, scale, most, cuts=(), held_as=jnp.bfloat16):
    array = jax.random.normal(rng, dims, jnp.float32) * scale
    if len(cuts) > 0:
        array = steps_of(rng, dims, cuts, -0.22, 0.18) * array
    return jnp.clip(array, min=-most, max=most).astype(held_as)


def setup_inputs(seed: int = 0) -> dict:
    streams_of = jax.random.split(jax.random.key(seed), 13)
    table_cells = draw_table_cells(jax.random.fold_in(streams_of[12], 71), 0)
    w_query = draw_w_query(jax.random.fold_in(streams_of[12], 71), 0)
    w_key = draw_w_key(jax.random.fold_in(streams_of[12], 71), 0)
    w_value = centred(streams_of[3], (D, HEADS * DH), D ** -0.5, 0.125, ((1, 8),))
    w_out = centred(streams_of[4], (HEADS * DH, D), (HEADS * DH) ** -0.5, 0.125, ((0, 8),))
    norm_gain = jnp.clip(1.0 + 0.18 * jax.random.normal(streams_of[5], (D,), jnp.float32), 0.099609375, 1.8984375).astype(jnp.bfloat16)
    w_gate = centred(streams_of[6], (2 * EXPERTS, HALF, D), D ** -0.5, 0.125, ((0, 128),))
    w_up = centred(streams_of[7], (2 * EXPERTS, HALF, D), D ** -0.5, 0.125, ((0, 128),))
    w_down = centred(streams_of[8], (2 * EXPERTS, HALF, D), FF ** -0.5, 0.15625, ((0, 128),))
    lengths = draw_lengths(jax.random.fold_in(streams_of[12], 71), 0)
    expert_of_cell = draw_expert_of_cell(jax.random.fold_in(streams_of[12], 71), 0)
    slot_of_cell = draw_slot_of_cell(jax.random.fold_in(streams_of[12], 71), 0)
    return dict(table_cells=table_cells, w_query=w_query, w_key=w_key, w_value=w_value, w_out=w_out, norm_gain=norm_gain, w_gate=w_gate, w_up=w_up, w_down=w_down, lengths=lengths, expert_of_cell=expert_of_cell, slot_of_cell=slot_of_cell)


def attend_head(query_head, key_head, value_head, length):
    scores = jnp.dot(query_head, key_head.T, preferred_element_type=jnp.float32) * (1.0 / math.sqrt(DH))
    position = jnp.arange(query_head.shape[0], dtype=jnp.int32)
    scores = jnp.where(position[None, :] < length, scores, -jnp.inf)
    row_top = lax.optimization_barrier(jnp.max(scores, axis=-1, keepdims=True))
    exp_scores = jnp.exp(scores - row_top)
    denominator = lax.optimization_barrier(jnp.sum(exp_scores, axis=-1, keepdims=True))
    result = jnp.dot(exp_scores.astype(jnp.bfloat16), value_head, preferred_element_type=jnp.float32) / denominator
    result = jnp.where(position[:, None] < length, result, 0.0)
    return result.astype(jnp.bfloat16)

def run_expert(group_item):
    slot_rows, gate_pair, up_pair, down_pair = group_item
    summed = jnp.zeros((slot_rows.shape[0], D), jnp.float32)
    for half_index in range(2):
        gate_t = jnp.dot(gate_pair[half_index], slot_rows.T, preferred_element_type=jnp.float32)
        up_t = jnp.dot(up_pair[half_index], slot_rows.T, preferred_element_type=jnp.float32)
        hidden = (jax.nn.silu(gate_t) * up_t).astype(jnp.bfloat16)
        partial_value = jnp.dot(hidden.T, down_pair[half_index], preferred_element_type=jnp.float32).astype(jnp.bfloat16)
        summed = summed + partial_value.astype(jnp.float32)
    return summed.astype(jnp.bfloat16)

def reference(table_cells, w_query, w_key, w_value, w_out, norm_gain, w_gate, w_up, w_down, lengths, expert_of_cell, slot_of_cell):
    flat_cells = table_cells.reshape(LENGTH * SEQS, D)

    def heads_of(weight):
        projected = jnp.dot(flat_cells, weight, preferred_element_type=jnp.float32).astype(jnp.bfloat16)
        projected = projected.reshape(LENGTH, SEQS, HEADS, DH).transpose(1, 2, 0, 3)
        return projected.reshape(SEQS * HEADS, LENGTH, DH)
    queries = heads_of(w_query)
    key_rows = heads_of(w_key)
    value_rows = heads_of(w_value)
    length_rows = jnp.repeat(lengths, HEADS)
    attended = lax.map(lambda group_item: attend_head(*group_item), (queries, key_rows, value_rows, length_rows))
    attended = attended.reshape(SEQS, HEADS, LENGTH, DH).transpose(2, 0, 1, 3).reshape(LENGTH * SEQS, HEADS * DH)
    group_width = HEADS // N_HEAD * DH
    summed = jnp.zeros((LENGTH * SEQS, D), jnp.float32)
    for group_index in range(N_HEAD):
        lower = group_index * group_width
        partial_value = jnp.dot(attended[:, lower:lower + group_width], w_out[lower:lower + group_width], preferred_element_type=jnp.float32).astype(jnp.bfloat16)
        summed = summed + partial_value.astype(jnp.float32)
    residual = flat_cells.astype(jnp.float32) + summed
    mean_square = lax.optimization_barrier(jnp.mean(residual * residual, axis=-1, keepdims=True))
    normed = (residual * lax.rsqrt(mean_square + 1e-06) * norm_gain.astype(jnp.float32)).astype(jnp.bfloat16)
    device_of = jnp.arange(LENGTH * SEQS, dtype=jnp.int32) // (CELLS_DEV * SEQS)
    slot_place = device_of * (EXPERTS * CAP) + expert_of_cell.reshape(-1).astype(jnp.int32) * CAP + slot_of_cell.reshape(-1).astype(jnp.int32)
    buffer = jnp.zeros((BLOCKS * EXPERTS * CAP, D), jnp.bfloat16).at[slot_place].add(normed)
    buffer = buffer.reshape(BLOCKS, EXPERTS, CAP, D).transpose(1, 0, 2, 3).reshape(EXPERTS, BLOCKS * CAP, D)
    gate_pairs = w_gate.reshape(EXPERTS, 2, FF // 2, D)
    up_pairs = w_up.reshape(EXPERTS, 2, FF // 2, D)
    down_pairs = w_down.reshape(EXPERTS, 2, FF // 2, D)
    results = lax.map(run_expert, (buffer, gate_pairs, up_pairs, down_pairs))
    results = results.reshape(EXPERTS, BLOCKS, CAP, D).transpose(1, 0, 2, 3).reshape(BLOCKS * EXPERTS * CAP, D)
    expert_out = results[slot_place]
    updated = (residual + expert_out.astype(jnp.float32)).astype(jnp.bfloat16)
    return updated.reshape(LENGTH, SEQS, D)
```

```python
import functools
import math

import jax
import jax.numpy as jnp
from jax import lax
from jax.experimental import pallas as pl
from jax.experimental.pallas import tpu as pltpu

from jax.sharding import PartitionSpec as P

DH = 128
KEY_BLOCK = 512


def flash_body(scalars, q_ref, k_ref, v_ref, o_ref, m_ref, l_ref, acc_ref, *, scale, key_block):
    s = pl.program_id(0)
    j = pl.program_id(2)
    last = pl.num_programs(2) - 1
    length = scalars[s]
    start = j * key_block

    @pl.when(j == 0)
    def _():
        m_ref[...] = jnp.full(m_ref.shape, -1e30, jnp.float32)
        l_ref[...] = jnp.zeros(l_ref.shape, jnp.float32)
        acc_ref[...] = jnp.zeros(acc_ref.shape, jnp.float32)

    def update(masked):
        q = q_ref[...]
        k = k_ref[...]
        scores = lax.dot_general(
            q, k, (((1,), (1,)), ((), ())), preferred_element_type=jnp.float32
        ) * scale
        if masked:
            cols = start + lax.broadcasted_iota(jnp.int32, scores.shape, 1)
            scores = jnp.where(cols < length, scores, -jnp.inf)
        m_prev = m_ref[...]
        m_new = jnp.maximum(m_prev, jnp.max(scores, axis=1, keepdims=True))
        alpha = jnp.exp(m_prev - m_new)
        p = jnp.exp(scores - m_new[:, :1])
        l_ref[...] = alpha * l_ref[...] + jnp.sum(p, axis=1, keepdims=True)
        acc_ref[...] = acc_ref[...] * alpha + jnp.dot(
            p.astype(jnp.bfloat16), v_ref[...], preferred_element_type=jnp.float32
        )
        m_ref[...] = m_new

    @pl.when(start + key_block <= length)
    def _():
        update(False)

    @pl.when(jnp.logical_and(start < length, start + key_block > length))
    def _():
        update(True)

    @pl.when(j == last)
    def _():
        rows = scalars[2] + lax.broadcasted_iota(jnp.int32, acc_ref.shape, 0)
        out = acc_ref[...] / l_ref[...]
        o_ref[...] = jnp.where(rows < length, out, 0.0).astype(o_ref.dtype)


def flash_attention(scalars, q_all, kv_all, heads, scale):
    rows = q_all.shape[0]
    keys = kv_all.shape[0]
    tables = scalars.shape[0] - 1
    key_block = KEY_BLOCK
    nk = keys // key_block

    def clamp(j, sc, s):
        return jnp.minimum(j, (sc[s] - 1) // key_block)

    grid_spec = pltpu.PrefetchScalarGridSpec(
        num_scalar_prefetch=1,
        grid=(tables, heads, nk),
        in_specs=[
            pl.BlockSpec((rows, DH), lambda s, h, j, sc: (0, s * heads + h)),
            pl.BlockSpec((key_block, DH), lambda s, h, j, sc: (clamp(j, sc, s), s * 2 * heads + h)),
            pl.BlockSpec(
                (key_block, DH), lambda s, h, j, sc: (clamp(j, sc, s), s * 2 * heads + heads + h)
            ),
        ],
        out_specs=pl.BlockSpec((rows, DH), lambda s, h, j, sc: (0, s * heads + h)),
        scratch_shapes=[
            pltpu.VMEM((rows, DH), jnp.float32),
            pltpu.VMEM((rows, DH), jnp.float32),
            pltpu.VMEM((rows, DH), jnp.float32),
        ],
    )
    flops = 4 * tables * heads * rows * keys * DH
    return pl.pallas_call(
        functools.partial(flash_body, scale=scale, key_block=key_block),
        grid_spec=grid_spec,
        out_shape=jax.ShapeDtypeStruct((rows, tables * heads * DH), jnp.bfloat16),
        compiler_params=pltpu.CompilerParams(
            dimension_semantics=("arbitrary", "arbitrary", "arbitrary")
        ),
        cost_estimate=pl.CostEstimate(
            flops=flops,
            transcendentals=tables * heads * rows * keys,
            bytes_accessed=2 * (q_all.size * 2 + kv_all.size),
        ),
    )(scalars, q_all, kv_all, kv_all)


def expert_half(slot_rows, gate_half, up_half, down_half):
    contract_rows = (((1,), (1,)), ((), ()))
    gate_t = lax.dot_general(
        gate_half, slot_rows, contract_rows, preferred_element_type=jnp.float32
    )
    up_t = lax.dot_general(up_half, slot_rows, contract_rows, preferred_element_type=jnp.float32)
    hidden = (jax.nn.silu(gate_t) * up_t).astype(jnp.bfloat16)
    product = lax.dot_general(
        hidden, down_half, (((0,), (0,)), ((), ())), preferred_element_type=jnp.float32
    )
    return product.astype(jnp.bfloat16)


def shards(
    table_cells,
    w_query,
    w_key,
    w_value,
    w_out,
    norm_gain,
    w_gate,
    w_up,
    w_down,
    lengths,
    expert_of_cell,
    slot_of_cell,
):
    cell_count, tables, model_width = table_cells.shape
    head_width = w_query.shape[1]
    head_count = head_width // DH
    score_scale = 1.0 / math.sqrt(DH)
    shard_rows = lax.all_gather(table_cells, "head", axis=0, tiled=True)
    row_cells = shard_rows.shape[0]
    flat_rows = shard_rows.reshape(row_cells * tables, model_width)
    q_all = (
        jnp.dot(flat_rows, w_query, preferred_element_type=jnp.float32)
        .astype(jnp.bfloat16)
        .reshape(row_cells, tables * head_width)
    )
    kv_weight = jnp.concatenate([w_key, w_value], axis=1)
    kv_rows = (
        jnp.dot(flat_rows, kv_weight, preferred_element_type=jnp.float32)
        .astype(jnp.bfloat16)
        .reshape(row_cells, tables * 2 * head_width)
    )
    kv_all = lax.all_gather(kv_rows, "expert", axis=0, tiled=True)
    offset = lax.axis_index("expert") * row_cells
    scalars = jnp.concatenate(
        [lengths.astype(jnp.int32), jnp.reshape(offset, (1,)).astype(jnp.int32)]
    )
    attended = flash_attention(scalars, q_all, kv_all, head_count, score_scale)
    count_rows = cell_count * lax.axis_size("head")
    product = jnp.dot(
        attended.reshape(count_rows * tables, head_width), w_out, preferred_element_type=jnp.float32
    )
    summed = lax.psum_scatter(
        product.reshape(count_rows, tables, model_width).astype(jnp.bfloat16),
        "head",
        scatter_dimension=0,
        tiled=True,
    ).astype(jnp.float32)
    residual = table_cells.astype(jnp.float32) + summed
    mean_square = jnp.mean(residual * residual, axis=-1, keepdims=True)
    normed = (residual * lax.rsqrt(mean_square + 1e-06) * norm_gain.astype(jnp.float32)).astype(
        jnp.bfloat16
    )
    rows_dev = cell_count * tables
    normed_rows = normed.reshape(rows_dev, model_width)
    expert_count = lax.axis_size("expert") * lax.axis_size("head") // 2
    slot_cap = 2 * max(1, rows_dev // expert_count)
    target = expert_of_cell.reshape(rows_dev) * slot_cap + slot_of_cell.reshape(rows_dev)
    slot_table = (
        jnp.arange(expert_count * slot_cap, dtype=jnp.int32)[:, None] == target[None, :]
    ).astype(jnp.bfloat16)
    send_rows = jnp.dot(slot_table, normed_rows, preferred_element_type=jnp.float32).astype(
        jnp.bfloat16
    )
    gate_half = w_gate[0]
    up_half = w_up[0]
    down_half = w_down[0]
    doubled = jnp.repeat(send_rows.reshape(expert_count, slot_cap, model_width), 2, axis=0)
    received = lax.all_to_all(doubled, ("expert", "head"), split_axis=0, concat_axis=0, tiled=True)
    sources = received.shape[0]
    item_count = received.shape[1]
    flat_rows = received.reshape(sources * item_count, model_width)
    gathered = lax.all_to_all(
        expert_half(flat_rows, gate_half, up_half, down_half).reshape(
            sources, item_count, model_width
        ),
        ("expert", "head"),
        split_axis=0,
        concat_axis=0,
        tiled=True,
    )
    halves = gathered.reshape(expert_count, 2, slot_cap, model_width).astype(jnp.float32)
    combined = (
        (halves[:, 0] + halves[:, 1])
        .astype(jnp.bfloat16)
        .reshape(expert_count * slot_cap, model_width)
    )
    expert_out = lax.dot_general(
        slot_table, combined, (((0,), (0,)), ((), ())), preferred_element_type=jnp.float32
    )
    updated = (residual.reshape(rows_dev, model_width) + expert_out).astype(jnp.bfloat16)
    return updated.reshape(cell_count, tables, model_width)


def solution(mesh):
    placed = (
        P(("expert", "head"), None, None),
        P(None, "head"),
        P(None, "head"),
        P(None, "head"),
        P("head", None),
        P(),
        P(("expert", "head"), None, None),
        P(("expert", "head"), None, None),
        P(("expert", "head"), None, None),
        P(),
        P(("expert", "head"), None),
        P(("expert", "head"), None),
    )
    return jax.shard_map(
        shards,
        mesh=mesh,
        in_specs=placed,
        out_specs=P(("expert", "head"), None, None),
        check_vma=False,
    )
```

```python
import functools
import math

import jax
import jax.numpy as jnp
from jax import lax
from jax.experimental import pallas as pl
from jax.experimental.pallas import tpu as pltpu

from jax.sharding import PartitionSpec as P

DH = 128
KEY_BLOCK = 512


def flash_body(scalars, q_ref, k_ref, v_ref, o_ref, m_ref, l_ref, acc_ref, *, scale, key_block):
    j = pl.program_id(1)
    last = pl.num_programs(1) - 1
    length = scalars[0]
    start = j * key_block

    @pl.when(j == 0)
    def _():
        m_ref[...] = jnp.full(m_ref.shape, -1e30, jnp.float32)
        l_ref[...] = jnp.zeros(l_ref.shape, jnp.float32)
        acc_ref[...] = jnp.zeros(acc_ref.shape, jnp.float32)

    def update(masked):
        q = q_ref[...]
        k = k_ref[...]
        scores = lax.dot_general(
            q, k, (((1,), (1,)), ((), ())), preferred_element_type=jnp.float32
        ) * scale
        if masked:
            cols = start + lax.broadcasted_iota(jnp.int32, scores.shape, 1)
            scores = jnp.where(cols < length, scores, -jnp.inf)
        m_prev = m_ref[...]
        m_new = jnp.maximum(m_prev, jnp.max(scores, axis=1, keepdims=True))
        alpha = jnp.exp(m_prev - m_new)
        p = jnp.exp(scores - m_new[:, :1])
        l_ref[...] = alpha * l_ref[...] + jnp.sum(p, axis=1, keepdims=True)
        acc_ref[...] = acc_ref[...] * alpha + jnp.dot(
            p.astype(jnp.bfloat16), v_ref[...], preferred_element_type=jnp.float32
        )
        m_ref[...] = m_new

    @pl.when(start + key_block <= length)
    def _():
        update(False)

    @pl.when(jnp.logical_and(start < length, start + key_block > length))
    def _():
        update(True)

    @pl.when(j == last)
    def _():
        rows = scalars[1] + lax.broadcasted_iota(jnp.int32, acc_ref.shape, 0)
        out = acc_ref[...] / l_ref[...]
        o_ref[...] = jnp.where(rows < length, out, 0.0).astype(o_ref.dtype)


def flash_attention(scalars, q_all, kv_all, heads, scale, table):
    rows = q_all.shape[0]
    keys = kv_all.shape[0]
    key_block = KEY_BLOCK
    nk = keys // key_block

    def clamp(j, sc):
        return jnp.minimum(j, (sc[0] - 1) // key_block)

    grid_spec = pltpu.PrefetchScalarGridSpec(
        num_scalar_prefetch=1,
        grid=(heads, nk),
        in_specs=[
            pl.BlockSpec((rows, DH), lambda h, j, sc: (0, table * heads + h)),
            pl.BlockSpec((key_block, DH), lambda h, j, sc: (clamp(j, sc), h)),
            pl.BlockSpec((key_block, DH), lambda h, j, sc: (clamp(j, sc), heads + h)),
        ],
        out_specs=pl.BlockSpec((rows, DH), lambda h, j, sc: (0, h)),
        scratch_shapes=[
            pltpu.VMEM((rows, DH), jnp.float32),
            pltpu.VMEM((rows, DH), jnp.float32),
            pltpu.VMEM((rows, DH), jnp.float32),
        ],
    )
    flops = 4 * heads * rows * keys * DH
    return pl.pallas_call(
        functools.partial(flash_body, scale=scale, key_block=key_block),
        grid_spec=grid_spec,
        out_shape=jax.ShapeDtypeStruct((rows, heads * DH), jnp.bfloat16),
        compiler_params=pltpu.CompilerParams(dimension_semantics=("arbitrary", "arbitrary")),
        cost_estimate=pl.CostEstimate(
            flops=flops,
            transcendentals=heads * rows * keys,
            bytes_accessed=2 * (rows * heads * DH * 2 + kv_all.size),
        ),
    )(scalars, q_all, kv_all, kv_all)


def expert_half(slot_rows, gate_half, up_half, down_half):
    contract_rows = (((1,), (1,)), ((), ()))
    gate_t = lax.dot_general(
        gate_half, slot_rows, contract_rows, preferred_element_type=jnp.float32
    )
    up_t = lax.dot_general(up_half, slot_rows, contract_rows, preferred_element_type=jnp.float32)
    hidden = (jax.nn.silu(gate_t) * up_t).astype(jnp.bfloat16)
    product = lax.dot_general(
        hidden, down_half, (((0,), (0,)), ((), ())), preferred_element_type=jnp.float32
    )
    return product.astype(jnp.bfloat16)


def shards(
    table_cells,
    w_query,
    w_key,
    w_value,
    w_out,
    norm_gain,
    w_gate,
    w_up,
    w_down,
    lengths,
    expert_of_cell,
    slot_of_cell,
):
    cell_count, tables, model_width = table_cells.shape
    head_width = w_query.shape[1]
    head_count = head_width // DH
    score_scale = 1.0 / math.sqrt(DH)
    shard_rows = lax.all_gather(table_cells, "head", axis=0, tiled=True)
    row_cells = shard_rows.shape[0]
    flat_rows = shard_rows.reshape(row_cells * tables, model_width)
    q_all = (
        jnp.dot(flat_rows, w_query, preferred_element_type=jnp.float32)
        .astype(jnp.bfloat16)
        .reshape(row_cells, tables * head_width)
    )
    kv_weight = jnp.concatenate([w_key, w_value], axis=1)
    kv_rows = (
        jnp.dot(flat_rows, kv_weight, preferred_element_type=jnp.float32)
        .astype(jnp.bfloat16)
        .reshape(row_cells, tables * 2 * head_width)
    )
    offset = lax.axis_index("expert") * row_cells
    count_rows = cell_count * lax.axis_size("head")
    summed_tables = []
    for table in range(tables):
        scalars = jnp.stack(
            [lengths[table].astype(jnp.int32), jnp.asarray(offset, jnp.int32)]
        )
        kv_piece = kv_rows[:, table * 2 * head_width : (table + 1) * 2 * head_width]
        kv_all = lax.all_gather(kv_piece, "expert", axis=0, tiled=True)
        attended = flash_attention(scalars, q_all, kv_all, head_count, score_scale, table)
        product = jnp.dot(attended, w_out, preferred_element_type=jnp.float32)
        summed_tables.append(
            lax.psum_scatter(
                product.astype(jnp.bfloat16), "head", scatter_dimension=0, tiled=True
            ).astype(jnp.float32)
        )
    summed = jnp.stack(summed_tables, axis=1)
    residual = table_cells.astype(jnp.float32) + summed
    mean_square = jnp.mean(residual * residual, axis=-1, keepdims=True)
    normed = (residual * lax.rsqrt(mean_square + 1e-06) * norm_gain.astype(jnp.float32)).astype(
        jnp.bfloat16
    )
    rows_dev = cell_count * tables
    normed_rows = normed.reshape(rows_dev, model_width)
    expert_count = lax.axis_size("expert") * lax.axis_size("head") // 2
    slot_cap = 2 * max(1, rows_dev // expert_count)
    target = expert_of_cell.reshape(rows_dev) * slot_cap + slot_of_cell.reshape(rows_dev)
    slot_table = (
        jnp.arange(expert_count * slot_cap, dtype=jnp.int32)[:, None] == target[None, :]
    ).astype(jnp.bfloat16)
    send_rows = jnp.dot(slot_table, normed_rows, preferred_element_type=jnp.float32).astype(
        jnp.bfloat16
    )
    gate_half = w_gate[0]
    up_half = w_up[0]
    down_half = w_down[0]
    doubled = jnp.repeat(send_rows.reshape(expert_count, slot_cap, model_width), 2, axis=0)
    received = lax.all_to_all(doubled, ("expert", "head"), split_axis=0, concat_axis=0, tiled=True)
    sources = received.shape[0]
    item_count = received.shape[1]
    flat_rows = received.reshape(sources * item_count, model_width)
    gathered = lax.all_to_all(
        expert_half(flat_rows, gate_half, up_half, down_half).reshape(
            sources, item_count, model_width
        ),
        ("expert", "head"),
        split_axis=0,
        concat_axis=0,
        tiled=True,
    )
    halves = gathered.reshape(expert_count, 2, slot_cap, model_width).astype(jnp.float32)
    combined = (
        (halves[:, 0] + halves[:, 1])
        .astype(jnp.bfloat16)
        .reshape(expert_count * slot_cap, model_width)
    )
    expert_out = lax.dot_general(
        slot_table, combined, (((0,), (0,)), ((), ())), preferred_element_type=jnp.float32
    )
    updated = (residual.reshape(rows_dev, model_width) + expert_out).astype(jnp.bfloat16)
    return updated.reshape(cell_count, tables, model_width)


def solution(mesh):
    placed = (
        P(("expert", "head"), None, None),
        P(None, "head"),
        P(None, "head"),
        P(None, "head"),
        P("head", None),
        P(),
        P(("expert", "head"), None, None),
        P(("expert", "head"), None, None),
        P(("expert", "head"), None, None),
        P(),
        P(("expert", "head"), None),
        P(("expert", "head"), None),
    )
    return jax.shard_map(
        shards,
        mesh=mesh,
        in_specs=placed,
        out_specs=P(("expert", "head"), None, None),
        check_vma=False,
    )
```

```python
import functools
import math

import jax
import jax.numpy as jnp
from jax import lax
from jax.experimental import pallas as pl
from jax.experimental.pallas import tpu as pltpu

from jax.sharding import PartitionSpec as P

DH = 128
KEY_BLOCK = 512
QUERY_BLOCK = 1024


def flash_body(scalars, q_ref, k_ref, v_ref, o_ref, m_ref, l_ref, acc_ref, *, scale, key_block):
    j = pl.program_id(1)
    last = pl.num_programs(1) - 1
    length = scalars[0]
    start = j * key_block

    @pl.when(j == 0)
    def _():
        m_ref[...] = jnp.full(m_ref.shape, -1e30, jnp.float32)
        l_ref[...] = jnp.zeros(l_ref.shape, jnp.float32)
        acc_ref[...] = jnp.zeros(acc_ref.shape, jnp.float32)

    def update(masked):
        scores = lax.dot_general(
            q_ref[...], k_ref[...], (((1,), (1,)), ((), ())), preferred_element_type=jnp.float32
        ) * scale
        if masked:
            cols = start + lax.broadcasted_iota(jnp.int32, scores.shape, 1)
            scores = jnp.where(cols < length, scores, -jnp.inf)
        m_prev = m_ref[...]
        m_new = jnp.maximum(m_prev, jnp.max(scores, axis=1, keepdims=True))
        alpha = jnp.exp(m_prev - m_new)
        p = jnp.exp(scores - m_new[:, :1])
        l_ref[...] = alpha * l_ref[...] + jnp.sum(p, axis=1, keepdims=True)
        acc_ref[...] = acc_ref[...] * alpha + jnp.dot(
            p.astype(jnp.bfloat16), v_ref[...], preferred_element_type=jnp.float32
        )
        m_ref[...] = m_new

    @pl.when(start + key_block <= length)
    def _():
        update(False)

    @pl.when(jnp.logical_and(start < length, start + key_block > length))
    def _():
        update(True)

    @pl.when(j == last)
    def _():
        o_ref[...] = (acc_ref[...] / l_ref[...]).astype(o_ref.dtype)


def flash_attention(scalars, q_rows, kv_rows, scale):
    rows = q_rows.shape[0]
    keys = kv_rows.shape[0]
    key_block = KEY_BLOCK
    query_block = min(rows, QUERY_BLOCK)
    nk = keys // key_block

    def clamp(j, sc):
        return jnp.minimum(j, (sc[0] - 1) // key_block)

    grid_spec = pltpu.PrefetchScalarGridSpec(
        num_scalar_prefetch=1,
        grid=(rows // query_block, nk),
        in_specs=[
            pl.BlockSpec((query_block, DH), lambda i, j, sc: (i, 0)),
            pl.BlockSpec((key_block, DH), lambda i, j, sc: (clamp(j, sc), 0)),
            pl.BlockSpec((key_block, DH), lambda i, j, sc: (clamp(j, sc), 1)),
        ],
        out_specs=pl.BlockSpec((query_block, DH), lambda i, j, sc: (i, 0)),
        scratch_shapes=[
            pltpu.VMEM((query_block, DH), jnp.float32),
            pltpu.VMEM((query_block, DH), jnp.float32),
            pltpu.VMEM((query_block, DH), jnp.float32),
        ],
    )
    return pl.pallas_call(
        functools.partial(flash_body, scale=scale, key_block=key_block),
        grid_spec=grid_spec,
        out_shape=jax.ShapeDtypeStruct((rows, DH), jnp.bfloat16),
        compiler_params=pltpu.CompilerParams(dimension_semantics=("arbitrary", "arbitrary")),
        cost_estimate=pl.CostEstimate(
            flops=4 * rows * keys * DH,
            transcendentals=rows * keys,
            bytes_accessed=2 * (2 * rows * DH + kv_rows.size * (rows // query_block)),
        ),
    )(scalars, q_rows, kv_rows, kv_rows)


def expert_half(slot_rows, gate_half, up_half, down_half):
    contract_rows = (((1,), (1,)), ((), ()))
    gate_t = lax.dot_general(
        gate_half, slot_rows, contract_rows, preferred_element_type=jnp.float32
    )
    up_t = lax.dot_general(up_half, slot_rows, contract_rows, preferred_element_type=jnp.float32)
    hidden = (jax.nn.silu(gate_t) * up_t).astype(jnp.bfloat16)
    product = lax.dot_general(
        hidden, down_half, (((0,), (0,)), ((), ())), preferred_element_type=jnp.float32
    )
    return product.astype(jnp.bfloat16)


def shards(
    table_cells,
    w_query,
    w_key,
    w_value,
    w_out,
    norm_gain,
    w_gate,
    w_up,
    w_down,
    lengths,
    expert_of_cell,
    slot_of_cell,
):
    cell_count, tables, model_width = table_cells.shape
    head_width = w_query.shape[1]
    head_count = head_width // DH
    score_scale = 1.0 / math.sqrt(DH)
    shard_rows = lax.all_gather(table_cells, "head", axis=0, tiled=True)
    row_cells = shard_rows.shape[0]
    flat_rows = shard_rows.reshape(row_cells * tables, model_width)
    pairs = tables * head_count
    expert_size = lax.axis_size("expert")
    quarters = expert_size // pairs
    me = lax.axis_index("expert")
    q_pairs = (
        jnp.dot(flat_rows, w_query, preferred_element_type=jnp.float32)
        .astype(jnp.bfloat16)
        .reshape(row_cells, pairs, DH)
    )
    kv_weight = jnp.concatenate(
        [w_key.reshape(model_width, head_count, DH), w_value.reshape(model_width, head_count, DH)],
        axis=2,
    ).reshape(model_width, 2 * head_width)
    kv_pairs = (
        jnp.dot(flat_rows, kv_weight, preferred_element_type=jnp.float32)
        .astype(jnp.bfloat16)
        .reshape(row_cells, pairs, 2 * DH)
        .transpose(1, 0, 2)
    )
    send = jnp.repeat(kv_pairs, quarters, axis=0)
    kv_here = lax.all_to_all(send, "expert", 0, 0, tiled=True).reshape(
        expert_size * row_cells, 2 * DH
    )
    my_pair = me // quarters
    my_part = me % quarters
    q_parts = []
    for shift in range(quarters):
        perm = [
            (src, quarters * ((src % quarters + shift) % quarters) + src // quarters)
            for src in range(expert_size)
        ]
        sent_pair = (my_part + shift) % quarters
        q_parts.append(
            lax.ppermute(
                lax.dynamic_index_in_dim(q_pairs, sent_pair, axis=1, keepdims=False),
                "expert",
                perm,
            )
        )
    q_stack = jnp.stack(q_parts)
    q_rows = jnp.take(q_stack, (my_pair - jnp.arange(quarters)) % quarters, axis=0)
    scalars = jnp.reshape(lengths[my_pair // head_count], (1,)).astype(jnp.int32)
    out_rows = flash_attention(
        scalars, q_rows.reshape(quarters * row_cells, DH), kv_here, score_scale
    ).reshape(quarters, row_cells, DH)
    back_parts = []
    for shift in range(quarters):
        perm = [
            (quarters * ((src % quarters + shift) % quarters) + src // quarters, src)
            for src in range(expert_size)
        ]
        source_slot = (my_pair - shift) % quarters
        back_parts.append(
            lax.ppermute(
                lax.dynamic_index_in_dim(out_rows, source_slot, axis=0, keepdims=False),
                "expert",
                perm,
            )
        )
    back_stack = jnp.stack(back_parts)
    attended = jnp.take(back_stack, (jnp.arange(pairs) - my_part) % quarters, axis=0)
    positions = me * row_cells + jnp.arange(row_cells, dtype=jnp.int32)
    live = positions[:, None] < lengths[None, :]
    attended = attended.reshape(tables, head_count, row_cells, DH).transpose(2, 0, 1, 3)
    attended = jnp.where(live[:, :, None, None], attended, jnp.zeros_like(attended))
    count_rows = cell_count * lax.axis_size("head")
    product = jnp.dot(
        attended.reshape(count_rows * tables, head_width), w_out, preferred_element_type=jnp.float32
    )
    summed = lax.psum_scatter(
        product.reshape(count_rows, tables, model_width).astype(jnp.bfloat16),
        "head",
        scatter_dimension=0,
        tiled=True,
    ).astype(jnp.float32)
    residual = table_cells.astype(jnp.float32) + summed
    mean_square = jnp.mean(residual * residual, axis=-1, keepdims=True)
    normed = (residual * lax.rsqrt(mean_square + 1e-06) * norm_gain.astype(jnp.float32)).astype(
        jnp.bfloat16
    )
    rows_dev = cell_count * tables
    normed_rows = normed.reshape(rows_dev, model_width)
    expert_count = lax.axis_size("expert") * lax.axis_size("head") // 2
    slot_cap = 2 * max(1, rows_dev // expert_count)
    target = expert_of_cell.reshape(rows_dev) * slot_cap + slot_of_cell.reshape(rows_dev)
    slot_table = (
        jnp.arange(expert_count * slot_cap, dtype=jnp.int32)[:, None] == target[None, :]
    ).astype(jnp.bfloat16)
    send_rows = jnp.dot(slot_table, normed_rows, preferred_element_type=jnp.float32).astype(
        jnp.bfloat16
    )
    gate_half = w_gate[0]
    up_half = w_up[0]
    down_half = w_down[0]
    doubled = jnp.repeat(send_rows.reshape(expert_count, slot_cap, model_width), 2, axis=0)
    received = lax.all_to_all(doubled, ("expert", "head"), split_axis=0, concat_axis=0, tiled=True)
    sources = received.shape[0]
    item_count = received.shape[1]
    flat_rows = received.reshape(sources * item_count, model_width)
    gathered = lax.all_to_all(
        expert_half(flat_rows, gate_half, up_half, down_half).reshape(
            sources, item_count, model_width
        ),
        ("expert", "head"),
        split_axis=0,
        concat_axis=0,
        tiled=True,
    )
    halves = gathered.reshape(expert_count, 2, slot_cap, model_width).astype(jnp.float32)
    combined = (
        (halves[:, 0] + halves[:, 1])
        .astype(jnp.bfloat16)
        .reshape(expert_count * slot_cap, model_width)
    )
    expert_out = lax.dot_general(
        slot_table, combined, (((0,), (0,)), ((), ())), preferred_element_type=jnp.float32
    )
    updated = (residual.reshape(rows_dev, model_width) + expert_out).astype(jnp.bfloat16)
    return updated.reshape(cell_count, tables, model_width)


def solution(mesh):
    placed = (
        P(("expert", "head"), None, None),
        P(None, "head"),
        P(None, "head"),
        P(None, "head"),
        P("head", None),
        P(),
        P(("expert", "head"), None, None),
        P(("expert", "head"), None, None),
        P(("expert", "head"), None, None),
        P(),
        P(("expert", "head"), None),
        P(("expert", "head"), None),
    )
    return jax.shard_map(
        shards,
        mesh=mesh,
        in_specs=placed,
        out_specs=P(("expert", "head"), None, None),
        check_vma=False,
    )
```

```python
import functools
import math

import jax
import jax.numpy as jnp
from jax import lax
from jax.experimental import pallas as pl
from jax.experimental.pallas import tpu as pltpu

from jax.sharding import PartitionSpec as P

DH = 128
KEY_BLOCK = 4096


def flash_body(scalars, q_ref, k_ref, v_ref, o_ref, m_ref, l_ref, acc_ref, *, scale, key_block):
    s = pl.program_id(0)
    j = pl.program_id(2)
    last = pl.num_programs(2) - 1
    length = scalars[s]
    start = j * key_block

    @pl.when(j == 0)
    def _():
        m_ref[...] = jnp.full(m_ref.shape, -1e30, jnp.float32)
        l_ref[...] = jnp.zeros(l_ref.shape, jnp.float32)
        acc_ref[...] = jnp.zeros(acc_ref.shape, jnp.float32)

    def update(masked):
        q = q_ref[...]
        k = k_ref[...]
        scores = lax.dot_general(
            q, k, (((1,), (1,)), ((), ())), preferred_element_type=jnp.float32
        ) * scale
        if masked:
            cols = start + lax.broadcasted_iota(jnp.int32, scores.shape, 1)
            scores = jnp.where(cols < length, scores, -jnp.inf)
        m_prev = m_ref[...]
        m_new = jnp.maximum(m_prev, jnp.max(scores, axis=1, keepdims=True))
        alpha = jnp.exp(m_prev - m_new)
        p = jnp.exp(scores - m_new[:, :1])
        l_ref[...] = alpha * l_ref[...] + jnp.sum(p, axis=1, keepdims=True)
        acc_ref[...] = acc_ref[...] * alpha + jnp.dot(
            p.astype(jnp.bfloat16), v_ref[...], preferred_element_type=jnp.float32
        )
        m_ref[...] = m_new

    @pl.when(start + key_block <= length)
    def _():
        update(False)

    @pl.when(jnp.logical_and(start < length, start + key_block > length))
    def _():
        update(True)

    @pl.when(j == last)
    def _():
        rows = scalars[2] + lax.broadcasted_iota(jnp.int32, acc_ref.shape, 0)
        out = acc_ref[...] / l_ref[...]
        o_ref[...] = jnp.where(rows < length, out, 0.0).astype(o_ref.dtype)


def flash_attention(scalars, q_all, kv_all, heads, scale):
    rows = q_all.shape[0]
    keys = kv_all.shape[0]
    tables = scalars.shape[0] - 1
    key_block = KEY_BLOCK
    nk = keys // key_block

    def clamp(j, sc, s):
        return jnp.minimum(j, (sc[s] - 1) // key_block)

    grid_spec = pltpu.PrefetchScalarGridSpec(
        num_scalar_prefetch=1,
        grid=(tables, heads, nk),
        in_specs=[
            pl.BlockSpec((rows, DH), lambda s, h, j, sc: (0, s * heads + h)),
            pl.BlockSpec((key_block, DH), lambda s, h, j, sc: (clamp(j, sc, s), s * 2 * heads + h)),
            pl.BlockSpec(
                (key_block, DH), lambda s, h, j, sc: (clamp(j, sc, s), s * 2 * heads + heads + h)
            ),
        ],
        out_specs=pl.BlockSpec((rows, DH), lambda s, h, j, sc: (0, s * heads + h)),
        scratch_shapes=[
            pltpu.VMEM((rows, DH), jnp.float32),
            pltpu.VMEM((rows, DH), jnp.float32),
            pltpu.VMEM((rows, DH), jnp.float32),
        ],
    )
    flops = 4 * tables * heads * rows * keys * DH
    return pl.pallas_call(
        functools.partial(flash_body, scale=scale, key_block=key_block),
        grid_spec=grid_spec,
        out_shape=jax.ShapeDtypeStruct((rows, tables * heads * DH), jnp.bfloat16),
        compiler_params=pltpu.CompilerParams(
            dimension_semantics=("arbitrary", "arbitrary", "arbitrary")
        ),
        cost_estimate=pl.CostEstimate(
            flops=flops,
            transcendentals=tables * heads * rows * keys,
            bytes_accessed=2 * (q_all.size * 2 + kv_all.size),
        ),
    )(scalars, q_all, kv_all, kv_all)


def expert_half(slot_rows, gate_half, up_half, down_half):
    contract_rows = (((1,), (1,)), ((), ()))
    gate_t = lax.dot_general(
        gate_half, slot_rows, contract_rows, preferred_element_type=jnp.float32
    )
    up_t = lax.dot_general(up_half, slot_rows, contract_rows, preferred_element_type=jnp.float32)
    hidden = (jax.nn.silu(gate_t) * up_t).astype(jnp.bfloat16)
    product = lax.dot_general(
        hidden, down_half, (((0,), (0,)), ((), ())), preferred_element_type=jnp.float32
    )
    return product.astype(jnp.bfloat16)


def shards(
    table_cells,
    w_query,
    w_key,
    w_value,
    w_out,
    norm_gain,
    w_gate,
    w_up,
    w_down,
    lengths,
    expert_of_cell,
    slot_of_cell,
):
    cell_count, tables, model_width = table_cells.shape
    head_width = w_query.shape[1]
    head_count = head_width // DH
    score_scale = 1.0 / math.sqrt(DH)
    shard_rows = lax.all_gather(table_cells, "head", axis=0, tiled=True)
    row_cells = shard_rows.shape[0]
    flat_rows = shard_rows.reshape(row_cells * tables, model_width)
    q_all = (
        jnp.dot(flat_rows, w_query, preferred_element_type=jnp.float32)
        .astype(jnp.bfloat16)
        .reshape(row_cells, tables * head_width)
    )
    kv_weight = jnp.concatenate([w_key, w_value], axis=1)
    kv_rows = (
        jnp.dot(flat_rows, kv_weight, preferred_element_type=jnp.float32)
        .astype(jnp.bfloat16)
        .reshape(row_cells, tables * 2 * head_width)
    )
    kv_all = lax.all_gather(kv_rows, "expert", axis=0, tiled=True)
    offset = lax.axis_index("expert") * row_cells
    scalars = jnp.concatenate(
        [lengths.astype(jnp.int32), jnp.reshape(offset, (1,)).astype(jnp.int32)]
    )
    attended = flash_attention(scalars, q_all, kv_all, head_count, score_scale)
    count_rows = cell_count * lax.axis_size("head")
    product = jnp.dot(
        attended.reshape(count_rows * tables, head_width), w_out, preferred_element_type=jnp.float32
    )
    summed = lax.psum_scatter(
        product.reshape(count_rows, tables, model_width).astype(jnp.bfloat16),
        "head",
        scatter_dimension=0,
        tiled=True,
    ).astype(jnp.float32)
    residual = table_cells.astype(jnp.float32) + summed
    mean_square = jnp.mean(residual * residual, axis=-1, keepdims=True)
    normed = (residual * lax.rsqrt(mean_square + 1e-06) * norm_gain.astype(jnp.float32)).astype(
        jnp.bfloat16
    )
    rows_dev = cell_count * tables
    normed_rows = normed.reshape(rows_dev, model_width)
    expert_count = lax.axis_size("expert") * lax.axis_size("head") // 2
    slot_cap = 2 * max(1, rows_dev // expert_count)
    target = expert_of_cell.reshape(rows_dev) * slot_cap + slot_of_cell.reshape(rows_dev)
    slot_table = (
        jnp.arange(expert_count * slot_cap, dtype=jnp.int32)[:, None] == target[None, :]
    ).astype(jnp.bfloat16)
    send_rows = jnp.dot(slot_table, normed_rows, preferred_element_type=jnp.float32).astype(
        jnp.bfloat16
    )
    gate_half = w_gate[0]
    up_half = w_up[0]
    down_half = w_down[0]
    doubled = jnp.repeat(send_rows.reshape(expert_count, slot_cap, model_width), 2, axis=0)
    received = lax.all_to_all(doubled, ("expert", "head"), split_axis=0, concat_axis=0, tiled=True)
    sources = received.shape[0]
    item_count = received.shape[1]
    flat_rows = received.reshape(sources * item_count, model_width)
    gathered = lax.all_to_all(
        expert_half(flat_rows, gate_half, up_half, down_half).reshape(
            sources, item_count, model_width
        ),
        ("expert", "head"),
        split_axis=0,
        concat_axis=0,
        tiled=True,
    )
    halves = gathered.reshape(expert_count, 2, slot_cap, model_width).astype(jnp.float32)
    combined = (
        (halves[:, 0] + halves[:, 1])
        .astype(jnp.bfloat16)
        .reshape(expert_count * slot_cap, model_width)
    )
    expert_out = lax.dot_general(
        slot_table, combined, (((0,), (0,)), ((), ())), preferred_element_type=jnp.float32
    )
    updated = (residual.reshape(rows_dev, model_width) + expert_out).astype(jnp.bfloat16)
    return updated.reshape(cell_count, tables, model_width)


def solution(mesh):
    placed = (
        P(("expert", "head"), None, None),
        P(None, "head"),
        P(None, "head"),
        P(None, "head"),
        P("head", None),
        P(),
        P(("expert", "head"), None, None),
        P(("expert", "head"), None, None),
        P(("expert", "head"), None, None),
        P(),
        P(("expert", "head"), None),
        P(("expert", "head"), None),
    )
    return jax.shard_map(
        shards,
        mesh=mesh,
        in_specs=placed,
        out_specs=P(("expert", "head"), None, None),
        check_vma=False,
    )
```

```python
import functools
import math

import jax
import jax.numpy as jnp
from jax import lax
from jax.experimental import pallas as pl
from jax.experimental.pallas import tpu as pltpu

from jax.sharding import PartitionSpec as P

DH = 128
KEY_BLOCK = 4096


def flash_body(scalars, q_ref, k_ref, v_ref, o_ref, m_ref, l_ref, acc_ref, *, scale, key_block):
    s = pl.program_id(0)
    j = pl.program_id(2)
    last = pl.num_programs(2) - 1
    length = scalars[s]
    start = j * key_block

    @pl.when(j == 0)
    def _():
        m_ref[...] = jnp.full(m_ref.shape, -1e30, jnp.float32)
        l_ref[...] = jnp.zeros(l_ref.shape, jnp.float32)
        acc_ref[...] = jnp.zeros(acc_ref.shape, jnp.float32)

    def update(masked):
        q = q_ref[...]
        k = k_ref[...]
        scores = lax.dot_general(
            q, k, (((1,), (1,)), ((), ())), preferred_element_type=jnp.float32
        ) * scale
        if masked:
            cols = start + lax.broadcasted_iota(jnp.int32, scores.shape, 1)
            scores = jnp.where(cols < length, scores, -jnp.inf)
        m_prev = m_ref[...]
        m_new = jnp.maximum(m_prev, jnp.max(scores, axis=1, keepdims=True))
        alpha = jnp.exp(m_prev - m_new)
        p = jnp.exp(scores - m_new[:, :1])
        l_ref[...] = alpha * l_ref[...] + jnp.sum(p, axis=1, keepdims=True)
        acc_ref[...] = acc_ref[...] * alpha + jnp.dot(
            p.astype(jnp.bfloat16), v_ref[...], preferred_element_type=jnp.float32
        )
        m_ref[...] = m_new

    @pl.when(start + key_block <= length)
    def _():
        update(False)

    @pl.when(jnp.logical_and(start < length, start + key_block > length))
    def _():
        update(True)

    @pl.when(j == last)
    def _():
        rows = scalars[2] + lax.broadcasted_iota(jnp.int32, acc_ref.shape, 0)
        out = acc_ref[...] / l_ref[...]
        o_ref[...] = jnp.where(rows < length, out, 0.0).astype(o_ref.dtype)


def flash_attention(scalars, q_all, kv_all, heads, scale):
    rows = q_all.shape[0]
    keys = kv_all.shape[0]
    tables = scalars.shape[0] - 1
    key_block = KEY_BLOCK
    nk = keys // key_block

    def clamp(j, sc, s):
        return jnp.minimum(j, (sc[s] - 1) // key_block)

    grid_spec = pltpu.PrefetchScalarGridSpec(
        num_scalar_prefetch=1,
        grid=(tables, heads, nk),
        in_specs=[
            pl.BlockSpec((rows, DH), lambda s, h, j, sc: (0, s * heads + h)),
            pl.BlockSpec((key_block, DH), lambda s, h, j, sc: (clamp(j, sc, s), s * 2 * heads + h)),
            pl.BlockSpec(
                (key_block, DH), lambda s, h, j, sc: (clamp(j, sc, s), s * 2 * heads + heads + h)
            ),
        ],
        out_specs=pl.BlockSpec((rows, DH), lambda s, h, j, sc: (0, s * heads + h)),
        scratch_shapes=[
            pltpu.VMEM((rows, DH), jnp.float32),
            pltpu.VMEM((rows, DH), jnp.float32),
            pltpu.VMEM((rows, DH), jnp.float32),
        ],
    )
    flops = 4 * tables * heads * rows * keys * DH
    return pl.pallas_call(
        functools.partial(flash_body, scale=scale, key_block=key_block),
        grid_spec=grid_spec,
        out_shape=jax.ShapeDtypeStruct((rows, tables * heads * DH), jnp.bfloat16),
        compiler_params=pltpu.CompilerParams(
            dimension_semantics=("arbitrary", "arbitrary", "arbitrary")
        ),
        cost_estimate=pl.CostEstimate(
            flops=flops,
            transcendentals=tables * heads * rows * keys,
            bytes_accessed=2 * (q_all.size * 2 + kv_all.size),
        ),
    )(scalars, q_all, kv_all, kv_all)


def expert_half(slot_rows, gate_half, up_half, down_half):
    contract_rows = (((1,), (1,)), ((), ()))
    gate_t = lax.dot_general(
        gate_half, slot_rows, contract_rows, preferred_element_type=jnp.float32
    )
    up_t = lax.dot_general(up_half, slot_rows, contract_rows, preferred_element_type=jnp.float32)
    hidden = (jax.nn.silu(gate_t) * up_t).astype(jnp.bfloat16)
    product = lax.dot_general(
        hidden, down_half, (((0,), (0,)), ((), ())), preferred_element_type=jnp.float32
    )
    return product.astype(jnp.bfloat16)


def shards(
    table_cells,
    w_query,
    w_key,
    w_value,
    w_out,
    norm_gain,
    w_gate,
    w_up,
    w_down,
    lengths,
    expert_of_cell,
    slot_of_cell,
):
    cell_count, tables, model_width = table_cells.shape
    head_width = w_query.shape[1]
    head_count = head_width // DH
    score_scale = 1.0 / math.sqrt(DH)
    shard_rows = lax.all_gather(table_cells, "head", axis=0, tiled=True)
    row_cells = shard_rows.shape[0]
    flat_rows = shard_rows.reshape(row_cells * tables, model_width)
    q_all = (
        jnp.dot(flat_rows, w_query, preferred_element_type=jnp.float32)
        .astype(jnp.bfloat16)
        .reshape(row_cells, tables * head_width)
    )
    kv_weight = jnp.concatenate([w_key, w_value], axis=1)
    kv_rows = (
        jnp.dot(flat_rows, kv_weight, preferred_element_type=jnp.float32)
        .astype(jnp.bfloat16)
        .reshape(row_cells, tables * 2 * head_width)
    )
    kv_all = lax.all_gather(kv_rows, "expert", axis=0, tiled=True)
    offset = lax.axis_index("expert") * row_cells
    scalars = jnp.concatenate(
        [lengths.astype(jnp.int32), jnp.reshape(offset, (1,)).astype(jnp.int32)]
    )
    attended = flash_attention(scalars, q_all, kv_all, head_count, score_scale)
    count_rows = cell_count * lax.axis_size("head")
    product = jnp.dot(
        attended.reshape(count_rows * tables, head_width), w_out, preferred_element_type=jnp.float32
    )
    summed = lax.psum_scatter(
        product.reshape(count_rows, tables, model_width).astype(jnp.bfloat16),
        "head",
        scatter_dimension=0,
        tiled=True,
    ).astype(jnp.float32)
    residual = table_cells.astype(jnp.float32) + summed
    mean_square = jnp.mean(residual * residual, axis=-1, keepdims=True)
    normed = (residual * lax.rsqrt(mean_square + 1e-06) * norm_gain.astype(jnp.float32)).astype(
        jnp.bfloat16
    )
    rows_dev = cell_count * tables
    normed_rows = normed.reshape(rows_dev, model_width)
    expert_count = lax.axis_size("expert") * lax.axis_size("head") // 2
    slot_cap = 2 * max(1, rows_dev // expert_count)
    target = expert_of_cell.reshape(rows_dev) * slot_cap + slot_of_cell.reshape(rows_dev)
    slot_table = (
        jnp.arange(expert_count * slot_cap, dtype=jnp.int32)[:, None] == target[None, :]
    ).astype(jnp.bfloat16)
    send_rows = jnp.dot(slot_table, normed_rows, preferred_element_type=jnp.float32).astype(
        jnp.bfloat16
    )
    gate_half = w_gate[0]
    up_half = w_up[0]
    down_half = w_down[0]
    pieces = 2
    spread = send_rows.reshape(expert_count * pieces, slot_cap // pieces, model_width)
    received = lax.all_to_all(spread, ("expert", "head"), 0, 0, tiled=True)
    swap = [(index, index ^ 1) for index in range(lax.axis_size("head"))]
    from_partner = lax.ppermute(received, "head", swap)
    both = jnp.concatenate([received, from_partner], axis=1)
    sources = both.shape[0]
    item_count = both.shape[1]
    half_out = expert_half(
        both.reshape(sources * item_count, model_width), gate_half, up_half, down_half
    ).reshape(sources, item_count, model_width)
    mine = half_out[:, : slot_cap // pieces]
    theirs = lax.ppermute(half_out[:, slot_cap // pieces :], "head", swap)
    summed_halves = (mine.astype(jnp.float32) + theirs.astype(jnp.float32)).astype(jnp.bfloat16)
    combined = lax.all_to_all(summed_halves, ("expert", "head"), 0, 0, tiled=True).reshape(
        expert_count * slot_cap, model_width
    )
    expert_out = lax.dot_general(
        slot_table, combined, (((0,), (0,)), ((), ())), preferred_element_type=jnp.float32
    )
    updated = (residual.reshape(rows_dev, model_width) + expert_out).astype(jnp.bfloat16)
    return updated.reshape(cell_count, tables, model_width)


def solution(mesh):
    placed = (
        P(("expert", "head"), None, None),
        P(None, "head"),
        P(None, "head"),
        P(None, "head"),
        P("head", None),
        P(),
        P(("expert", "head"), None, None),
        P(("expert", "head"), None, None),
        P(("expert", "head"), None, None),
        P(),
        P(("expert", "head"), None),
        P(("expert", "head"), None),
    )
    return jax.shard_map(
        shards,
        mesh=mesh,
        in_specs=placed,
        out_specs=P(("expert", "head"), None, None),
        check_vma=False,
    )
```

```python
import functools
import math

import jax
import jax.numpy as jnp
from jax import lax
from jax.experimental import pallas as pl
from jax.experimental.pallas import tpu as pltpu

from jax.sharding import PartitionSpec as P

DH = 128
KEY_BLOCK = 4096


def flash_body(scalars, q_ref, k_ref, v_ref, o_ref, m_ref, l_ref, acc_ref, *, scale, key_block):
    s = pl.program_id(0)
    j = pl.program_id(2)
    last = pl.num_programs(2) - 1
    length = scalars[s]
    start = j * key_block

    @pl.when(j == 0)
    def _():
        m_ref[...] = jnp.full(m_ref.shape, -1e30, jnp.float32)
        l_ref[...] = jnp.zeros(l_ref.shape, jnp.float32)
        acc_ref[...] = jnp.zeros(acc_ref.shape, jnp.float32)

    def update(masked):
        q = q_ref[...]
        k = k_ref[...]
        scores = lax.dot_general(
            q, k, (((1,), (1,)), ((), ())), preferred_element_type=jnp.float32
        ) * scale
        if masked:
            cols = start + lax.broadcasted_iota(jnp.int32, scores.shape, 1)
            scores = jnp.where(cols < length, scores, -jnp.inf)
        m_prev = m_ref[...]
        m_new = jnp.maximum(m_prev, jnp.max(scores, axis=1, keepdims=True))
        alpha = jnp.exp(m_prev - m_new)
        p = jnp.exp(scores - m_new[:, :1])
        l_ref[...] = alpha * l_ref[...] + jnp.sum(p, axis=1, keepdims=True)
        acc_ref[...] = acc_ref[...] * alpha + jnp.dot(
            p.astype(jnp.bfloat16), v_ref[...], preferred_element_type=jnp.float32
        )
        m_ref[...] = m_new

    @pl.when(start + key_block <= length)
    def _():
        update(False)

    @pl.when(jnp.logical_and(start < length, start + key_block > length))
    def _():
        update(True)

    @pl.when(j == last)
    def _():
        o_ref[...] = (acc_ref[...] / l_ref[...]).astype(o_ref.dtype)


def flash_attention(scalars, q_all, kv_all, heads, scale):
    rows = q_all.shape[0]
    keys = kv_all.shape[0]
    tables = scalars.shape[0]
    key_block = KEY_BLOCK
    nk = keys // key_block

    def clamp(j, sc, s):
        return jnp.minimum(j, (sc[s] - 1) // key_block)

    grid_spec = pltpu.PrefetchScalarGridSpec(
        num_scalar_prefetch=1,
        grid=(tables, heads, nk),
        in_specs=[
            pl.BlockSpec((rows, DH), lambda s, h, j, sc: (0, s * heads + h)),
            pl.BlockSpec((key_block, DH), lambda s, h, j, sc: (clamp(j, sc, s), s * 2 * heads + h)),
            pl.BlockSpec(
                (key_block, DH), lambda s, h, j, sc: (clamp(j, sc, s), s * 2 * heads + heads + h)
            ),
        ],
        out_specs=pl.BlockSpec((rows, DH), lambda s, h, j, sc: (0, s * heads + h)),
        scratch_shapes=[
            pltpu.VMEM((rows, DH), jnp.float32),
            pltpu.VMEM((rows, DH), jnp.float32),
            pltpu.VMEM((rows, DH), jnp.float32),
        ],
    )
    flops = 4 * tables * heads * rows * keys * DH
    return pl.pallas_call(
        functools.partial(flash_body, scale=scale, key_block=key_block),
        grid_spec=grid_spec,
        out_shape=jax.ShapeDtypeStruct((rows, tables * heads * DH), jnp.bfloat16),
        compiler_params=pltpu.CompilerParams(
            dimension_semantics=("arbitrary", "arbitrary", "arbitrary")
        ),
        cost_estimate=pl.CostEstimate(
            flops=flops,
            transcendentals=tables * heads * rows * keys,
            bytes_accessed=2 * (q_all.size * 2 + kv_all.size),
        ),
    )(scalars, q_all, kv_all, kv_all)


def expert_half(slot_rows, gate_half, up_half, down_half):
    contract_rows = (((1,), (1,)), ((), ()))
    gate_t = lax.dot_general(
        gate_half, slot_rows, contract_rows, preferred_element_type=jnp.float32
    )
    up_t = lax.dot_general(up_half, slot_rows, contract_rows, preferred_element_type=jnp.float32)
    hidden = (jax.nn.silu(gate_t) * up_t).astype(jnp.bfloat16)
    product = lax.dot_general(
        hidden, down_half, (((0,), (0,)), ((), ())), preferred_element_type=jnp.float32
    )
    return product.astype(jnp.bfloat16)


def shards(
    table_cells,
    w_query,
    w_key,
    w_value,
    w_out,
    norm_gain,
    w_gate,
    w_up,
    w_down,
    lengths,
    expert_of_cell,
    slot_of_cell,
):
    cell_count, tables, model_width = table_cells.shape
    head_width = w_query.shape[1]
    head_count = head_width // DH
    score_scale = 1.0 / math.sqrt(DH)
    shard_rows = lax.all_gather(table_cells, "head", axis=0, tiled=True)
    row_cells = shard_rows.shape[0]
    flat_rows = shard_rows.reshape(row_cells * tables, model_width)
    q_all = (
        jnp.dot(flat_rows, w_query, preferred_element_type=jnp.float32)
        .astype(jnp.bfloat16)
        .reshape(row_cells, tables * head_width)
    )
    kv_weight = jnp.concatenate([w_key, w_value], axis=1)
    kv_rows = (
        jnp.dot(flat_rows, kv_weight, preferred_element_type=jnp.float32)
        .astype(jnp.bfloat16)
        .reshape(row_cells, tables * 2 * head_width)
    )
    kv_all = lax.all_gather(kv_rows, "expert", axis=0, tiled=True)
    head_size = lax.axis_size("head")
    chunks = 2
    q_chunks = q_all.reshape(head_size, chunks, cell_count // chunks, tables * head_width)
    parts = []
    for chunk in range(chunks):
        attended = flash_attention(
            lengths.astype(jnp.int32),
            q_chunks[:, chunk].reshape(row_cells // chunks, tables * head_width),
            kv_all,
            head_count,
            score_scale,
        )
        product = jnp.dot(
            attended.reshape(row_cells // chunks * tables, head_width),
            w_out,
            preferred_element_type=jnp.float32,
        )
        parts.append(
            lax.psum_scatter(
                product.reshape(row_cells // chunks, tables, model_width).astype(jnp.bfloat16),
                "head",
                scatter_dimension=0,
                tiled=True,
            )
        )
    own_cells = (
        lax.axis_index("expert") * row_cells
        + lax.axis_index("head") * cell_count
        + jnp.arange(cell_count, dtype=jnp.int32)
    )
    live = own_cells[:, None] < lengths[None, :]
    summed = jnp.where(
        live[:, :, None], jnp.concatenate(parts, axis=0).astype(jnp.float32), 0.0
    )
    residual = table_cells.astype(jnp.float32) + summed
    mean_square = jnp.mean(residual * residual, axis=-1, keepdims=True)
    normed = (residual * lax.rsqrt(mean_square + 1e-06) * norm_gain.astype(jnp.float32)).astype(
        jnp.bfloat16
    )
    rows_dev = cell_count * tables
    normed_rows = normed.reshape(rows_dev, model_width)
    expert_count = lax.axis_size("expert") * lax.axis_size("head") // 2
    slot_cap = 2 * max(1, rows_dev // expert_count)
    target = expert_of_cell.reshape(rows_dev) * slot_cap + slot_of_cell.reshape(rows_dev)
    slot_table = (
        jnp.arange(expert_count * slot_cap, dtype=jnp.int32)[:, None] == target[None, :]
    ).astype(jnp.bfloat16)
    send_rows = jnp.dot(slot_table, normed_rows, preferred_element_type=jnp.float32).astype(
        jnp.bfloat16
    )
    gate_half = w_gate[0]
    up_half = w_up[0]
    down_half = w_down[0]
    pieces = 2
    spread = send_rows.reshape(expert_count * pieces, slot_cap // pieces, model_width)
    received = lax.all_to_all(spread, ("expert", "head"), 0, 0, tiled=True)
    swap = [(index, index ^ 1) for index in range(lax.axis_size("head"))]
    from_partner = lax.ppermute(received, "head", swap)
    both = jnp.concatenate([received, from_partner], axis=1)
    sources = both.shape[0]
    item_count = both.shape[1]
    half_out = expert_half(
        both.reshape(sources * item_count, model_width), gate_half, up_half, down_half
    ).reshape(sources, item_count, model_width)
    mine = half_out[:, : slot_cap // pieces]
    theirs = lax.ppermute(half_out[:, slot_cap // pieces :], "head", swap)
    summed_halves = (mine.astype(jnp.float32) + theirs.astype(jnp.float32)).astype(jnp.bfloat16)
    combined = lax.all_to_all(summed_halves, ("expert", "head"), 0, 0, tiled=True).reshape(
        expert_count * slot_cap, model_width
    )
    expert_out = lax.dot_general(
        slot_table, combined, (((0,), (0,)), ((), ())), preferred_element_type=jnp.float32
    )
    updated = (residual.reshape(rows_dev, model_width) + expert_out).astype(jnp.bfloat16)
    return updated.reshape(cell_count, tables, model_width)


def solution(mesh):
    placed = (
        P(("expert", "head"), None, None),
        P(None, "head"),
        P(None, "head"),
        P(None, "head"),
        P("head", None),
        P(),
        P(("expert", "head"), None, None),
        P(("expert", "head"), None, None),
        P(("expert", "head"), None, None),
        P(),
        P(("expert", "head"), None),
        P(("expert", "head"), None),
    )
    return jax.shard_map(
        shards,
        mesh=mesh,
        in_specs=placed,
        out_specs=P(("expert", "head"), None, None),
        check_vma=False,
    )
```

```python
import functools
import math

import jax
import jax.numpy as jnp
from jax import lax
from jax.experimental import pallas as pl
from jax.experimental.pallas import tpu as pltpu

from jax.sharding import PartitionSpec as P

DH = 128
KEY_BLOCK = 4096


def flash_body(scalars, q_ref, k_ref, v_ref, o_ref, m_ref, l_ref, acc_ref, *, scale, key_block):
    s = pl.program_id(0)
    j = pl.program_id(2)
    last = pl.num_programs(2) - 1
    length = scalars[s]
    start = j * key_block

    @pl.when(j == 0)
    def _():
        m_ref[...] = jnp.full(m_ref.shape, -1e30, jnp.float32)
        l_ref[...] = jnp.zeros(l_ref.shape, jnp.float32)
        acc_ref[...] = jnp.zeros(acc_ref.shape, jnp.float32)

    def update(masked):
        q = q_ref[...]
        k = k_ref[...]
        scores = lax.dot_general(
            q, k, (((1,), (1,)), ((), ())), preferred_element_type=jnp.float32
        ) * scale
        if masked:
            cols = start + lax.broadcasted_iota(jnp.int32, scores.shape, 1)
            scores = jnp.where(cols < length, scores, -jnp.inf)
        m_prev = m_ref[...]
        m_new = jnp.maximum(m_prev, jnp.max(scores, axis=1, keepdims=True))
        alpha = jnp.exp(m_prev - m_new)
        p = jnp.exp(scores - m_new[:, :1])
        l_ref[...] = alpha * l_ref[...] + jnp.sum(p, axis=1, keepdims=True)
        acc_ref[...] = acc_ref[...] * alpha + jnp.dot(
            p.astype(jnp.bfloat16), v_ref[...], preferred_element_type=jnp.float32
        )
        m_ref[...] = m_new

    @pl.when(start + key_block <= length)
    def _():
        update(False)

    @pl.when(jnp.logical_and(start < length, start + key_block > length))
    def _():
        update(True)

    @pl.when(j == last)
    def _():
        rows = scalars[2] + lax.broadcasted_iota(jnp.int32, acc_ref.shape, 0)
        out = acc_ref[...] / l_ref[...]
        o_ref[...] = jnp.where(rows < length, out, 0.0).astype(o_ref.dtype)


def flash_attention(scalars, q_all, kv_all, heads, scale):
    rows = q_all.shape[0]
    keys = kv_all.shape[0]
    tables = scalars.shape[0] - 1
    key_block = KEY_BLOCK
    nk = keys // key_block

    def clamp(j, sc, s):
        return jnp.minimum(j, (sc[s] - 1) // key_block)

    grid_spec = pltpu.PrefetchScalarGridSpec(
        num_scalar_prefetch=1,
        grid=(tables, heads, nk),
        in_specs=[
            pl.BlockSpec((rows, DH), lambda s, h, j, sc: (0, s * heads + h)),
            pl.BlockSpec((key_block, DH), lambda s, h, j, sc: (clamp(j, sc, s), s * 2 * heads + h)),
            pl.BlockSpec(
                (key_block, DH), lambda s, h, j, sc: (clamp(j, sc, s), s * 2 * heads + heads + h)
            ),
        ],
        out_specs=pl.BlockSpec((rows, DH), lambda s, h, j, sc: (0, s * heads + h)),
        scratch_shapes=[
            pltpu.VMEM((rows, DH), jnp.float32),
            pltpu.VMEM((rows, DH), jnp.float32),
            pltpu.VMEM((rows, DH), jnp.float32),
        ],
    )
    flops = 4 * tables * heads * rows * keys * DH
    return pl.pallas_call(
        functools.partial(flash_body, scale=scale, key_block=key_block),
        grid_spec=grid_spec,
        out_shape=jax.ShapeDtypeStruct((rows, tables * heads * DH), jnp.bfloat16),
        compiler_params=pltpu.CompilerParams(
            dimension_semantics=("arbitrary", "arbitrary", "arbitrary")
        ),
        cost_estimate=pl.CostEstimate(
            flops=flops,
            transcendentals=tables * heads * rows * keys,
            bytes_accessed=2 * (q_all.size * 2 + kv_all.size),
        ),
    )(scalars, q_all, kv_all, kv_all)


def expert_half(slot_rows, gate_half, up_half, down_half):
    contract_rows = (((1,), (1,)), ((), ()))
    gate_t = lax.dot_general(
        gate_half, slot_rows, contract_rows, preferred_element_type=jnp.float32
    )
    up_t = lax.dot_general(up_half, slot_rows, contract_rows, preferred_element_type=jnp.float32)
    hidden = (jax.nn.silu(gate_t) * up_t).astype(jnp.bfloat16)
    product = lax.dot_general(
        hidden, down_half, (((0,), (0,)), ((), ())), preferred_element_type=jnp.float32
    )
    return product.astype(jnp.bfloat16)


def shards(
    table_cells,
    w_query,
    w_key,
    w_value,
    w_out,
    norm_gain,
    w_gate,
    w_up,
    w_down,
    lengths,
    expert_of_cell,
    slot_of_cell,
):
    cell_count, tables, model_width = table_cells.shape
    head_width = w_query.shape[1]
    head_count = head_width // DH
    score_scale = 1.0 / math.sqrt(DH)
    shard_rows = lax.all_gather(table_cells, "head", axis=0, tiled=True)
    row_cells = shard_rows.shape[0]
    flat_rows = shard_rows.reshape(row_cells * tables, model_width)
    q_all = (
        jnp.dot(flat_rows, w_query, preferred_element_type=jnp.float32)
        .astype(jnp.bfloat16)
        .reshape(row_cells, tables * head_width)
    )
    kv_weight = jnp.concatenate([w_key, w_value], axis=1)
    kv_rows = (
        jnp.dot(flat_rows, kv_weight, preferred_element_type=jnp.float32)
        .astype(jnp.bfloat16)
        .reshape(row_cells, tables * 2 * head_width)
    )
    kv_all = lax.all_gather(kv_rows, "expert", axis=0, tiled=True)
    offset = lax.axis_index("expert") * row_cells
    scalars = jnp.concatenate(
        [lengths.astype(jnp.int32), jnp.reshape(offset, (1,)).astype(jnp.int32)]
    )
    attended = flash_attention(scalars, q_all, kv_all, head_count, score_scale)
    head_size = lax.axis_size("head")
    me_head = lax.axis_index("head")
    w_parts = [w_out]
    for shift in range(1, head_size):
        w_parts.append(
            lax.ppermute(
                w_out, "head", [(index, (index + shift) % head_size) for index in range(head_size)]
            )
        )
    w_rel = jnp.concatenate(w_parts, axis=0)
    by_owner = lax.all_to_all(
        attended.reshape(head_size, cell_count, tables, head_width), "head", 0, 0, tiled=True
    )
    groups_rel = (me_head - jnp.arange(head_size)) % head_size
    rel = jnp.take(by_owner, groups_rel, axis=0).transpose(1, 2, 0, 3)
    summed = jnp.dot(
        rel.reshape(cell_count * tables, head_size * head_width),
        w_rel,
        preferred_element_type=jnp.float32,
    ).reshape(cell_count, tables, model_width)
    residual = table_cells.astype(jnp.float32) + summed
    mean_square = jnp.mean(residual * residual, axis=-1, keepdims=True)
    normed = (residual * lax.rsqrt(mean_square + 1e-06) * norm_gain.astype(jnp.float32)).astype(
        jnp.bfloat16
    )
    rows_dev = cell_count * tables
    normed_rows = normed.reshape(rows_dev, model_width)
    expert_count = lax.axis_size("expert") * lax.axis_size("head") // 2
    slot_cap = 2 * max(1, rows_dev // expert_count)
    target = expert_of_cell.reshape(rows_dev) * slot_cap + slot_of_cell.reshape(rows_dev)
    slot_table = (
        jnp.arange(expert_count * slot_cap, dtype=jnp.int32)[:, None] == target[None, :]
    ).astype(jnp.bfloat16)
    send_rows = jnp.dot(slot_table, normed_rows, preferred_element_type=jnp.float32).astype(
        jnp.bfloat16
    )
    gate_half = w_gate[0]
    up_half = w_up[0]
    down_half = w_down[0]
    pieces = 2
    spread = send_rows.reshape(expert_count * pieces, slot_cap // pieces, model_width)
    received = lax.all_to_all(spread, ("expert", "head"), 0, 0, tiled=True)
    swap = [(index, index ^ 1) for index in range(lax.axis_size("head"))]
    from_partner = lax.ppermute(received, "head", swap)
    both = jnp.concatenate([received, from_partner], axis=1)
    sources = both.shape[0]
    item_count = both.shape[1]
    half_out = expert_half(
        both.reshape(sources * item_count, model_width), gate_half, up_half, down_half
    ).reshape(sources, item_count, model_width)
    mine = half_out[:, : slot_cap // pieces]
    theirs = lax.ppermute(half_out[:, slot_cap // pieces :], "head", swap)
    summed_halves = (mine.astype(jnp.float32) + theirs.astype(jnp.float32)).astype(jnp.bfloat16)
    combined = lax.all_to_all(summed_halves, ("expert", "head"), 0, 0, tiled=True).reshape(
        expert_count * slot_cap, model_width
    )
    expert_out = lax.dot_general(
        slot_table, combined, (((0,), (0,)), ((), ())), preferred_element_type=jnp.float32
    )
    updated = (residual.reshape(rows_dev, model_width) + expert_out).astype(jnp.bfloat16)
    return updated.reshape(cell_count, tables, model_width)


def solution(mesh):
    placed = (
        P(("expert", "head"), None, None),
        P(None, "head"),
        P(None, "head"),
        P(None, "head"),
        P("head", None),
        P(),
        P(("expert", "head"), None, None),
        P(("expert", "head"), None, None),
        P(("expert", "head"), None, None),
        P(),
        P(("expert", "head"), None),
        P(("expert", "head"), None),
    )
    return jax.shard_map(
        shards,
        mesh=mesh,
        in_specs=placed,
        out_specs=P(("expert", "head"), None, None),
        check_vma=False,
    )
```

```python
import functools
import math

import jax
import jax.numpy as jnp
from jax import lax
from jax.experimental import pallas as pl
from jax.experimental.pallas import tpu as pltpu

from jax.sharding import PartitionSpec as P

DH = 128
KEY_BLOCK = 4096


def flash_body(scalars, q_ref, k_ref, v_ref, o_ref, m_ref, l_ref, acc_ref, *, scale, key_block):
    s = pl.program_id(0)
    j = pl.program_id(2)
    last = pl.num_programs(2) - 1
    length = scalars[s]
    start = j * key_block

    @pl.when(j == 0)
    def _():
        m_ref[...] = jnp.full(m_ref.shape, -1e30, jnp.float32)
        l_ref[...] = jnp.zeros(l_ref.shape, jnp.float32)
        acc_ref[...] = jnp.zeros(acc_ref.shape, jnp.float32)

    def update(masked):
        q = q_ref[...]
        k = k_ref[...]
        scores = lax.dot_general(
            q, k, (((1,), (1,)), ((), ())), preferred_element_type=jnp.float32
        ) * scale
        if masked:
            cols = start + lax.broadcasted_iota(jnp.int32, scores.shape, 1)
            scores = jnp.where(cols < length, scores, -jnp.inf)
        m_prev = m_ref[...]
        m_new = jnp.maximum(m_prev, jnp.max(scores, axis=1, keepdims=True))
        alpha = jnp.exp(m_prev - m_new)
        p = jnp.exp(scores - m_new[:, :1])
        l_ref[...] = alpha * l_ref[...] + jnp.sum(p, axis=1, keepdims=True)
        acc_ref[...] = acc_ref[...] * alpha + jnp.dot(
            p.astype(jnp.bfloat16), v_ref[...], preferred_element_type=jnp.float32
        )
        m_ref[...] = m_new

    @pl.when(start + key_block <= length)
    def _():
        update(False)

    @pl.when(jnp.logical_and(start < length, start + key_block > length))
    def _():
        update(True)

    @pl.when(j == last)
    def _():
        rows = scalars[2] + lax.broadcasted_iota(jnp.int32, acc_ref.shape, 0)
        out = acc_ref[...] / l_ref[...]
        o_ref[...] = jnp.where(rows < length, out, 0.0).astype(o_ref.dtype)


def flash_attention(scalars, q_all, kv_all, heads, scale):
    rows = q_all.shape[0]
    keys = kv_all.shape[0]
    tables = scalars.shape[0] - 1
    key_block = KEY_BLOCK
    nk = keys // key_block

    def clamp(j, sc, s):
        return jnp.minimum(j, (sc[s] - 1) // key_block)

    grid_spec = pltpu.PrefetchScalarGridSpec(
        num_scalar_prefetch=1,
        grid=(tables, heads, nk),
        in_specs=[
            pl.BlockSpec((rows, DH), lambda s, h, j, sc: (0, s * heads + h)),
            pl.BlockSpec((key_block, DH), lambda s, h, j, sc: (clamp(j, sc, s), s * 2 * heads + h)),
            pl.BlockSpec(
                (key_block, DH), lambda s, h, j, sc: (clamp(j, sc, s), s * 2 * heads + heads + h)
            ),
        ],
        out_specs=pl.BlockSpec((rows, DH), lambda s, h, j, sc: (0, s * heads + h)),
        scratch_shapes=[
            pltpu.VMEM((rows, DH), jnp.float32),
            pltpu.VMEM((rows, DH), jnp.float32),
            pltpu.VMEM((rows, DH), jnp.float32),
        ],
    )
    flops = 4 * tables * heads * rows * keys * DH
    return pl.pallas_call(
        functools.partial(flash_body, scale=scale, key_block=key_block),
        grid_spec=grid_spec,
        out_shape=jax.ShapeDtypeStruct((rows, tables * heads * DH), jnp.bfloat16),
        compiler_params=pltpu.CompilerParams(
            dimension_semantics=("arbitrary", "arbitrary", "arbitrary")
        ),
        cost_estimate=pl.CostEstimate(
            flops=flops,
            transcendentals=tables * heads * rows * keys,
            bytes_accessed=2 * (q_all.size * 2 + kv_all.size),
        ),
    )(scalars, q_all, kv_all, kv_all)


def expert_half(slot_rows, gate_half, up_half, down_half):
    contract_rows = (((1,), (1,)), ((), ()))
    gate_t = lax.dot_general(
        gate_half, slot_rows, contract_rows, preferred_element_type=jnp.float32
    )
    up_t = lax.dot_general(up_half, slot_rows, contract_rows, preferred_element_type=jnp.float32)
    hidden = (jax.nn.silu(gate_t) * up_t).astype(jnp.bfloat16)
    product = lax.dot_general(
        hidden, down_half, (((0,), (0,)), ((), ())), preferred_element_type=jnp.float32
    )
    return product.astype(jnp.bfloat16)


def shards(
    table_cells,
    w_query,
    w_key,
    w_value,
    w_out,
    norm_gain,
    w_gate,
    w_up,
    w_down,
    lengths,
    expert_of_cell,
    slot_of_cell,
):
    cell_count, tables, model_width = table_cells.shape
    head_width = w_query.shape[1]
    head_count = head_width // DH
    score_scale = 1.0 / math.sqrt(DH)
    cells_flat = table_cells.reshape(cell_count * tables, model_width)
    flat_rows = lax.all_gather(cells_flat, "head", axis=0, tiled=True)
    row_cells = flat_rows.shape[0] // tables
    q_all = (
        jnp.dot(flat_rows, w_query, preferred_element_type=jnp.float32)
        .astype(jnp.bfloat16)
        .reshape(row_cells, tables * head_width)
    )
    kv_weight = jnp.concatenate([w_key, w_value], axis=1)
    kv_rows = (
        jnp.dot(flat_rows, kv_weight, preferred_element_type=jnp.float32)
        .astype(jnp.bfloat16)
        .reshape(row_cells, tables * 2 * head_width)
    )
    kv_all = lax.all_gather(kv_rows, "expert", axis=0, tiled=True)
    offset = lax.axis_index("expert") * row_cells
    scalars = jnp.concatenate(
        [lengths.astype(jnp.int32), jnp.reshape(offset, (1,)).astype(jnp.int32)]
    )
    attended = flash_attention(scalars, q_all, kv_all, head_count, score_scale)
    head_size = lax.axis_size("head")
    me_head = lax.axis_index("head")
    w_parts = [w_out]
    for shift in range(1, head_size):
        w_parts.append(
            lax.ppermute(
                w_out, "head", [(index, (index + shift) % head_size) for index in range(head_size)]
            )
        )
    w_rel = jnp.concatenate(w_parts, axis=0)
    by_owner = lax.all_to_all(
        attended.reshape(head_size, cell_count, tables, head_width), "head", 0, 0, tiled=True
    )
    groups_rel = (me_head - jnp.arange(head_size)) % head_size
    rel = jnp.take(by_owner, groups_rel, axis=0).transpose(1, 2, 0, 3)
    summed = jnp.dot(
        rel.reshape(cell_count * tables, head_size * head_width),
        w_rel,
        preferred_element_type=jnp.float32,
    )
    residual = cells_flat.astype(jnp.float32) + summed
    mean_square = jnp.mean(residual * residual, axis=-1, keepdims=True)
    normed = (residual * lax.rsqrt(mean_square + 1e-06) * norm_gain.astype(jnp.float32)).astype(
        jnp.bfloat16
    )
    rows_dev = cell_count * tables
    normed_rows = normed.reshape(rows_dev, model_width)
    expert_count = lax.axis_size("expert") * lax.axis_size("head") // 2
    slot_cap = 2 * max(1, rows_dev // expert_count)
    target = expert_of_cell.reshape(rows_dev) * slot_cap + slot_of_cell.reshape(rows_dev)
    slot_table = (
        jnp.arange(expert_count * slot_cap, dtype=jnp.int32)[:, None] == target[None, :]
    ).astype(jnp.bfloat16)
    send_rows = jnp.dot(slot_table, normed_rows, preferred_element_type=jnp.float32).astype(
        jnp.bfloat16
    )
    gate_half = w_gate[0]
    up_half = w_up[0]
    down_half = w_down[0]
    pieces = 2
    spread = send_rows.reshape(expert_count * pieces, slot_cap // pieces, model_width)
    received = lax.all_to_all(spread, ("expert", "head"), 0, 0, tiled=True)
    swap = [(index, index ^ 1) for index in range(lax.axis_size("head"))]
    from_partner = lax.ppermute(received, "head", swap)
    both = jnp.concatenate([received, from_partner], axis=1)
    sources = both.shape[0]
    item_count = both.shape[1]
    half_out = expert_half(
        both.reshape(sources * item_count, model_width), gate_half, up_half, down_half
    ).reshape(sources, item_count, model_width)
    mine = half_out[:, : slot_cap // pieces]
    theirs = lax.ppermute(half_out[:, slot_cap // pieces :], "head", swap)
    summed_halves = (mine.astype(jnp.float32) + theirs.astype(jnp.float32)).astype(jnp.bfloat16)
    combined = lax.all_to_all(summed_halves, ("expert", "head"), 0, 0, tiled=True).reshape(
        expert_count * slot_cap, model_width
    )
    expert_out = lax.dot_general(
        slot_table, combined, (((0,), (0,)), ((), ())), preferred_element_type=jnp.float32
    )
    updated = (residual.reshape(rows_dev, model_width) + expert_out).astype(jnp.bfloat16)
    return updated.reshape(cell_count, tables, model_width)


def solution(mesh):
    placed = (
        P(("expert", "head"), None, None),
        P(None, "head"),
        P(None, "head"),
        P(None, "head"),
        P("head", None),
        P(),
        P(("expert", "head"), None, None),
        P(("expert", "head"), None, None),
        P(("expert", "head"), None, None),
        P(),
        P(("expert", "head"), None),
        P(("expert", "head"), None),
    )
    return jax.shard_map(
        shards,
        mesh=mesh,
        in_specs=placed,
        out_specs=P(("expert", "head"), None, None),
        check_vma=False,
    )
```

```python
import functools
import math

import jax
import jax.numpy as jnp
from jax import lax
from jax.experimental import pallas as pl
from jax.experimental.pallas import tpu as pltpu

from jax.sharding import PartitionSpec as P

DH = 128
KEY_BLOCK = 4096
QUERY_BLOCK = 512


def flash_body(scalars, q_ref, k_ref, v_ref, o_ref, m_ref, l_ref, acc_ref, *, scale, key_block):
    j = pl.program_id(1)
    last = pl.num_programs(1) - 1
    length = scalars[0]
    start = j * key_block

    @pl.when(j == 0)
    def _():
        m_ref[...] = jnp.full(m_ref.shape, -1e30, jnp.float32)
        l_ref[...] = jnp.zeros(l_ref.shape, jnp.float32)
        acc_ref[...] = jnp.zeros(acc_ref.shape, jnp.float32)

    def update(masked):
        scores = lax.dot_general(
            q_ref[...], k_ref[...], (((1,), (1,)), ((), ())), preferred_element_type=jnp.float32
        ) * scale
        if masked:
            cols = start + lax.broadcasted_iota(jnp.int32, scores.shape, 1)
            scores = jnp.where(cols < length, scores, -jnp.inf)
        m_prev = m_ref[...]
        m_new = jnp.maximum(m_prev, jnp.max(scores, axis=1, keepdims=True))
        alpha = jnp.exp(m_prev - m_new)
        p = jnp.exp(scores - m_new[:, :1])
        l_ref[...] = alpha * l_ref[...] + jnp.sum(p, axis=1, keepdims=True)
        acc_ref[...] = acc_ref[...] * alpha + jnp.dot(
            p.astype(jnp.bfloat16), v_ref[...], preferred_element_type=jnp.float32
        )
        m_ref[...] = m_new

    @pl.when(start + key_block <= length)
    def _():
        update(False)

    @pl.when(jnp.logical_and(start < length, start + key_block > length))
    def _():
        update(True)

    @pl.when(j == last)
    def _():
        o_ref[...] = (acc_ref[...] / l_ref[...]).astype(o_ref.dtype)


def flash_attention(scalars, q_rows, kv_rows, scale):
    rows = q_rows.shape[0]
    keys = kv_rows.shape[0]
    key_block = KEY_BLOCK
    query_block = min(rows, QUERY_BLOCK)
    nk = keys // key_block

    def clamp(j, sc):
        return jnp.minimum(j, (sc[0] - 1) // key_block)

    grid_spec = pltpu.PrefetchScalarGridSpec(
        num_scalar_prefetch=1,
        grid=(rows // query_block, nk),
        in_specs=[
            pl.BlockSpec((query_block, DH), lambda i, j, sc: (i, 0)),
            pl.BlockSpec((key_block, DH), lambda i, j, sc: (clamp(j, sc), 0)),
            pl.BlockSpec((key_block, DH), lambda i, j, sc: (clamp(j, sc), 1)),
        ],
        out_specs=pl.BlockSpec((query_block, DH), lambda i, j, sc: (i, 0)),
        scratch_shapes=[
            pltpu.VMEM((query_block, DH), jnp.float32),
            pltpu.VMEM((query_block, DH), jnp.float32),
            pltpu.VMEM((query_block, DH), jnp.float32),
        ],
    )
    return pl.pallas_call(
        functools.partial(flash_body, scale=scale, key_block=key_block),
        grid_spec=grid_spec,
        out_shape=jax.ShapeDtypeStruct((rows, DH), jnp.bfloat16),
        compiler_params=pltpu.CompilerParams(dimension_semantics=("arbitrary", "arbitrary")),
        cost_estimate=pl.CostEstimate(
            flops=4 * rows * keys * DH,
            transcendentals=rows * keys,
            bytes_accessed=2 * (2 * rows * DH + kv_rows.size * (rows // query_block)),
        ),
    )(scalars, q_rows, kv_rows, kv_rows)


def expert_half(slot_rows, gate_half, up_half, down_half):
    contract_rows = (((1,), (1,)), ((), ()))
    gate_t = lax.dot_general(
        gate_half, slot_rows, contract_rows, preferred_element_type=jnp.float32
    )
    up_t = lax.dot_general(up_half, slot_rows, contract_rows, preferred_element_type=jnp.float32)
    hidden = (jax.nn.silu(gate_t) * up_t).astype(jnp.bfloat16)
    product = lax.dot_general(
        hidden, down_half, (((0,), (0,)), ((), ())), preferred_element_type=jnp.float32
    )
    return product.astype(jnp.bfloat16)


def shards(
    table_cells,
    w_query,
    w_key,
    w_value,
    w_out,
    norm_gain,
    w_gate,
    w_up,
    w_down,
    lengths,
    expert_of_cell,
    slot_of_cell,
):
    cell_count, tables, model_width = table_cells.shape
    head_width = w_query.shape[1]
    head_count = head_width // DH
    score_scale = 1.0 / math.sqrt(DH)
    cells_flat = table_cells.reshape(cell_count * tables, model_width)
    flat_rows = lax.all_gather(cells_flat, "head", axis=0, tiled=True)
    row_cells = flat_rows.shape[0] // tables
    pairs = tables * head_count
    expert_size = lax.axis_size("expert")
    quarters = expert_size // pairs
    me = lax.axis_index("expert")
    q_pairs = (
        jnp.dot(flat_rows, w_query, preferred_element_type=jnp.float32)
        .astype(jnp.bfloat16)
        .reshape(row_cells, pairs, DH)
    )
    kv_weight = jnp.concatenate(
        [w_key.reshape(model_width, head_count, DH), w_value.reshape(model_width, head_count, DH)],
        axis=2,
    ).reshape(model_width, 2 * head_width)
    kv_pairs = (
        jnp.dot(flat_rows, kv_weight, preferred_element_type=jnp.float32)
        .astype(jnp.bfloat16)
        .reshape(row_cells, pairs, 2 * DH)
        .transpose(1, 0, 2)
    )
    send = jnp.repeat(kv_pairs, quarters, axis=0)
    kv_here = lax.all_to_all(send, "expert", 0, 0, tiled=True).reshape(
        expert_size * row_cells, 2 * DH
    )
    my_pair = me // quarters
    my_part = me % quarters
    q_parts = []
    for shift in range(quarters):
        perm = [
            (src, quarters * ((src % quarters + shift) % quarters) + src // quarters)
            for src in range(expert_size)
        ]
        sent_pair = (my_part + shift) % quarters
        q_parts.append(
            lax.ppermute(
                lax.dynamic_index_in_dim(q_pairs, sent_pair, axis=1, keepdims=False),
                "expert",
                perm,
            )
        )
    q_stack = jnp.stack(q_parts)
    q_rows = jnp.take(q_stack, (my_pair - jnp.arange(quarters)) % quarters, axis=0)
    scalars = jnp.reshape(lengths[my_pair // head_count], (1,)).astype(jnp.int32)
    out_rows = flash_attention(
        scalars, q_rows.reshape(quarters * row_cells, DH), kv_here, score_scale
    ).reshape(quarters, row_cells, DH)
    back_parts = []
    for shift in range(quarters):
        perm = [
            (quarters * ((src % quarters + shift) % quarters) + src // quarters, src)
            for src in range(expert_size)
        ]
        source_slot = (my_pair - shift) % quarters
        back_parts.append(
            lax.ppermute(
                lax.dynamic_index_in_dim(out_rows, source_slot, axis=0, keepdims=False),
                "expert",
                perm,
            )
        )
    back_stack = jnp.stack(back_parts)
    attended = jnp.take(back_stack, (jnp.arange(pairs) - my_part) % quarters, axis=0)
    positions = me * row_cells + jnp.arange(row_cells, dtype=jnp.int32)
    live = positions[:, None] < lengths[None, :]
    attended = attended.reshape(tables, head_count, row_cells, DH).transpose(2, 0, 1, 3)
    attended = jnp.where(live[:, :, None, None], attended, jnp.zeros_like(attended))
    head_size = lax.axis_size("head")
    me_head = lax.axis_index("head")
    w_parts = [w_out]
    for shift in range(1, head_size):
        w_parts.append(
            lax.ppermute(
                w_out, "head", [(index, (index + shift) % head_size) for index in range(head_size)]
            )
        )
    w_rel = jnp.concatenate(w_parts, axis=0)
    by_owner = lax.all_to_all(
        attended.reshape(head_size, cell_count, tables, head_width), "head", 0, 0, tiled=True
    )
    groups_rel = (me_head - jnp.arange(head_size)) % head_size
    rel = jnp.take(by_owner, groups_rel, axis=0).transpose(1, 2, 0, 3)
    summed = jnp.dot(
        rel.reshape(cell_count * tables, head_size * head_width),
        w_rel,
        preferred_element_type=jnp.float32,
    )
    residual = cells_flat.astype(jnp.float32) + summed
    mean_square = jnp.mean(residual * residual, axis=-1, keepdims=True)
    normed = (residual * lax.rsqrt(mean_square + 1e-06) * norm_gain.astype(jnp.float32)).astype(
        jnp.bfloat16
    )
    rows_dev = cell_count * tables
    normed_rows = normed.reshape(rows_dev, model_width)
    expert_count = lax.axis_size("expert") * lax.axis_size("head") // 2
    slot_cap = 2 * max(1, rows_dev // expert_count)
    target = expert_of_cell.reshape(rows_dev) * slot_cap + slot_of_cell.reshape(rows_dev)
    slot_table = (
        jnp.arange(expert_count * slot_cap, dtype=jnp.int32)[:, None] == target[None, :]
    ).astype(jnp.bfloat16)
    send_rows = jnp.dot(slot_table, normed_rows, preferred_element_type=jnp.float32).astype(
        jnp.bfloat16
    )
    gate_half = w_gate[0]
    up_half = w_up[0]
    down_half = w_down[0]
    pieces = 2
    spread = send_rows.reshape(expert_count * pieces, slot_cap // pieces, model_width)
    received = lax.all_to_all(spread, ("expert", "head"), 0, 0, tiled=True)
    swap = [(index, index ^ 1) for index in range(lax.axis_size("head"))]
    from_partner = lax.ppermute(received, "head", swap)
    both = jnp.concatenate([received, from_partner], axis=1)
    sources = both.shape[0]
    item_count = both.shape[1]
    half_out = expert_half(
        both.reshape(sources * item_count, model_width), gate_half, up_half, down_half
    ).reshape(sources, item_count, model_width)
    mine = half_out[:, : slot_cap // pieces]
    theirs = lax.ppermute(half_out[:, slot_cap // pieces :], "head", swap)
    summed_halves = (mine.astype(jnp.float32) + theirs.astype(jnp.float32)).astype(jnp.bfloat16)
    combined = lax.all_to_all(summed_halves, ("expert", "head"), 0, 0, tiled=True).reshape(
        expert_count * slot_cap, model_width
    )
    expert_out = lax.dot_general(
        slot_table, combined, (((0,), (0,)), ((), ())), preferred_element_type=jnp.float32
    )
    updated = (residual.reshape(rows_dev, model_width) + expert_out).astype(jnp.bfloat16)
    return updated.reshape(cell_count, tables, model_width)


def solution(mesh):
    placed = (
        P(("expert", "head"), None, None),
        P(None, "head"),
        P(None, "head"),
        P(None, "head"),
        P("head", None),
        P(),
        P(("expert", "head"), None, None),
        P(("expert", "head"), None, None),
        P(("expert", "head"), None, None),
        P(),
        P(("expert", "head"), None),
        P(("expert", "head"), None),
    )
    return jax.shard_map(
        shards,
        mesh=mesh,
        in_specs=placed,
        out_specs=P(("expert", "head"), None, None),
        check_vma=False,
    )
```

```python
import functools
import math

import jax
import jax.numpy as jnp
from jax import lax
from jax.experimental import pallas as pl
from jax.experimental.pallas import tpu as pltpu

from jax.sharding import PartitionSpec as P

DH = 128
KEY_BLOCK = 4096


def flash_body(scalars, q_ref, k_ref, v_ref, o_ref, m_ref, l_ref, acc_ref, *, scale, key_block):
    s = pl.program_id(0)
    j = pl.program_id(2)
    last = pl.num_programs(2) - 1
    length = scalars[s]
    start = j * key_block

    @pl.when(j == 0)
    def _():
        m_ref[...] = jnp.full(m_ref.shape, -1e30, jnp.float32)
        l_ref[...] = jnp.zeros(l_ref.shape, jnp.float32)
        acc_ref[...] = jnp.zeros(acc_ref.shape, jnp.float32)

    def update(masked):
        q = q_ref[...]
        k = k_ref[...]
        scores = lax.dot_general(
            q, k, (((1,), (1,)), ((), ())), preferred_element_type=jnp.float32
        ) * scale
        if masked:
            cols = start + lax.broadcasted_iota(jnp.int32, scores.shape, 1)
            scores = jnp.where(cols < length, scores, -jnp.inf)
        m_prev = m_ref[...]
        m_new = jnp.maximum(m_prev, jnp.max(scores, axis=1, keepdims=True))
        alpha = jnp.exp(m_prev - m_new)
        p = jnp.exp(scores - m_new[:, :1])
        l_ref[...] = alpha * l_ref[...] + jnp.sum(p, axis=1, keepdims=True)
        acc_ref[...] = acc_ref[...] * alpha + jnp.dot(
            p.astype(jnp.bfloat16), v_ref[...], preferred_element_type=jnp.float32
        )
        m_ref[...] = m_new

    @pl.when(start + key_block <= length)
    def _():
        update(False)

    @pl.when(jnp.logical_and(start < length, start + key_block > length))
    def _():
        update(True)

    @pl.when(j == last)
    def _():
        rows = scalars[2] + lax.broadcasted_iota(jnp.int32, acc_ref.shape, 0)
        out = acc_ref[...] / l_ref[...]
        o_ref[...] = jnp.where(rows < length, out, 0.0).astype(o_ref.dtype)


def flash_attention(scalars, q_all, kv_all, heads, scale):
    rows = q_all.shape[0]
    keys = kv_all.shape[0]
    tables = scalars.shape[0] - 1
    key_block = KEY_BLOCK
    nk = keys // key_block

    def clamp(j, sc, s):
        return jnp.minimum(j, (sc[s] - 1) // key_block)

    grid_spec = pltpu.PrefetchScalarGridSpec(
        num_scalar_prefetch=1,
        grid=(tables, heads, nk),
        in_specs=[
            pl.BlockSpec((rows, DH), lambda s, h, j, sc: (0, s * heads + h)),
            pl.BlockSpec((key_block, DH), lambda s, h, j, sc: (clamp(j, sc, s), s * 2 * heads + h)),
            pl.BlockSpec(
                (key_block, DH), lambda s, h, j, sc: (clamp(j, sc, s), s * 2 * heads + heads + h)
            ),
        ],
        out_specs=pl.BlockSpec((rows, DH), lambda s, h, j, sc: (0, s * heads + h)),
        scratch_shapes=[
            pltpu.VMEM((rows, DH), jnp.float32),
            pltpu.VMEM((rows, DH), jnp.float32),
            pltpu.VMEM((rows, DH), jnp.float32),
        ],
    )
    flops = 4 * tables * heads * rows * keys * DH
    return pl.pallas_call(
        functools.partial(flash_body, scale=scale, key_block=key_block),
        grid_spec=grid_spec,
        out_shape=jax.ShapeDtypeStruct((rows, tables * heads * DH), jnp.bfloat16),
        compiler_params=pltpu.CompilerParams(
            dimension_semantics=("arbitrary", "arbitrary", "arbitrary")
        ),
        cost_estimate=pl.CostEstimate(
            flops=flops,
            transcendentals=tables * heads * rows * keys,
            bytes_accessed=2 * (q_all.size * 2 + kv_all.size),
        ),
    )(scalars, q_all, kv_all, kv_all)


def expert_half(slot_rows, gate_half, up_half, down_half):
    contract_rows = (((1,), (1,)), ((), ()))
    gate_t = lax.dot_general(
        gate_half, slot_rows, contract_rows, preferred_element_type=jnp.float32
    )
    up_t = lax.dot_general(up_half, slot_rows, contract_rows, preferred_element_type=jnp.float32)
    hidden = (jax.nn.silu(gate_t) * up_t).astype(jnp.bfloat16)
    product = lax.dot_general(
        hidden, down_half, (((0,), (0,)), ((), ())), preferred_element_type=jnp.float32
    )
    return product.astype(jnp.bfloat16)


def shards(
    table_cells,
    w_query,
    w_key,
    w_value,
    w_out,
    norm_gain,
    w_gate,
    w_up,
    w_down,
    lengths,
    expert_of_cell,
    slot_of_cell,
):
    cell_count, tables, model_width = table_cells.shape
    head_width = w_query.shape[1]
    head_count = head_width // DH
    score_scale = 1.0 / math.sqrt(DH)
    cells_flat = table_cells.reshape(cell_count * tables, model_width)
    flat_rows = lax.all_gather(cells_flat, "head", axis=0, tiled=True)
    row_cells = flat_rows.shape[0] // tables
    q_all = (
        jnp.dot(flat_rows, w_query, preferred_element_type=jnp.float32)
        .astype(jnp.bfloat16)
        .reshape(row_cells, tables * head_width)
    )
    kv_weight = jnp.concatenate([w_key, w_value], axis=1)
    kv_rows = (
        jnp.dot(flat_rows, kv_weight, preferred_element_type=jnp.float32)
        .astype(jnp.bfloat16)
        .reshape(row_cells, tables * 2 * head_width)
    )
    kv_all = lax.all_gather(kv_rows, "expert", axis=0, tiled=True)
    offset = lax.axis_index("expert") * row_cells
    scalars = jnp.concatenate(
        [lengths.astype(jnp.int32), jnp.reshape(offset, (1,)).astype(jnp.int32)]
    )
    attended = flash_attention(scalars, q_all, kv_all, head_count, score_scale)
    head_size = lax.axis_size("head")
    me_head = lax.axis_index("head")
    w_parts = [w_out]
    for shift in range(1, head_size):
        w_parts.append(
            lax.ppermute(
                w_out, "head", [(index, (index + shift) % head_size) for index in range(head_size)]
            )
        )
    w_rel = jnp.concatenate(w_parts, axis=0)
    by_owner = lax.all_to_all(
        attended.reshape(head_size, cell_count, tables, head_width), "head", 0, 0, tiled=True
    )
    groups_rel = (me_head - jnp.arange(head_size)) % head_size
    rel = jnp.take(by_owner, groups_rel, axis=0).transpose(1, 2, 0, 3)
    summed = jnp.dot(
        rel.reshape(cell_count * tables, head_size * head_width),
        w_rel,
        preferred_element_type=jnp.float32,
    )
    residual = cells_flat.astype(jnp.float32) + summed
    mean_square = jnp.mean(residual * residual, axis=-1, keepdims=True)
    normed = (residual * lax.rsqrt(mean_square + 1e-06) * norm_gain.astype(jnp.float32)).astype(
        jnp.bfloat16
    )
    rows_dev = cell_count * tables
    normed_rows = normed.reshape(rows_dev, model_width)
    expert_count = lax.axis_size("expert") * lax.axis_size("head") // 2
    slot_cap = 2 * max(1, rows_dev // expert_count)
    target = expert_of_cell.reshape(rows_dev) * slot_cap + slot_of_cell.reshape(rows_dev)
    slot_table = (
        jnp.arange(expert_count * slot_cap, dtype=jnp.int32)[:, None] == target[None, :]
    ).astype(jnp.bfloat16)
    send_rows = jnp.dot(slot_table, normed_rows, preferred_element_type=jnp.float32).astype(
        jnp.bfloat16
    )
    gate_half = w_gate[0]
    up_half = w_up[0]
    down_half = w_down[0]
    pieces = 2
    received = lax.all_to_all(send_rows, ("expert", "head"), 0, 0, tiled=True)
    swap = [(index, index ^ 1) for index in range(lax.axis_size("head"))]
    from_partner = lax.ppermute(received, "head", swap)
    both = jnp.concatenate([received, from_partner], axis=0)
    half_out = expert_half(both, gate_half, up_half, down_half)
    mine = half_out[: received.shape[0]]
    theirs = lax.ppermute(half_out[received.shape[0] :], "head", swap)
    summed_halves = (mine.astype(jnp.float32) + theirs.astype(jnp.float32)).astype(jnp.bfloat16)
    combined = lax.all_to_all(summed_halves, ("expert", "head"), 0, 0, tiled=True)
    expert_out = lax.dot_general(
        slot_table, combined, (((0,), (0,)), ((), ())), preferred_element_type=jnp.float32
    )
    updated = (residual.reshape(rows_dev, model_width) + expert_out).astype(jnp.bfloat16)
    return updated.reshape(cell_count, tables, model_width)


def solution(mesh):
    placed = (
        P(("expert", "head"), None, None),
        P(None, "head"),
        P(None, "head"),
        P(None, "head"),
        P("head", None),
        P(),
        P(("expert", "head"), None, None),
        P(("expert", "head"), None, None),
        P(("expert", "head"), None, None),
        P(),
        P(("expert", "head"), None),
        P(("expert", "head"), None),
    )
    return jax.shard_map(
        shards,
        mesh=mesh,
        in_specs=placed,
        out_specs=P(("expert", "head"), None, None),
        check_vma=False,
    )
```

```python
import functools
import math

import jax
import jax.numpy as jnp
from jax import lax
from jax.experimental import pallas as pl
from jax.experimental.pallas import tpu as pltpu

from jax.sharding import PartitionSpec as P

DH = 128
KEY_BLOCK = 4096


def flash_body(scalars, q_ref, k_ref, v_ref, o_ref, m_ref, l_ref, acc_ref, *, scale, key_block):
    s = pl.program_id(0)
    j = pl.program_id(2)
    last = pl.num_programs(2) - 1
    length = scalars[s]
    start = j * key_block

    @pl.when(j == 0)
    def _():
        m_ref[...] = jnp.full(m_ref.shape, -1e30, jnp.float32)
        l_ref[...] = jnp.zeros(l_ref.shape, jnp.float32)
        acc_ref[...] = jnp.zeros(acc_ref.shape, jnp.float32)

    def update(masked):
        q = q_ref[...]
        k = k_ref[...]
        scores = lax.dot_general(
            q, k, (((1,), (1,)), ((), ())), preferred_element_type=jnp.float32
        ) * scale
        if masked:
            cols = start + lax.broadcasted_iota(jnp.int32, scores.shape, 1)
            scores = jnp.where(cols < length, scores, -jnp.inf)
        m_prev = m_ref[...]
        m_new = jnp.maximum(m_prev, jnp.max(scores, axis=1, keepdims=True))
        alpha = jnp.exp(m_prev - m_new)
        p = jnp.exp(scores - m_new[:, :1])
        l_ref[...] = alpha * l_ref[...] + jnp.sum(p, axis=1, keepdims=True)
        acc_ref[...] = acc_ref[...] * alpha + jnp.dot(
            p.astype(jnp.bfloat16), v_ref[...], preferred_element_type=jnp.float32
        )
        m_ref[...] = m_new

    @pl.when(start + key_block <= length)
    def _():
        update(False)

    @pl.when(jnp.logical_and(start < length, start + key_block > length))
    def _():
        update(True)

    @pl.when(j == last)
    def _():
        rows = scalars[2] + lax.broadcasted_iota(jnp.int32, acc_ref.shape, 0)
        out = acc_ref[...] / l_ref[...]
        o_ref[...] = jnp.where(rows < length, out, 0.0).astype(o_ref.dtype)


def flash_attention(scalars, q_all, kv_all, heads, scale):
    rows = q_all.shape[0]
    keys = kv_all.shape[0]
    tables = scalars.shape[0] - 1
    key_block = KEY_BLOCK
    nk = keys // key_block

    def clamp(j, sc, s):
        return jnp.minimum(j, (sc[s] - 1) // key_block)

    grid_spec = pltpu.PrefetchScalarGridSpec(
        num_scalar_prefetch=1,
        grid=(tables, heads, nk),
        in_specs=[
            pl.BlockSpec((rows, DH), lambda s, h, j, sc: (0, s * heads + h)),
            pl.BlockSpec((key_block, DH), lambda s, h, j, sc: (clamp(j, sc, s), s * 2 * heads + h)),
            pl.BlockSpec(
                (key_block, DH), lambda s, h, j, sc: (clamp(j, sc, s), s * 2 * heads + heads + h)
            ),
        ],
        out_specs=pl.BlockSpec((rows, DH), lambda s, h, j, sc: (0, s * heads + h)),
        scratch_shapes=[
            pltpu.VMEM((rows, DH), jnp.float32),
            pltpu.VMEM((rows, DH), jnp.float32),
            pltpu.VMEM((rows, DH), jnp.float32),
        ],
    )
    flops = 4 * tables * heads * rows * keys * DH
    return pl.pallas_call(
        functools.partial(flash_body, scale=scale, key_block=key_block),
        grid_spec=grid_spec,
        out_shape=jax.ShapeDtypeStruct((rows, tables * heads * DH), jnp.bfloat16),
        compiler_params=pltpu.CompilerParams(
            dimension_semantics=("arbitrary", "arbitrary", "arbitrary")
        ),
        cost_estimate=pl.CostEstimate(
            flops=flops,
            transcendentals=tables * heads * rows * keys,
            bytes_accessed=2 * (q_all.size * 2 + kv_all.size),
        ),
    )(scalars, q_all, kv_all, kv_all)


MESH_ID = pl.DeviceIdType.MESH


def head_gather_body(x_ref, out_ref, send_sem, recv_sem, local_sem, *, size):
    chips = size // 2
    me = lax.axis_index("head")
    core = me % 2
    z = me // 2
    partner = me + 1 - 2 * core

    def peer_of(k):
        return ((z + k) % chips) * 2 + core

    def source_of(k):
        return ((z + chips - k) % chips) * 2 + core

    barrier = pltpu.get_barrier_semaphore()
    for k in range(1, chips):
        pl.semaphore_signal(barrier, 1, device_id={"head": peer_of(k)}, device_id_type=MESH_ID)
    pl.semaphore_signal(barrier, 1, device_id={"head": partner}, device_id_type=MESH_ID)
    pl.semaphore_wait(barrier, chips)

    local = pltpu.make_async_copy(x_ref, out_ref.at[me], local_sem)
    local.start()
    sent = []
    for k in range(1, chips):
        copy = pltpu.make_async_remote_copy(
            x_ref, out_ref.at[me], send_sem.at[k - 1], recv_sem.at[me],
            device_id={"head": peer_of(k)}, device_id_type=MESH_ID,
        )
        copy.start()
        sent.append(copy)
    own = pltpu.make_async_remote_copy(
        x_ref, out_ref.at[me], send_sem.at[chips - 1], recv_sem.at[me],
        device_id={"head": partner}, device_id_type=MESH_ID,
    )
    own.start()
    sent.append(own)
    for k in range(1, chips):
        source = source_of(k)
        arriving = pltpu.make_async_remote_copy(
            x_ref, out_ref.at[source], send_sem.at[k - 1], recv_sem.at[source],
            device_id={"head": source}, device_id_type=MESH_ID,
        )
        arriving.wait_recv()
        forward = pltpu.make_async_remote_copy(
            out_ref.at[source], out_ref.at[source], send_sem.at[chips - 1 + k],
            recv_sem.at[source], device_id={"head": partner}, device_id_type=MESH_ID,
        )
        forward.start()
        sent.append(forward)
    for j in range(chips):
        slot = j * 2 + 1 - core
        arriving = pltpu.make_async_remote_copy(
            x_ref, out_ref.at[slot], send_sem.at[0], recv_sem.at[slot],
            device_id={"head": partner}, device_id_type=MESH_ID,
        )
        arriving.wait_recv()
    local.wait()
    for copy in sent:
        copy.wait_send()


def head_gather(x, size):
    return pl.pallas_call(
        functools.partial(head_gather_body, size=size),
        out_shape=jax.ShapeDtypeStruct((size,) + x.shape, x.dtype),
        in_specs=[pl.BlockSpec(memory_space=pltpu.VMEM)],
        out_specs=pl.BlockSpec(memory_space=pl.ANY),
        scratch_shapes=[
            pltpu.SemaphoreType.DMA((size - 1,)),
            pltpu.SemaphoreType.DMA((size,)),
            pltpu.SemaphoreType.DMA,
        ],
        compiler_params=pltpu.CompilerParams(collective_id=0, has_side_effects=True),
    )(x)


def expert_half(slot_rows, gate_half, up_half, down_half):
    contract_rows = (((1,), (1,)), ((), ()))
    gate_t = lax.dot_general(
        gate_half, slot_rows, contract_rows, preferred_element_type=jnp.float32
    )
    up_t = lax.dot_general(up_half, slot_rows, contract_rows, preferred_element_type=jnp.float32)
    hidden = (jax.nn.silu(gate_t) * up_t).astype(jnp.bfloat16)
    product = lax.dot_general(
        hidden, down_half, (((0,), (0,)), ((), ())), preferred_element_type=jnp.float32
    )
    return product.astype(jnp.bfloat16)


def shards(
    table_cells,
    w_query,
    w_key,
    w_value,
    w_out,
    norm_gain,
    w_gate,
    w_up,
    w_down,
    lengths,
    expert_of_cell,
    slot_of_cell,
):
    cell_count, tables, model_width = table_cells.shape
    head_width = w_query.shape[1]
    head_count = head_width // DH
    score_scale = 1.0 / math.sqrt(DH)
    cells_flat = table_cells.reshape(cell_count * tables, model_width)
    head_size = lax.axis_size("head")
    flat_rows = head_gather(cells_flat, head_size).reshape(
        head_size * cells_flat.shape[0], model_width
    )
    row_cells = flat_rows.shape[0] // tables
    q_all = (
        jnp.dot(flat_rows, w_query, preferred_element_type=jnp.float32)
        .astype(jnp.bfloat16)
        .reshape(row_cells, tables * head_width)
    )
    kv_weight = jnp.concatenate([w_key, w_value], axis=1)
    kv_rows = (
        jnp.dot(flat_rows, kv_weight, preferred_element_type=jnp.float32)
        .astype(jnp.bfloat16)
        .reshape(row_cells, tables * 2 * head_width)
    )
    kv_all = lax.all_gather(kv_rows, "expert", axis=0, tiled=True)
    offset = lax.axis_index("expert") * row_cells
    scalars = jnp.concatenate(
        [lengths.astype(jnp.int32), jnp.reshape(offset, (1,)).astype(jnp.int32)]
    )
    attended = flash_attention(scalars, q_all, kv_all, head_count, score_scale)
    head_size = lax.axis_size("head")
    me_head = lax.axis_index("head")
    w_parts = [w_out]
    for shift in range(1, head_size):
        w_parts.append(
            lax.ppermute(
                w_out, "head", [(index, (index + shift) % head_size) for index in range(head_size)]
            )
        )
    w_rel = jnp.concatenate(w_parts, axis=0)
    by_owner = lax.all_to_all(
        attended.reshape(head_size, cell_count, tables, head_width), "head", 0, 0, tiled=True
    )
    groups_rel = (me_head - jnp.arange(head_size)) % head_size
    rel = jnp.take(by_owner, groups_rel, axis=0).transpose(1, 2, 0, 3)
    summed = jnp.dot(
        rel.reshape(cell_count * tables, head_size * head_width),
        w_rel,
        preferred_element_type=jnp.float32,
    )
    residual = cells_flat.astype(jnp.float32) + summed
    mean_square = jnp.mean(residual * residual, axis=-1, keepdims=True)
    normed = (residual * lax.rsqrt(mean_square + 1e-06) * norm_gain.astype(jnp.float32)).astype(
        jnp.bfloat16
    )
    rows_dev = cell_count * tables
    normed_rows = normed.reshape(rows_dev, model_width)
    expert_count = lax.axis_size("expert") * lax.axis_size("head") // 2
    slot_cap = 2 * max(1, rows_dev // expert_count)
    target = expert_of_cell.reshape(rows_dev) * slot_cap + slot_of_cell.reshape(rows_dev)
    slot_table = (
        jnp.arange(expert_count * slot_cap, dtype=jnp.int32)[:, None] == target[None, :]
    ).astype(jnp.bfloat16)
    send_rows = jnp.dot(slot_table, normed_rows, preferred_element_type=jnp.float32).astype(
        jnp.bfloat16
    )
    gate_half = w_gate[0]
    up_half = w_up[0]
    down_half = w_down[0]
    pieces = 2
    received = lax.all_to_all(send_rows, ("expert", "head"), 0, 0, tiled=True)
    swap = [(index, index ^ 1) for index in range(lax.axis_size("head"))]
    from_partner = lax.ppermute(received, "head", swap)
    both = jnp.concatenate([received, from_partner], axis=0)
    half_out = expert_half(both, gate_half, up_half, down_half)
    mine = half_out[: received.shape[0]]
    theirs = lax.ppermute(half_out[received.shape[0] :], "head", swap)
    summed_halves = (mine.astype(jnp.float32) + theirs.astype(jnp.float32)).astype(jnp.bfloat16)
    combined = lax.all_to_all(summed_halves, ("expert", "head"), 0, 0, tiled=True)
    expert_out = lax.dot_general(
        slot_table, combined, (((0,), (0,)), ((), ())), preferred_element_type=jnp.float32
    )
    updated = (residual.reshape(rows_dev, model_width) + expert_out).astype(jnp.bfloat16)
    return updated.reshape(cell_count, tables, model_width)


def solution(mesh):
    placed = (
        P(("expert", "head"), None, None),
        P(None, "head"),
        P(None, "head"),
        P(None, "head"),
        P("head", None),
        P(),
        P(("expert", "head"), None, None),
        P(("expert", "head"), None, None),
        P(("expert", "head"), None, None),
        P(),
        P(("expert", "head"), None),
        P(("expert", "head"), None),
    )
    return jax.shard_map(
        shards,
        mesh=mesh,
        in_specs=placed,
        out_specs=P(("expert", "head"), None, None),
        check_vma=False,
    )
```

```python
import functools
import math

import jax
import jax.numpy as jnp
from jax import lax
from jax.experimental import pallas as pl
from jax.experimental.pallas import tpu as pltpu

from jax.sharding import PartitionSpec as P

DH = 128
KEY_BLOCK = 4096


def flash_body(scalars, q_ref, k_ref, v_ref, o_ref, m_ref, l_ref, acc_ref, *, scale, key_block):
    s = pl.program_id(0)
    j = pl.program_id(2)
    last = pl.num_programs(2) - 1
    length = scalars[s]
    start = j * key_block

    @pl.when(j == 0)
    def _():
        m_ref[...] = jnp.full(m_ref.shape, -1e30, jnp.float32)
        l_ref[...] = jnp.zeros(l_ref.shape, jnp.float32)
        acc_ref[...] = jnp.zeros(acc_ref.shape, jnp.float32)

    def update(masked):
        q = q_ref[...]
        k = k_ref[...]
        scores = lax.dot_general(
            q, k, (((1,), (1,)), ((), ())), preferred_element_type=jnp.float32
        ) * scale
        if masked:
            cols = start + lax.broadcasted_iota(jnp.int32, scores.shape, 1)
            scores = jnp.where(cols < length, scores, -jnp.inf)
        m_prev = m_ref[...]
        m_new = jnp.maximum(m_prev, jnp.max(scores, axis=1, keepdims=True))
        alpha = jnp.exp(m_prev - m_new)
        p = jnp.exp(scores - m_new[:, :1])
        l_ref[...] = alpha * l_ref[...] + jnp.sum(p, axis=1, keepdims=True)
        acc_ref[...] = acc_ref[...] * alpha + jnp.dot(
            p.astype(jnp.bfloat16), v_ref[...], preferred_element_type=jnp.float32
        )
        m_ref[...] = m_new

    @pl.when(start + key_block <= length)
    def _():
        update(False)

    @pl.when(jnp.logical_and(start < length, start + key_block > length))
    def _():
        update(True)

    @pl.when(j == last)
    def _():
        rows = scalars[2] + lax.broadcasted_iota(jnp.int32, acc_ref.shape, 0)
        out = acc_ref[...] / l_ref[...]
        o_ref[...] = jnp.where(rows < length, out, 0.0).astype(o_ref.dtype)


def flash_attention(scalars, q_all, kv_all, heads, scale):
    rows = q_all.shape[0]
    keys = kv_all.shape[0]
    tables = scalars.shape[0] - 1
    key_block = KEY_BLOCK
    nk = keys // key_block

    def clamp(j, sc, s):
        return jnp.minimum(j, (sc[s] - 1) // key_block)

    grid_spec = pltpu.PrefetchScalarGridSpec(
        num_scalar_prefetch=1,
        grid=(tables, heads, nk),
        in_specs=[
            pl.BlockSpec((rows, DH), lambda s, h, j, sc: (0, s * heads + h)),
            pl.BlockSpec((key_block, DH), lambda s, h, j, sc: (clamp(j, sc, s), s * 2 * heads + h)),
            pl.BlockSpec(
                (key_block, DH), lambda s, h, j, sc: (clamp(j, sc, s), s * 2 * heads + heads + h)
            ),
        ],
        out_specs=pl.BlockSpec((rows, DH), lambda s, h, j, sc: (0, s * heads + h)),
        scratch_shapes=[
            pltpu.VMEM((rows, DH), jnp.float32),
            pltpu.VMEM((rows, DH), jnp.float32),
            pltpu.VMEM((rows, DH), jnp.float32),
        ],
    )
    flops = 4 * tables * heads * rows * keys * DH
    return pl.pallas_call(
        functools.partial(flash_body, scale=scale, key_block=key_block),
        grid_spec=grid_spec,
        out_shape=jax.ShapeDtypeStruct((rows, tables * heads * DH), jnp.bfloat16),
        compiler_params=pltpu.CompilerParams(
            dimension_semantics=("arbitrary", "arbitrary", "arbitrary")
        ),
        cost_estimate=pl.CostEstimate(
            flops=flops,
            transcendentals=tables * heads * rows * keys,
            bytes_accessed=2 * (q_all.size * 2 + kv_all.size),
        ),
    )(scalars, q_all, kv_all, kv_all)


MESH_ID = pl.DeviceIdType.MESH


def head_gather_body(x_ref, out_ref, send_sem, recv_sem, local_sem, *, size):
    chips = size // 2
    me = lax.axis_index("head")
    core = me % 2
    z = me // 2
    partner = me + 1 - 2 * core
    step = 1 - 2 * core
    ahead = ((z + chips + step) % chips) * 2 + core
    behind = ((z + chips - step) % chips) * 2 + core
    far = ((z + 2) % chips) * 2 + core

    def remote(src, slot, sem, device):
        return pltpu.make_async_remote_copy(
            src, out_ref.at[slot], send_sem.at[sem], recv_sem.at[slot],
            device_id={"head": device}, device_id_type=MESH_ID,
        )

    barrier = pltpu.get_barrier_semaphore()
    for device in (ahead, behind, partner):
        pl.semaphore_signal(barrier, 1, device_id={"head": device}, device_id_type=MESH_ID)
    pl.semaphore_wait(barrier, 3)

    local = pltpu.make_async_copy(x_ref, out_ref.at[me], local_sem)
    local.start()
    sent = [remote(x_ref, me, 0, ahead), remote(x_ref, me, 1, behind), remote(x_ref, me, 2, partner)]
    for copy in sent:
        copy.start()
    remote(x_ref, behind, 0, behind).wait_recv()
    relay = remote(out_ref.at[behind], behind, 3, ahead)
    relay.start()
    to_partner = remote(out_ref.at[behind], behind, 4, partner)
    to_partner.start()
    sent += [relay, to_partner]
    remote(x_ref, ahead, 0, ahead).wait_recv()
    to_partner = remote(out_ref.at[ahead], ahead, 5, partner)
    to_partner.start()
    sent.append(to_partner)
    remote(x_ref, far, 0, behind).wait_recv()
    to_partner = remote(out_ref.at[far], far, 6, partner)
    to_partner.start()
    sent.append(to_partner)
    for j in range(chips):
        remote(x_ref, j * 2 + 1 - core, 0, partner).wait_recv()
    local.wait()
    for copy in sent:
        copy.wait_send()


def head_gather(x, size):
    return pl.pallas_call(
        functools.partial(head_gather_body, size=size),
        out_shape=jax.ShapeDtypeStruct((size,) + x.shape, x.dtype),
        in_specs=[pl.BlockSpec(memory_space=pltpu.VMEM)],
        out_specs=pl.BlockSpec(memory_space=pl.ANY),
        scratch_shapes=[
            pltpu.SemaphoreType.DMA((size - 1,)),
            pltpu.SemaphoreType.DMA((size,)),
            pltpu.SemaphoreType.DMA,
        ],
        compiler_params=pltpu.CompilerParams(collective_id=0, has_side_effects=True),
    )(x)


def expert_half(slot_rows, gate_half, up_half, down_half):
    contract_rows = (((1,), (1,)), ((), ()))
    gate_t = lax.dot_general(
        gate_half, slot_rows, contract_rows, preferred_element_type=jnp.float32
    )
    up_t = lax.dot_general(up_half, slot_rows, contract_rows, preferred_element_type=jnp.float32)
    hidden = (jax.nn.silu(gate_t) * up_t).astype(jnp.bfloat16)
    product = lax.dot_general(
        hidden, down_half, (((0,), (0,)), ((), ())), preferred_element_type=jnp.float32
    )
    return product.astype(jnp.bfloat16)


def shards(
    table_cells,
    w_query,
    w_key,
    w_value,
    w_out,
    norm_gain,
    w_gate,
    w_up,
    w_down,
    lengths,
    expert_of_cell,
    slot_of_cell,
):
    cell_count, tables, model_width = table_cells.shape
    head_width = w_query.shape[1]
    head_count = head_width // DH
    score_scale = 1.0 / math.sqrt(DH)
    cells_flat = table_cells.reshape(cell_count * tables, model_width)
    head_size = lax.axis_size("head")
    flat_rows = head_gather(cells_flat, head_size).reshape(
        head_size * cells_flat.shape[0], model_width
    )
    row_cells = flat_rows.shape[0] // tables
    q_all = (
        jnp.dot(flat_rows, w_query, preferred_element_type=jnp.float32)
        .astype(jnp.bfloat16)
        .reshape(row_cells, tables * head_width)
    )
    kv_weight = jnp.concatenate([w_key, w_value], axis=1)
    kv_rows = (
        jnp.dot(flat_rows, kv_weight, preferred_element_type=jnp.float32)
        .astype(jnp.bfloat16)
        .reshape(row_cells, tables * 2 * head_width)
    )
    kv_all = lax.all_gather(kv_rows, "expert", axis=0, tiled=True)
    offset = lax.axis_index("expert") * row_cells
    scalars = jnp.concatenate(
        [lengths.astype(jnp.int32), jnp.reshape(offset, (1,)).astype(jnp.int32)]
    )
    attended = flash_attention(scalars, q_all, kv_all, head_count, score_scale)
    head_size = lax.axis_size("head")
    me_head = lax.axis_index("head")
    w_parts = [w_out]
    for shift in range(1, head_size):
        w_parts.append(
            lax.ppermute(
                w_out, "head", [(index, (index + shift) % head_size) for index in range(head_size)]
            )
        )
    w_rel = jnp.concatenate(w_parts, axis=0)
    by_owner = lax.all_to_all(
        attended.reshape(head_size, cell_count, tables, head_width), "head", 0, 0, tiled=True
    )
    groups_rel = (me_head - jnp.arange(head_size)) % head_size
    rel = jnp.take(by_owner, groups_rel, axis=0).transpose(1, 2, 0, 3)
    summed = jnp.dot(
        rel.reshape(cell_count * tables, head_size * head_width),
        w_rel,
        preferred_element_type=jnp.float32,
    )
    residual = cells_flat.astype(jnp.float32) + summed
    mean_square = jnp.mean(residual * residual, axis=-1, keepdims=True)
    normed = (residual * lax.rsqrt(mean_square + 1e-06) * norm_gain.astype(jnp.float32)).astype(
        jnp.bfloat16
    )
    rows_dev = cell_count * tables
    normed_rows = normed.reshape(rows_dev, model_width)
    expert_count = lax.axis_size("expert") * lax.axis_size("head") // 2
    slot_cap = 2 * max(1, rows_dev // expert_count)
    target = expert_of_cell.reshape(rows_dev) * slot_cap + slot_of_cell.reshape(rows_dev)
    slot_table = (
        jnp.arange(expert_count * slot_cap, dtype=jnp.int32)[:, None] == target[None, :]
    ).astype(jnp.bfloat16)
    send_rows = jnp.dot(slot_table, normed_rows, preferred_element_type=jnp.float32).astype(
        jnp.bfloat16
    )
    gate_half = w_gate[0]
    up_half = w_up[0]
    down_half = w_down[0]
    pieces = 2
    received = lax.all_to_all(send_rows, ("expert", "head"), 0, 0, tiled=True)
    swap = [(index, index ^ 1) for index in range(lax.axis_size("head"))]
    from_partner = lax.ppermute(received, "head", swap)
    both = jnp.concatenate([received, from_partner], axis=0)
    half_out = expert_half(both, gate_half, up_half, down_half)
    mine = half_out[: received.shape[0]]
    theirs = lax.ppermute(half_out[received.shape[0] :], "head", swap)
    summed_halves = (mine.astype(jnp.float32) + theirs.astype(jnp.float32)).astype(jnp.bfloat16)
    combined = lax.all_to_all(summed_halves, ("expert", "head"), 0, 0, tiled=True)
    expert_out = lax.dot_general(
        slot_table, combined, (((0,), (0,)), ((), ())), preferred_element_type=jnp.float32
    )
    updated = (residual.reshape(rows_dev, model_width) + expert_out).astype(jnp.bfloat16)
    return updated.reshape(cell_count, tables, model_width)


def solution(mesh):
    placed = (
        P(("expert", "head"), None, None),
        P(None, "head"),
        P(None, "head"),
        P(None, "head"),
        P("head", None),
        P(),
        P(("expert", "head"), None, None),
        P(("expert", "head"), None, None),
        P(("expert", "head"), None, None),
        P(),
        P(("expert", "head"), None),
        P(("expert", "head"), None),
    )
    return jax.shard_map(
        shards,
        mesh=mesh,
        in_specs=placed,
        out_specs=P(("expert", "head"), None, None),
        check_vma=False,
    )
```

```python
import functools
import math

import jax
import jax.numpy as jnp
from jax import lax
from jax.experimental import pallas as pl
from jax.experimental.pallas import tpu as pltpu

from jax.sharding import PartitionSpec as P

DH = 128
KEY_BLOCK = 4096


def flash_body(scalars, q_ref, k_ref, v_ref, o_ref, m_ref, l_ref, acc_ref, *, scale, key_block):
    s = pl.program_id(0)
    j = pl.program_id(2)
    last = pl.num_programs(2) - 1
    length = scalars[s]
    start = j * key_block

    @pl.when(j == 0)
    def _():
        m_ref[...] = jnp.full(m_ref.shape, -1e30, jnp.float32)
        l_ref[...] = jnp.zeros(l_ref.shape, jnp.float32)
        acc_ref[...] = jnp.zeros(acc_ref.shape, jnp.float32)

    def update(masked):
        q = q_ref[...]
        k = k_ref[...]
        scores = lax.dot_general(
            q, k, (((1,), (1,)), ((), ())), preferred_element_type=jnp.float32
        ) * scale
        if masked:
            cols = start + lax.broadcasted_iota(jnp.int32, scores.shape, 1)
            scores = jnp.where(cols < length, scores, -jnp.inf)
        m_prev = m_ref[...]
        m_new = jnp.maximum(m_prev, jnp.max(scores, axis=1, keepdims=True))
        alpha = jnp.exp(m_prev - m_new)
        p = jnp.exp(scores - m_new[:, :1])
        l_ref[...] = alpha * l_ref[...] + jnp.sum(p, axis=1, keepdims=True)
        acc_ref[...] = acc_ref[...] * alpha + jnp.dot(
            p.astype(jnp.bfloat16), v_ref[...], preferred_element_type=jnp.float32
        )
        m_ref[...] = m_new

    @pl.when(start + key_block <= length)
    def _():
        update(False)

    @pl.when(jnp.logical_and(start < length, start + key_block > length))
    def _():
        update(True)

    @pl.when(j == last)
    def _():
        rows = scalars[2] + lax.broadcasted_iota(jnp.int32, acc_ref.shape, 0)
        out = acc_ref[...] / l_ref[...]
        o_ref[...] = jnp.where(rows < length, out, 0.0).astype(o_ref.dtype)


def flash_attention(scalars, q_all, kv_all, heads, scale):
    rows = q_all.shape[0]
    keys = kv_all.shape[0]
    tables = scalars.shape[0] - 1
    key_block = KEY_BLOCK
    nk = keys // key_block

    def clamp(j, sc, s):
        return jnp.minimum(j, (sc[s] - 1) // key_block)

    grid_spec = pltpu.PrefetchScalarGridSpec(
        num_scalar_prefetch=1,
        grid=(tables, heads, nk),
        in_specs=[
            pl.BlockSpec((rows, DH), lambda s, h, j, sc: (0, s * heads + h)),
            pl.BlockSpec((key_block, DH), lambda s, h, j, sc: (clamp(j, sc, s), s * 2 * heads + h)),
            pl.BlockSpec(
                (key_block, DH), lambda s, h, j, sc: (clamp(j, sc, s), s * 2 * heads + heads + h)
            ),
        ],
        out_specs=pl.BlockSpec((rows, DH), lambda s, h, j, sc: (0, s * heads + h)),
        scratch_shapes=[
            pltpu.VMEM((rows, DH), jnp.float32),
            pltpu.VMEM((rows, DH), jnp.float32),
            pltpu.VMEM((rows, DH), jnp.float32),
        ],
    )
    flops = 4 * tables * heads * rows * keys * DH
    return pl.pallas_call(
        functools.partial(flash_body, scale=scale, key_block=key_block),
        grid_spec=grid_spec,
        out_shape=jax.ShapeDtypeStruct((rows, tables * heads * DH), jnp.bfloat16),
        compiler_params=pltpu.CompilerParams(
            dimension_semantics=("arbitrary", "arbitrary", "arbitrary")
        ),
        cost_estimate=pl.CostEstimate(
            flops=flops,
            transcendentals=tables * heads * rows * keys,
            bytes_accessed=2 * (q_all.size * 2 + kv_all.size),
        ),
    )(scalars, q_all, kv_all, kv_all)


MESH_ID = pl.DeviceIdType.MESH


def head_gather_body(x_ref, out_ref, send_sem, recv_sem, local_sem, *, size):
    chips = size // 2
    me = lax.axis_index("head")
    core = me % 2
    z = me // 2
    partner = me + 1 - 2 * core
    step = 1 - 2 * core
    ahead = ((z + chips + step) % chips) * 2 + core
    behind = ((z + chips - step) % chips) * 2 + core
    far = ((z + 2) % chips) * 2 + core

    def remote(src, slot, sem, device):
        return pltpu.make_async_remote_copy(
            src, out_ref.at[slot], send_sem.at[sem], recv_sem.at[slot],
            device_id={"head": device}, device_id_type=MESH_ID,
        )

    barrier = pltpu.get_barrier_semaphore()
    for device in (ahead, behind, partner):
        pl.semaphore_signal(barrier, 1, device_id={"head": device}, device_id_type=MESH_ID)
    pl.semaphore_wait(barrier, 3)

    local = pltpu.make_async_copy(x_ref, out_ref.at[me], local_sem)
    local.start()
    sent = [remote(x_ref, me, 0, ahead), remote(x_ref, me, 1, behind), remote(x_ref, me, 2, partner)]
    for copy in sent:
        copy.start()
    remote(x_ref, behind, 0, behind).wait_recv()
    relay = remote(out_ref.at[behind], behind, 3, ahead)
    relay.start()
    to_partner = remote(out_ref.at[behind], behind, 4, partner)
    to_partner.start()
    sent += [relay, to_partner]
    remote(x_ref, ahead, 0, ahead).wait_recv()
    to_partner = remote(out_ref.at[ahead], ahead, 5, partner)
    to_partner.start()
    sent.append(to_partner)
    remote(x_ref, far, 0, behind).wait_recv()
    to_partner = remote(out_ref.at[far], far, 6, partner)
    to_partner.start()
    sent.append(to_partner)
    for j in range(chips):
        remote(x_ref, j * 2 + 1 - core, 0, partner).wait_recv()
    local.wait()
    for copy in sent:
        copy.wait_send()


def head_gather(x, size):
    return pl.pallas_call(
        functools.partial(head_gather_body, size=size),
        out_shape=jax.ShapeDtypeStruct((size,) + x.shape, x.dtype),
        in_specs=[pl.BlockSpec(memory_space=pltpu.VMEM)],
        out_specs=pl.BlockSpec(memory_space=pl.ANY),
        scratch_shapes=[
            pltpu.SemaphoreType.DMA((size - 1,)),
            pltpu.SemaphoreType.DMA((size,)),
            pltpu.SemaphoreType.DMA,
        ],
        compiler_params=pltpu.CompilerParams(collective_id=0, has_side_effects=True),
    )(x)


def expert_half(slot_rows, gate_half, up_half, down_half):
    contract_rows = (((1,), (1,)), ((), ()))
    gate_t = lax.dot_general(
        gate_half, slot_rows, contract_rows, preferred_element_type=jnp.float32
    )
    up_t = lax.dot_general(up_half, slot_rows, contract_rows, preferred_element_type=jnp.float32)
    hidden = (jax.nn.silu(gate_t) * up_t).astype(jnp.bfloat16)
    product = lax.dot_general(
        hidden, down_half, (((0,), (0,)), ((), ())), preferred_element_type=jnp.float32
    )
    return product.astype(jnp.bfloat16)


def shards(
    table_cells,
    w_query,
    w_key,
    w_value,
    w_out,
    norm_gain,
    w_gate,
    w_up,
    w_down,
    lengths,
    expert_of_cell,
    slot_of_cell,
):
    cell_count, tables, model_width = table_cells.shape
    head_width = w_query.shape[1]
    head_count = head_width // DH
    score_scale = 1.0 / math.sqrt(DH)
    cells_flat = table_cells.reshape(cell_count * tables, model_width)
    head_size = lax.axis_size("head")
    flat_rows = head_gather(cells_flat, head_size).reshape(
        head_size * cells_flat.shape[0], model_width
    )
    row_cells = flat_rows.shape[0] // tables
    q_all = (
        jnp.dot(flat_rows, w_query, preferred_element_type=jnp.float32)
        .astype(jnp.bfloat16)
        .reshape(row_cells, tables * head_width)
    )
    kv_weight = jnp.concatenate([w_key, w_value], axis=1)
    kv_rows = (
        jnp.dot(flat_rows, kv_weight, preferred_element_type=jnp.float32)
        .astype(jnp.bfloat16)
        .reshape(row_cells, tables * 2 * head_width)
    )
    kv_all = lax.all_gather(kv_rows, "expert", axis=0, tiled=True)
    offset = lax.axis_index("expert") * row_cells
    scalars = jnp.concatenate(
        [lengths.astype(jnp.int32), jnp.reshape(offset, (1,)).astype(jnp.int32)]
    )
    attended = flash_attention(scalars, q_all, kv_all, head_count, score_scale)
    head_size = lax.axis_size("head")
    me_head = lax.axis_index("head")
    w_parts = [w_out]
    for shift in range(1, head_size):
        w_parts.append(
            lax.ppermute(
                w_out, "head", [(index, (index + shift) % head_size) for index in range(head_size)]
            )
        )
    by_owner = lax.all_to_all(
        attended.reshape(head_size, cell_count, tables, head_width), "head", 0, 0, tiled=True
    )
    groups_rel = (me_head - jnp.arange(head_size)) % head_size
    rel = jnp.take(by_owner, groups_rel, axis=0).reshape(head_size, cell_count * tables, head_width)
    summed = jnp.dot(rel[0], w_parts[0], preferred_element_type=jnp.float32)
    for shift in range(1, head_size):
        summed = summed + jnp.dot(rel[shift], w_parts[shift], preferred_element_type=jnp.float32)
    residual = cells_flat.astype(jnp.float32) + summed
    mean_square = jnp.mean(residual * residual, axis=-1, keepdims=True)
    normed = (residual * lax.rsqrt(mean_square + 1e-06) * norm_gain.astype(jnp.float32)).astype(
        jnp.bfloat16
    )
    rows_dev = cell_count * tables
    normed_rows = normed.reshape(rows_dev, model_width)
    expert_count = lax.axis_size("expert") * lax.axis_size("head") // 2
    slot_cap = 2 * max(1, rows_dev // expert_count)
    target = expert_of_cell.reshape(rows_dev) * slot_cap + slot_of_cell.reshape(rows_dev)
    slot_table = (
        jnp.arange(expert_count * slot_cap, dtype=jnp.int32)[:, None] == target[None, :]
    ).astype(jnp.bfloat16)
    send_rows = jnp.dot(slot_table, normed_rows, preferred_element_type=jnp.float32).astype(
        jnp.bfloat16
    )
    gate_half = w_gate[0]
    up_half = w_up[0]
    down_half = w_down[0]
    pieces = 2
    received = lax.all_to_all(send_rows, ("expert", "head"), 0, 0, tiled=True)
    swap = [(index, index ^ 1) for index in range(lax.axis_size("head"))]
    from_partner = lax.ppermute(received, "head", swap)
    both = jnp.concatenate([received, from_partner], axis=0)
    half_out = expert_half(both, gate_half, up_half, down_half)
    mine = half_out[: received.shape[0]]
    theirs = lax.ppermute(half_out[received.shape[0] :], "head", swap)
    summed_halves = (mine.astype(jnp.float32) + theirs.astype(jnp.float32)).astype(jnp.bfloat16)
    combined = lax.all_to_all(summed_halves, ("expert", "head"), 0, 0, tiled=True)
    expert_out = lax.dot_general(
        slot_table, combined, (((0,), (0,)), ((), ())), preferred_element_type=jnp.float32
    )
    updated = (residual.reshape(rows_dev, model_width) + expert_out).astype(jnp.bfloat16)
    return updated.reshape(cell_count, tables, model_width)


def solution(mesh):
    placed = (
        P(("expert", "head"), None, None),
        P(None, "head"),
        P(None, "head"),
        P(None, "head"),
        P("head", None),
        P(),
        P(("expert", "head"), None, None),
        P(("expert", "head"), None, None),
        P(("expert", "head"), None, None),
        P(),
        P(("expert", "head"), None),
        P(("expert", "head"), None),
    )
    return jax.shard_map(
        shards,
        mesh=mesh,
        in_specs=placed,
        out_specs=P(("expert", "head"), None, None),
        check_vma=False,
    )
```

```python
import functools
import math

import jax
import jax.numpy as jnp
from jax import lax
from jax.experimental import pallas as pl
from jax.experimental.pallas import tpu as pltpu

from jax.sharding import PartitionSpec as P

DH = 128
KEY_BLOCK = 4096


def flash_body(scalars, q_ref, k_ref, v_ref, o_ref, m_ref, l_ref, acc_ref, *, scale, key_block):
    s = pl.program_id(0)
    j = pl.program_id(2)
    last = pl.num_programs(2) - 1
    length = scalars[s]
    start = j * key_block

    @pl.when(j == 0)
    def _():
        m_ref[...] = jnp.full(m_ref.shape, -1e30, jnp.float32)
        l_ref[...] = jnp.zeros(l_ref.shape, jnp.float32)
        acc_ref[...] = jnp.zeros(acc_ref.shape, jnp.float32)

    def update(masked):
        q = q_ref[...]
        k = k_ref[...]
        scores = lax.dot_general(
            q, k, (((1,), (1,)), ((), ())), preferred_element_type=jnp.float32
        ) * scale
        if masked:
            cols = start + lax.broadcasted_iota(jnp.int32, scores.shape, 1)
            scores = jnp.where(cols < length, scores, -jnp.inf)
        m_prev = m_ref[...]
        m_new = jnp.maximum(m_prev, jnp.max(scores, axis=1, keepdims=True))
        alpha = jnp.exp(m_prev - m_new)
        p = jnp.exp(scores - m_new[:, :1])
        l_ref[...] = alpha * l_ref[...] + jnp.sum(p, axis=1, keepdims=True)
        acc_ref[...] = acc_ref[...] * alpha + jnp.dot(
            p.astype(jnp.bfloat16), v_ref[...], preferred_element_type=jnp.float32
        )
        m_ref[...] = m_new

    @pl.when(start + key_block <= length)
    def _():
        update(False)

    @pl.when(jnp.logical_and(start < length, start + key_block > length))
    def _():
        update(True)

    @pl.when(j == last)
    def _():
        rows = scalars[2] + lax.broadcasted_iota(jnp.int32, acc_ref.shape, 0)
        out = acc_ref[...] / l_ref[...]
        o_ref[...] = jnp.where(rows < length, out, 0.0).astype(o_ref.dtype)


def flash_attention(scalars, q_all, kv_all, heads, scale):
    rows = q_all.shape[0]
    keys = kv_all.shape[0]
    tables = scalars.shape[0] - 1
    key_block = KEY_BLOCK
    nk = keys // key_block

    def clamp(j, sc, s):
        return jnp.minimum(j, (sc[s] - 1) // key_block)

    grid_spec = pltpu.PrefetchScalarGridSpec(
        num_scalar_prefetch=1,
        grid=(tables, heads, nk),
        in_specs=[
            pl.BlockSpec((rows, DH), lambda s, h, j, sc: (0, s * heads + h)),
            pl.BlockSpec((key_block, DH), lambda s, h, j, sc: (clamp(j, sc, s), s * 2 * heads + h)),
            pl.BlockSpec(
                (key_block, DH), lambda s, h, j, sc: (clamp(j, sc, s), s * 2 * heads + heads + h)
            ),
        ],
        out_specs=pl.BlockSpec((rows, DH), lambda s, h, j, sc: (0, s * heads + h)),
        scratch_shapes=[
            pltpu.VMEM((rows, DH), jnp.float32),
            pltpu.VMEM((rows, DH), jnp.float32),
            pltpu.VMEM((rows, DH), jnp.float32),
        ],
    )
    flops = 4 * tables * heads * rows * keys * DH
    return pl.pallas_call(
        functools.partial(flash_body, scale=scale, key_block=key_block),
        grid_spec=grid_spec,
        out_shape=jax.ShapeDtypeStruct((rows, tables * heads * DH), jnp.bfloat16),
        compiler_params=pltpu.CompilerParams(
            dimension_semantics=("arbitrary", "arbitrary", "arbitrary")
        ),
        cost_estimate=pl.CostEstimate(
            flops=flops,
            transcendentals=tables * heads * rows * keys,
            bytes_accessed=2 * (q_all.size * 2 + kv_all.size),
        ),
    )(scalars, q_all, kv_all, kv_all)


MESH_ID = pl.DeviceIdType.MESH
GATHER_PARTS = 2


def head_gather_body(x_ref, out_ref, send_sem, recv_sem, local_sem, *, size, parts):
    chips = size // 2
    me = lax.axis_index("head")
    core = me % 2
    z = me // 2
    partner = me + 1 - 2 * core
    step = 1 - 2 * core
    ahead = ((z + chips + step) % chips) * 2 + core
    behind = ((z + chips - step) % chips) * 2 + core
    far = ((z + 2) % chips) * 2 + core
    rows = x_ref.shape[0] // parts

    def remote(src, slot, part, sem, device):
        piece = pl.ds(part * rows, rows)
        return pltpu.make_async_remote_copy(
            src.at[piece], out_ref.at[slot, piece], send_sem.at[sem * parts + part],
            recv_sem.at[slot * parts + part], device_id={"head": device}, device_id_type=MESH_ID,
        )

    barrier = pltpu.get_barrier_semaphore()
    for device in (ahead, behind, partner):
        pl.semaphore_signal(barrier, 1, device_id={"head": device}, device_id_type=MESH_ID)
    pl.semaphore_wait(barrier, 3)

    local = pltpu.make_async_copy(x_ref, out_ref.at[me], local_sem)
    local.start()
    sent = []
    for part in range(parts):
        for sem, device in ((0, ahead), (1, behind), (2, partner)):
            copy = remote(x_ref, me, part, sem, device)
            copy.start()
            sent.append(copy)
    for part in range(parts):
        remote(x_ref, behind, part, 0, behind).wait_recv()
        for sem, device in ((3, ahead), (4, partner)):
            copy = remote(out_ref.at[behind], behind, part, sem, device)
            copy.start()
            sent.append(copy)
    for part in range(parts):
        remote(x_ref, ahead, part, 0, ahead).wait_recv()
        copy = remote(out_ref.at[ahead], ahead, part, 5, partner)
        copy.start()
        sent.append(copy)
    for part in range(parts):
        remote(x_ref, far, part, 0, behind).wait_recv()
        copy = remote(out_ref.at[far], far, part, 6, partner)
        copy.start()
        sent.append(copy)
    for j in range(chips):
        for part in range(parts):
            remote(x_ref, j * 2 + 1 - core, part, 0, partner).wait_recv()
    local.wait()
    for copy in sent:
        copy.wait_send()


def head_gather(x, size):
    return pl.pallas_call(
        functools.partial(head_gather_body, size=size, parts=GATHER_PARTS),
        out_shape=jax.ShapeDtypeStruct((size,) + x.shape, x.dtype),
        in_specs=[pl.BlockSpec(memory_space=pltpu.VMEM)],
        out_specs=pl.BlockSpec(memory_space=pl.ANY),
        scratch_shapes=[
            pltpu.SemaphoreType.DMA(((size - 1) * GATHER_PARTS,)),
            pltpu.SemaphoreType.DMA((size * GATHER_PARTS,)),
            pltpu.SemaphoreType.DMA,
        ],
        compiler_params=pltpu.CompilerParams(collective_id=0, has_side_effects=True),
    )(x)


def expert_half(slot_rows, gate_half, up_half, down_half):
    contract_rows = (((1,), (1,)), ((), ()))
    gate_t = lax.dot_general(
        gate_half, slot_rows, contract_rows, preferred_element_type=jnp.float32
    )
    up_t = lax.dot_general(up_half, slot_rows, contract_rows, preferred_element_type=jnp.float32)
    hidden = (jax.nn.silu(gate_t) * up_t).astype(jnp.bfloat16)
    product = lax.dot_general(
        hidden, down_half, (((0,), (0,)), ((), ())), preferred_element_type=jnp.float32
    )
    return product.astype(jnp.bfloat16)


def shards(
    table_cells,
    w_query,
    w_key,
    w_value,
    w_out,
    norm_gain,
    w_gate,
    w_up,
    w_down,
    lengths,
    expert_of_cell,
    slot_of_cell,
):
    cell_count, tables, model_width = table_cells.shape
    head_width = w_query.shape[1]
    head_count = head_width // DH
    score_scale = 1.0 / math.sqrt(DH)
    cells_flat = table_cells.reshape(cell_count * tables, model_width)
    head_size = lax.axis_size("head")
    flat_rows = head_gather(cells_flat, head_size).reshape(
        head_size * cells_flat.shape[0], model_width
    )
    row_cells = flat_rows.shape[0] // tables
    q_all = (
        jnp.dot(flat_rows, w_query, preferred_element_type=jnp.float32)
        .astype(jnp.bfloat16)
        .reshape(row_cells, tables * head_width)
    )
    kv_weight = jnp.concatenate([w_key, w_value], axis=1)
    kv_rows = (
        jnp.dot(flat_rows, kv_weight, preferred_element_type=jnp.float32)
        .astype(jnp.bfloat16)
        .reshape(row_cells, tables * 2 * head_width)
    )
    kv_all = lax.all_gather(kv_rows, "expert", axis=0, tiled=True)
    offset = lax.axis_index("expert") * row_cells
    scalars = jnp.concatenate(
        [lengths.astype(jnp.int32), jnp.reshape(offset, (1,)).astype(jnp.int32)]
    )
    attended = flash_attention(scalars, q_all, kv_all, head_count, score_scale)
    head_size = lax.axis_size("head")
    me_head = lax.axis_index("head")
    w_parts = [w_out]
    for shift in range(1, head_size):
        w_parts.append(
            lax.ppermute(
                w_out, "head", [(index, (index + shift) % head_size) for index in range(head_size)]
            )
        )
    w_rel = jnp.concatenate(w_parts, axis=0)
    by_owner = lax.all_to_all(
        attended.reshape(head_size, cell_count, tables, head_width), "head", 0, 0, tiled=True
    )
    groups_rel = (me_head - jnp.arange(head_size)) % head_size
    rel = jnp.take(by_owner, groups_rel, axis=0).transpose(1, 2, 0, 3)
    summed = jnp.dot(
        rel.reshape(cell_count * tables, head_size * head_width),
        w_rel,
        preferred_element_type=jnp.float32,
    )
    residual = cells_flat.astype(jnp.float32) + summed
    mean_square = jnp.mean(residual * residual, axis=-1, keepdims=True)
    normed = (residual * lax.rsqrt(mean_square + 1e-06) * norm_gain.astype(jnp.float32)).astype(
        jnp.bfloat16
    )
    rows_dev = cell_count * tables
    normed_rows = normed.reshape(rows_dev, model_width)
    expert_count = lax.axis_size("expert") * lax.axis_size("head") // 2
    slot_cap = 2 * max(1, rows_dev // expert_count)
    target = expert_of_cell.reshape(rows_dev) * slot_cap + slot_of_cell.reshape(rows_dev)
    slot_table = (
        jnp.arange(expert_count * slot_cap, dtype=jnp.int32)[:, None] == target[None, :]
    ).astype(jnp.bfloat16)
    send_rows = jnp.dot(slot_table, normed_rows, preferred_element_type=jnp.float32).astype(
        jnp.bfloat16
    )
    gate_half = w_gate[0]
    up_half = w_up[0]
    down_half = w_down[0]
    pieces = 2
    received = lax.all_to_all(send_rows, ("expert", "head"), 0, 0, tiled=True)
    swap = [(index, index ^ 1) for index in range(lax.axis_size("head"))]
    from_partner = lax.ppermute(received, "head", swap)
    both = jnp.concatenate([received, from_partner], axis=0)
    half_out = expert_half(both, gate_half, up_half, down_half)
    mine = half_out[: received.shape[0]]
    theirs = lax.ppermute(half_out[received.shape[0] :], "head", swap)
    summed_halves = (mine.astype(jnp.float32) + theirs.astype(jnp.float32)).astype(jnp.bfloat16)
    combined = lax.all_to_all(summed_halves, ("expert", "head"), 0, 0, tiled=True)
    expert_out = lax.dot_general(
        slot_table, combined, (((0,), (0,)), ((), ())), preferred_element_type=jnp.float32
    )
    updated = (residual.reshape(rows_dev, model_width) + expert_out).astype(jnp.bfloat16)
    return updated.reshape(cell_count, tables, model_width)


def solution(mesh):
    placed = (
        P(("expert", "head"), None, None),
        P(None, "head"),
        P(None, "head"),
        P(None, "head"),
        P("head", None),
        P(),
        P(("expert", "head"), None, None),
        P(("expert", "head"), None, None),
        P(("expert", "head"), None, None),
        P(),
        P(("expert", "head"), None),
        P(("expert", "head"), None),
    )
    return jax.shard_map(
        shards,
        mesh=mesh,
        in_specs=placed,
        out_specs=P(("expert", "head"), None, None),
        check_vma=False,
    )
```

```python
import functools
import math

import jax
import jax.numpy as jnp
from jax import lax
from jax.experimental import pallas as pl
from jax.experimental.pallas import tpu as pltpu

from jax.sharding import PartitionSpec as P

DH = 128
KEY_BLOCK = 4096


def flash_body(scalars, q_ref, k_ref, v_ref, o_ref, m_ref, l_ref, acc_ref, *, scale, key_block):
    s = pl.program_id(0)
    j = pl.program_id(2)
    last = pl.num_programs(2) - 1
    length = scalars[s]
    start = j * key_block

    @pl.when(j == 0)
    def _():
        m_ref[...] = jnp.full(m_ref.shape, -1e30, jnp.float32)
        l_ref[...] = jnp.zeros(l_ref.shape, jnp.float32)
        acc_ref[...] = jnp.zeros(acc_ref.shape, jnp.float32)

    def update(masked):
        q = q_ref[...]
        k = k_ref[...]
        scores = lax.dot_general(
            q, k, (((1,), (1,)), ((), ())), preferred_element_type=jnp.float32
        ) * scale
        if masked:
            cols = start + lax.broadcasted_iota(jnp.int32, scores.shape, 1)
            scores = jnp.where(cols < length, scores, -jnp.inf)
        m_prev = m_ref[...]
        m_new = jnp.maximum(m_prev, jnp.max(scores, axis=1, keepdims=True))
        alpha = jnp.exp(m_prev - m_new)
        p = jnp.exp(scores - m_new[:, :1])
        l_ref[...] = alpha * l_ref[...] + jnp.sum(p, axis=1, keepdims=True)
        acc_ref[...] = acc_ref[...] * alpha + jnp.dot(
            p.astype(jnp.bfloat16), v_ref[...], preferred_element_type=jnp.float32
        )
        m_ref[...] = m_new

    @pl.when(start + key_block <= length)
    def _():
        update(False)

    @pl.when(jnp.logical_and(start < length, start + key_block > length))
    def _():
        update(True)

    @pl.when(j == last)
    def _():
        rows = scalars[2] + lax.broadcasted_iota(jnp.int32, acc_ref.shape, 0)
        out = acc_ref[...] / l_ref[...]
        o_ref[...] = jnp.where(rows < length, out, 0.0).astype(o_ref.dtype)


def flash_attention(scalars, q_all, kv_all, heads, scale):
    rows = q_all.shape[0]
    keys = kv_all.shape[0]
    tables = scalars.shape[0] - 1
    key_block = KEY_BLOCK
    nk = keys // key_block

    def clamp(j, sc, s):
        return jnp.minimum(j, (sc[s] - 1) // key_block)

    grid_spec = pltpu.PrefetchScalarGridSpec(
        num_scalar_prefetch=1,
        grid=(tables, heads, nk),
        in_specs=[
            pl.BlockSpec((rows, DH), lambda s, h, j, sc: (0, s * heads + h)),
            pl.BlockSpec((key_block, DH), lambda s, h, j, sc: (clamp(j, sc, s), s * 2 * heads + h)),
            pl.BlockSpec(
                (key_block, DH), lambda s, h, j, sc: (clamp(j, sc, s), s * 2 * heads + heads + h)
            ),
        ],
        out_specs=pl.BlockSpec((rows, DH), lambda s, h, j, sc: (0, s * heads + h)),
        scratch_shapes=[
            pltpu.VMEM((rows, DH), jnp.float32),
            pltpu.VMEM((rows, DH), jnp.float32),
            pltpu.VMEM((rows, DH), jnp.float32),
        ],
    )
    flops = 4 * tables * heads * rows * keys * DH
    return pl.pallas_call(
        functools.partial(flash_body, scale=scale, key_block=key_block),
        grid_spec=grid_spec,
        out_shape=jax.ShapeDtypeStruct((rows, tables * heads * DH), jnp.bfloat16),
        compiler_params=pltpu.CompilerParams(
            dimension_semantics=("arbitrary", "arbitrary", "arbitrary")
        ),
        cost_estimate=pl.CostEstimate(
            flops=flops,
            transcendentals=tables * heads * rows * keys,
            bytes_accessed=2 * (q_all.size * 2 + kv_all.size),
        ),
    )(scalars, q_all, kv_all, kv_all)


MESH_ID = pl.DeviceIdType.MESH
GATHER_PARTS = 4


def head_gather_body(x_ref, out_ref, send_sem, recv_sem, local_sem, *, size, parts):
    chips = size // 2
    me = lax.axis_index("head")
    core = me % 2
    z = me // 2
    partner = me + 1 - 2 * core
    step = 1 - 2 * core
    ahead = ((z + chips + step) % chips) * 2 + core
    behind = ((z + chips - step) % chips) * 2 + core
    far = ((z + 2) % chips) * 2 + core
    rows = x_ref.shape[0] // parts

    def remote(src, slot, part, sem, device):
        piece = pl.ds(part * rows, rows)
        return pltpu.make_async_remote_copy(
            src.at[piece], out_ref.at[slot, piece], send_sem.at[sem * parts + part],
            recv_sem.at[slot * parts + part], device_id={"head": device}, device_id_type=MESH_ID,
        )

    barrier = pltpu.get_barrier_semaphore()
    for device in (ahead, behind, partner):
        pl.semaphore_signal(barrier, 1, device_id={"head": device}, device_id_type=MESH_ID)
    pl.semaphore_wait(barrier, 3)

    local = pltpu.make_async_copy(x_ref, out_ref.at[me], local_sem)
    local.start()
    sent = []
    for part in range(parts):
        for sem, device in ((0, ahead), (1, behind), (2, partner)):
            copy = remote(x_ref, me, part, sem, device)
            copy.start()
            sent.append(copy)
    for part in range(parts):
        remote(x_ref, behind, part, 0, behind).wait_recv()
        for sem, device in ((3, ahead), (4, partner)):
            copy = remote(out_ref.at[behind], behind, part, sem, device)
            copy.start()
            sent.append(copy)
    for part in range(parts):
        remote(x_ref, ahead, part, 0, ahead).wait_recv()
        copy = remote(out_ref.at[ahead], ahead, part, 5, partner)
        copy.start()
        sent.append(copy)
    for part in range(parts):
        remote(x_ref, far, part, 0, behind).wait_recv()
        copy = remote(out_ref.at[far], far, part, 6, partner)
        copy.start()
        sent.append(copy)
    for j in range(chips):
        for part in range(parts):
            remote(x_ref, j * 2 + 1 - core, part, 0, partner).wait_recv()
    local.wait()
    for copy in sent:
        copy.wait_send()


def head_gather(x, size):
    return pl.pallas_call(
        functools.partial(head_gather_body, size=size, parts=GATHER_PARTS),
        out_shape=jax.ShapeDtypeStruct((size,) + x.shape, x.dtype),
        in_specs=[pl.BlockSpec(memory_space=pltpu.VMEM)],
        out_specs=pl.BlockSpec(memory_space=pl.ANY),
        scratch_shapes=[
            pltpu.SemaphoreType.DMA(((size - 1) * GATHER_PARTS,)),
            pltpu.SemaphoreType.DMA((size * GATHER_PARTS,)),
            pltpu.SemaphoreType.DMA,
        ],
        compiler_params=pltpu.CompilerParams(collective_id=0, has_side_effects=True),
    )(x)


def expert_half(slot_rows, gate_half, up_half, down_half):
    contract_rows = (((1,), (1,)), ((), ()))
    gate_t = lax.dot_general(
        gate_half, slot_rows, contract_rows, preferred_element_type=jnp.float32
    )
    up_t = lax.dot_general(up_half, slot_rows, contract_rows, preferred_element_type=jnp.float32)
    hidden = (jax.nn.silu(gate_t) * up_t).astype(jnp.bfloat16)
    product = lax.dot_general(
        hidden, down_half, (((0,), (0,)), ((), ())), preferred_element_type=jnp.float32
    )
    return product.astype(jnp.bfloat16)


def shards(
    table_cells,
    w_query,
    w_key,
    w_value,
    w_out,
    norm_gain,
    w_gate,
    w_up,
    w_down,
    lengths,
    expert_of_cell,
    slot_of_cell,
):
    cell_count, tables, model_width = table_cells.shape
    head_width = w_query.shape[1]
    head_count = head_width // DH
    score_scale = 1.0 / math.sqrt(DH)
    cells_flat = table_cells.reshape(cell_count * tables, model_width)
    head_size = lax.axis_size("head")
    flat_rows = head_gather(cells_flat, head_size).reshape(
        head_size * cells_flat.shape[0], model_width
    )
    row_cells = flat_rows.shape[0] // tables
    q_all = (
        jnp.dot(flat_rows, w_query, preferred_element_type=jnp.float32)
        .astype(jnp.bfloat16)
        .reshape(row_cells, tables * head_width)
    )
    kv_weight = jnp.concatenate([w_key, w_value], axis=1)
    kv_rows = (
        jnp.dot(flat_rows, kv_weight, preferred_element_type=jnp.float32)
        .astype(jnp.bfloat16)
        .reshape(row_cells, tables * 2 * head_width)
    )
    kv_all = lax.all_gather(kv_rows, "expert", axis=0, tiled=True)
    offset = lax.axis_index("expert") * row_cells
    scalars = jnp.concatenate(
        [lengths.astype(jnp.int32), jnp.reshape(offset, (1,)).astype(jnp.int32)]
    )
    attended = flash_attention(scalars, q_all, kv_all, head_count, score_scale)
    head_size = lax.axis_size("head")
    me_head = lax.axis_index("head")
    w_parts = [w_out]
    for shift in range(1, head_size):
        w_parts.append(
            lax.ppermute(
                w_out, "head", [(index, (index + shift) % head_size) for index in range(head_size)]
            )
        )
    w_rel = jnp.concatenate(w_parts, axis=0)
    by_owner = lax.all_to_all(
        attended.reshape(head_size, cell_count, tables, head_width), "head", 0, 0, tiled=True
    )
    groups_rel = (me_head - jnp.arange(head_size)) % head_size
    rel = jnp.take(by_owner, groups_rel, axis=0).transpose(1, 2, 0, 3)
    summed = jnp.dot(
        rel.reshape(cell_count * tables, head_size * head_width),
        w_rel,
        preferred_element_type=jnp.float32,
    )
    residual = cells_flat.astype(jnp.float32) + summed
    mean_square = jnp.mean(residual * residual, axis=-1, keepdims=True)
    normed = (residual * lax.rsqrt(mean_square + 1e-06) * norm_gain.astype(jnp.float32)).astype(
        jnp.bfloat16
    )
    rows_dev = cell_count * tables
    normed_rows = normed.reshape(rows_dev, model_width)
    expert_count = lax.axis_size("expert") * lax.axis_size("head") // 2
    slot_cap = 2 * max(1, rows_dev // expert_count)
    target = expert_of_cell.reshape(rows_dev) * slot_cap + slot_of_cell.reshape(rows_dev)
    slot_table = (
        jnp.arange(expert_count * slot_cap, dtype=jnp.int32)[:, None] == target[None, :]
    ).astype(jnp.bfloat16)
    send_rows = jnp.dot(slot_table, normed_rows, preferred_element_type=jnp.float32).astype(
        jnp.bfloat16
    )
    gate_half = w_gate[0]
    up_half = w_up[0]
    down_half = w_down[0]
    pieces = 2
    received = lax.all_to_all(send_rows, ("expert", "head"), 0, 0, tiled=True)
    swap = [(index, index ^ 1) for index in range(lax.axis_size("head"))]
    from_partner = lax.ppermute(received, "head", swap)
    both = jnp.concatenate([received, from_partner], axis=0)
    half_out = expert_half(both, gate_half, up_half, down_half)
    mine = half_out[: received.shape[0]]
    theirs = lax.ppermute(half_out[received.shape[0] :], "head", swap)
    summed_halves = (mine.astype(jnp.float32) + theirs.astype(jnp.float32)).astype(jnp.bfloat16)
    combined = lax.all_to_all(summed_halves, ("expert", "head"), 0, 0, tiled=True)
    expert_out = lax.dot_general(
        slot_table, combined, (((0,), (0,)), ((), ())), preferred_element_type=jnp.float32
    )
    updated = (residual.reshape(rows_dev, model_width) + expert_out).astype(jnp.bfloat16)
    return updated.reshape(cell_count, tables, model_width)


def solution(mesh):
    placed = (
        P(("expert", "head"), None, None),
        P(None, "head"),
        P(None, "head"),
        P(None, "head"),
        P("head", None),
        P(),
        P(("expert", "head"), None, None),
        P(("expert", "head"), None, None),
        P(("expert", "head"), None, None),
        P(),
        P(("expert", "head"), None),
        P(("expert", "head"), None),
    )
    return jax.shard_map(
        shards,
        mesh=mesh,
        in_specs=placed,
        out_specs=P(("expert", "head"), None, None),
        check_vma=False,
    )
```

```python
import functools
import math

import jax
import jax.numpy as jnp
from jax import lax
from jax.experimental import pallas as pl
from jax.experimental.pallas import tpu as pltpu

from jax.sharding import PartitionSpec as P

DH = 128
KEY_BLOCK = 4096


def flash_body(scalars, q_ref, k_ref, v_ref, o_ref, m_ref, l_ref, acc_ref, *, scale, key_block):
    s = pl.program_id(0)
    j = pl.program_id(2)
    last = pl.num_programs(2) - 1
    length = scalars[s]
    start = j * key_block

    @pl.when(j == 0)
    def _():
        m_ref[...] = jnp.full(m_ref.shape, -1e30, jnp.float32)
        l_ref[...] = jnp.zeros(l_ref.shape, jnp.float32)
        acc_ref[...] = jnp.zeros(acc_ref.shape, jnp.float32)

    def update(masked):
        q = q_ref[...]
        k = k_ref[...].reshape(-1, DH)
        scores = lax.dot_general(
            q, k, (((1,), (1,)), ((), ())), preferred_element_type=jnp.float32
        ) * scale
        if masked:
            cols = start + lax.broadcasted_iota(jnp.int32, scores.shape, 1)
            scores = jnp.where(cols < length, scores, -jnp.inf)
        m_prev = m_ref[...]
        m_new = jnp.maximum(m_prev, jnp.max(scores, axis=1, keepdims=True))
        alpha = jnp.exp(m_prev - m_new)
        p = jnp.exp(scores - m_new[:, :1])
        l_ref[...] = alpha * l_ref[...] + jnp.sum(p, axis=1, keepdims=True)
        acc_ref[...] = acc_ref[...] * alpha + jnp.dot(
            p.astype(jnp.bfloat16), v_ref[...].reshape(-1, DH), preferred_element_type=jnp.float32
        )
        m_ref[...] = m_new

    @pl.when(start + key_block <= length)
    def _():
        update(False)

    @pl.when(jnp.logical_and(start < length, start + key_block > length))
    def _():
        update(True)

    @pl.when(j == last)
    def _():
        rows = scalars[2] + lax.broadcasted_iota(jnp.int32, acc_ref.shape, 0)
        out = acc_ref[...] / l_ref[...]
        o_ref[...] = jnp.where(rows < length, out, 0.0).astype(o_ref.dtype)


def flash_attention(scalars, q_all, kv_all, heads, scale):
    rows = q_all.shape[1]
    keys = kv_all.shape[0] * kv_all.shape[2]
    tables = scalars.shape[0] - 1
    per_block = KEY_BLOCK // kv_all.shape[2]
    key_block = KEY_BLOCK
    nk = keys // key_block

    def clamp(j, sc, s):
        return jnp.minimum(j, (sc[s] - 1) // key_block)

    grid_spec = pltpu.PrefetchScalarGridSpec(
        num_scalar_prefetch=1,
        grid=(tables, heads, nk),
        in_specs=[
            pl.BlockSpec((pl.squeezed, rows, DH), lambda s, h, j, sc: (s, 0, h)),
            pl.BlockSpec(
                (per_block, pl.squeezed, kv_all.shape[2], DH),
                lambda s, h, j, sc: (clamp(j, sc, s), s, 0, h),
            ),
            pl.BlockSpec(
                (per_block, pl.squeezed, kv_all.shape[2], DH),
                lambda s, h, j, sc: (clamp(j, sc, s), s, 0, heads + h),
            ),
        ],
        out_specs=pl.BlockSpec((rows, DH), lambda s, h, j, sc: (0, s * heads + h)),
        scratch_shapes=[
            pltpu.VMEM((rows, DH), jnp.float32),
            pltpu.VMEM((rows, DH), jnp.float32),
            pltpu.VMEM((rows, DH), jnp.float32),
        ],
    )
    flops = 4 * tables * heads * rows * keys * DH
    return pl.pallas_call(
        functools.partial(flash_body, scale=scale, key_block=key_block),
        grid_spec=grid_spec,
        out_shape=jax.ShapeDtypeStruct((rows, tables * heads * DH), jnp.bfloat16),
        compiler_params=pltpu.CompilerParams(
            dimension_semantics=("arbitrary", "arbitrary", "arbitrary")
        ),
        cost_estimate=pl.CostEstimate(
            flops=flops,
            transcendentals=tables * heads * rows * keys,
            bytes_accessed=2 * (q_all.size * 2 + kv_all.size),
        ),
    )(scalars, q_all, kv_all, kv_all)


MESH_ID = pl.DeviceIdType.MESH
GATHER_PARTS = 2


def head_gather_body(x_ref, out_ref, send_sem, recv_sem, local_sem, *, size, parts):
    chips = size // 2
    me = lax.axis_index("head")
    core = me % 2
    z = me // 2
    partner = me + 1 - 2 * core
    step = 1 - 2 * core
    ahead = ((z + chips + step) % chips) * 2 + core
    behind = ((z + chips - step) % chips) * 2 + core
    far = ((z + 2) % chips) * 2 + core
    rows = x_ref.shape[1] // parts

    def remote(src, slot, part, sem, device):
        piece = pl.ds(part * rows, rows)
        return pltpu.make_async_remote_copy(
            src.at[:, piece], out_ref.at[:, slot, piece], send_sem.at[sem * parts + part],
            recv_sem.at[slot * parts + part], device_id={"head": device}, device_id_type=MESH_ID,
        )

    barrier = pltpu.get_barrier_semaphore()
    for device in (ahead, behind, partner):
        pl.semaphore_signal(barrier, 1, device_id={"head": device}, device_id_type=MESH_ID)
    pl.semaphore_wait(barrier, 3)

    local = pltpu.make_async_copy(x_ref, out_ref.at[:, me], local_sem)
    local.start()
    sent = []
    for part in range(parts):
        for sem, device in ((0, ahead), (1, behind), (2, partner)):
            copy = remote(x_ref, me, part, sem, device)
            copy.start()
            sent.append(copy)
    for part in range(parts):
        remote(x_ref, behind, part, 0, behind).wait_recv()
        for sem, device in ((3, ahead), (4, partner)):
            copy = remote(out_ref.at[:, behind], behind, part, sem, device)
            copy.start()
            sent.append(copy)
    for part in range(parts):
        remote(x_ref, ahead, part, 0, ahead).wait_recv()
        copy = remote(out_ref.at[:, ahead], ahead, part, 5, partner)
        copy.start()
        sent.append(copy)
    for part in range(parts):
        remote(x_ref, far, part, 0, behind).wait_recv()
        copy = remote(out_ref.at[:, far], far, part, 6, partner)
        copy.start()
        sent.append(copy)
    for j in range(chips):
        for part in range(parts):
            remote(x_ref, j * 2 + 1 - core, part, 0, partner).wait_recv()
    local.wait()
    for copy in sent:
        copy.wait_send()


def head_gather(x, size):
    return pl.pallas_call(
        functools.partial(head_gather_body, size=size, parts=GATHER_PARTS),
        out_shape=jax.ShapeDtypeStruct((x.shape[0], size) + x.shape[1:], x.dtype),
        in_specs=[pl.BlockSpec(memory_space=pltpu.VMEM)],
        out_specs=pl.BlockSpec(memory_space=pl.ANY),
        scratch_shapes=[
            pltpu.SemaphoreType.DMA(((size - 1) * GATHER_PARTS,)),
            pltpu.SemaphoreType.DMA((size * GATHER_PARTS,)),
            pltpu.SemaphoreType.DMA,
        ],
        compiler_params=pltpu.CompilerParams(collective_id=0, has_side_effects=True),
    )(x)


def expert_half(slot_rows, gate_half, up_half, down_half):
    contract_rows = (((1,), (1,)), ((), ()))
    gate_t = lax.dot_general(
        gate_half, slot_rows, contract_rows, preferred_element_type=jnp.float32
    )
    up_t = lax.dot_general(up_half, slot_rows, contract_rows, preferred_element_type=jnp.float32)
    hidden = (jax.nn.silu(gate_t) * up_t).astype(jnp.bfloat16)
    product = lax.dot_general(
        hidden, down_half, (((0,), (0,)), ((), ())), preferred_element_type=jnp.float32
    )
    return product.astype(jnp.bfloat16)


def shards(
    table_cells,
    w_query,
    w_key,
    w_value,
    w_out,
    norm_gain,
    w_gate,
    w_up,
    w_down,
    lengths,
    expert_of_cell,
    slot_of_cell,
):
    cell_count, tables, model_width = table_cells.shape
    head_width = w_query.shape[1]
    head_count = head_width // DH
    score_scale = 1.0 / math.sqrt(DH)
    cells_flat = table_cells.reshape(cell_count * tables, model_width)
    head_size = lax.axis_size("head")
    by_table = head_gather(table_cells.transpose(1, 0, 2), head_size)
    row_cells = head_size * cell_count
    by_table = by_table.reshape(tables, row_cells, model_width)
    q_all = jnp.einsum(
        "tcd,dk->tck", by_table, w_query, preferred_element_type=jnp.float32
    ).astype(jnp.bfloat16)
    kv_weight = jnp.concatenate([w_key, w_value], axis=1)
    kv_rows = jnp.einsum(
        "tcd,dk->tck", by_table, kv_weight, preferred_element_type=jnp.float32
    ).astype(jnp.bfloat16)
    kv_all = lax.all_gather(kv_rows, "expert", axis=0, tiled=False)
    offset = lax.axis_index("expert") * row_cells
    scalars = jnp.concatenate(
        [lengths.astype(jnp.int32), jnp.reshape(offset, (1,)).astype(jnp.int32)]
    )
    attended = flash_attention(scalars, q_all, kv_all, head_count, score_scale)
    head_size = lax.axis_size("head")
    me_head = lax.axis_index("head")
    w_parts = [w_out]
    for shift in range(1, head_size):
        w_parts.append(
            lax.ppermute(
                w_out, "head", [(index, (index + shift) % head_size) for index in range(head_size)]
            )
        )
    w_rel = jnp.concatenate(w_parts, axis=0)
    by_owner = lax.all_to_all(
        attended.reshape(head_size, cell_count, tables, head_width), "head", 0, 0, tiled=True
    )
    groups_rel = (me_head - jnp.arange(head_size)) % head_size
    rel = jnp.take(by_owner, groups_rel, axis=0).transpose(1, 2, 0, 3)
    summed = jnp.dot(
        rel.reshape(cell_count * tables, head_size * head_width),
        w_rel,
        preferred_element_type=jnp.float32,
    )
    residual = cells_flat.astype(jnp.float32) + summed
    mean_square = jnp.mean(residual * residual, axis=-1, keepdims=True)
    normed = (residual * lax.rsqrt(mean_square + 1e-06) * norm_gain.astype(jnp.float32)).astype(
        jnp.bfloat16
    )
    rows_dev = cell_count * tables
    normed_rows = normed.reshape(rows_dev, model_width)
    expert_count = lax.axis_size("expert") * lax.axis_size("head") // 2
    slot_cap = 2 * max(1, rows_dev // expert_count)
    target = expert_of_cell.reshape(rows_dev) * slot_cap + slot_of_cell.reshape(rows_dev)
    slot_table = (
        jnp.arange(expert_count * slot_cap, dtype=jnp.int32)[:, None] == target[None, :]
    ).astype(jnp.bfloat16)
    send_rows = jnp.dot(slot_table, normed_rows, preferred_element_type=jnp.float32).astype(
        jnp.bfloat16
    )
    gate_half = w_gate[0]
    up_half = w_up[0]
    down_half = w_down[0]
    pieces = 2
    received = lax.all_to_all(send_rows, ("expert", "head"), 0, 0, tiled=True)
    swap = [(index, index ^ 1) for index in range(lax.axis_size("head"))]
    from_partner = lax.ppermute(received, "head", swap)
    both = jnp.concatenate([received, from_partner], axis=0)
    half_out = expert_half(both, gate_half, up_half, down_half)
    mine = half_out[: received.shape[0]]
    theirs = lax.ppermute(half_out[received.shape[0] :], "head", swap)
    summed_halves = (mine.astype(jnp.float32) + theirs.astype(jnp.float32)).astype(jnp.bfloat16)
    combined = lax.all_to_all(summed_halves, ("expert", "head"), 0, 0, tiled=True)
    expert_out = lax.dot_general(
        slot_table, combined, (((0,), (0,)), ((), ())), preferred_element_type=jnp.float32
    )
    updated = (residual.reshape(rows_dev, model_width) + expert_out).astype(jnp.bfloat16)
    return updated.reshape(cell_count, tables, model_width)


def solution(mesh):
    placed = (
        P(("expert", "head"), None, None),
        P(None, "head"),
        P(None, "head"),
        P(None, "head"),
        P("head", None),
        P(),
        P(("expert", "head"), None, None),
        P(("expert", "head"), None, None),
        P(("expert", "head"), None, None),
        P(),
        P(("expert", "head"), None),
        P(("expert", "head"), None),
    )
    return jax.shard_map(
        shards,
        mesh=mesh,
        in_specs=placed,
        out_specs=P(("expert", "head"), None, None),
        check_vma=False,
    )
```

```python
import functools
import math

import jax
import jax.numpy as jnp
from jax import lax
from jax.experimental import pallas as pl
from jax.experimental.pallas import tpu as pltpu

from jax.sharding import PartitionSpec as P

DH = 128
KEY_BLOCK = 4096


def flash_body(scalars, q_ref, k_ref, v_ref, o_ref, m_ref, l_ref, acc_ref, *, scale, key_block):
    s = pl.program_id(0)
    j = pl.program_id(2)
    last = pl.num_programs(2) - 1
    length = scalars[s]
    start = j * key_block

    @pl.when(j == 0)
    def _():
        m_ref[...] = jnp.full(m_ref.shape, -1e30, jnp.float32)
        l_ref[...] = jnp.zeros(l_ref.shape, jnp.float32)
        acc_ref[...] = jnp.zeros(acc_ref.shape, jnp.float32)

    def update(masked):
        q = q_ref[...]
        k = k_ref[...]
        scores = lax.dot_general(
            q, k, (((1,), (1,)), ((), ())), preferred_element_type=jnp.float32
        ) * scale
        if masked:
            cols = start + lax.broadcasted_iota(jnp.int32, scores.shape, 1)
            scores = jnp.where(cols < length, scores, -jnp.inf)
        m_prev = m_ref[...]
        m_new = jnp.maximum(m_prev, jnp.max(scores, axis=1, keepdims=True))
        alpha = jnp.exp(m_prev - m_new)
        p = jnp.exp(scores - m_new[:, :1])
        l_ref[...] = alpha * l_ref[...] + jnp.sum(p, axis=1, keepdims=True)
        acc_ref[...] = acc_ref[...] * alpha + jnp.dot(
            p.astype(jnp.bfloat16), v_ref[...], preferred_element_type=jnp.float32
        )
        m_ref[...] = m_new

    @pl.when(start + key_block <= length)
    def _():
        update(False)

    @pl.when(jnp.logical_and(start < length, start + key_block > length))
    def _():
        update(True)

    @pl.when(j == last)
    def _():
        rows = scalars[2] + lax.broadcasted_iota(jnp.int32, acc_ref.shape, 0)
        out = acc_ref[...] / l_ref[...]
        o_ref[...] = jnp.where(rows < length, out, 0.0).astype(o_ref.dtype)


def flash_attention(scalars, q_all, kv_all, heads, scale):
    rows = q_all.shape[0]
    keys = kv_all.shape[0]
    tables = scalars.shape[0] - 1
    key_block = KEY_BLOCK
    nk = keys // key_block

    def clamp(j, sc, s):
        return jnp.minimum(j, (sc[s] - 1) // key_block)

    grid_spec = pltpu.PrefetchScalarGridSpec(
        num_scalar_prefetch=1,
        grid=(tables, heads, nk),
        in_specs=[
            pl.BlockSpec((rows, DH), lambda s, h, j, sc: (0, s * heads + h)),
            pl.BlockSpec((key_block, DH), lambda s, h, j, sc: (clamp(j, sc, s), s * 2 * heads + h)),
            pl.BlockSpec(
                (key_block, DH), lambda s, h, j, sc: (clamp(j, sc, s), s * 2 * heads + heads + h)
            ),
        ],
        out_specs=pl.BlockSpec((rows, DH), lambda s, h, j, sc: (0, s * heads + h)),
        scratch_shapes=[
            pltpu.VMEM((rows, DH), jnp.float32),
            pltpu.VMEM((rows, DH), jnp.float32),
            pltpu.VMEM((rows, DH), jnp.float32),
        ],
    )
    flops = 4 * tables * heads * rows * keys * DH
    return pl.pallas_call(
        functools.partial(flash_body, scale=scale, key_block=key_block),
        grid_spec=grid_spec,
        out_shape=jax.ShapeDtypeStruct((rows, tables * heads * DH), jnp.bfloat16),
        compiler_params=pltpu.CompilerParams(
            dimension_semantics=("arbitrary", "arbitrary", "arbitrary")
        ),
        cost_estimate=pl.CostEstimate(
            flops=flops,
            transcendentals=tables * heads * rows * keys,
            bytes_accessed=2 * (q_all.size * 2 + kv_all.size),
        ),
    )(scalars, q_all, kv_all, kv_all)


MESH_ID = pl.DeviceIdType.MESH
GATHER_PARTS = 2


def head_gather_body(x_ref, out_ref, send_sem, recv_sem, local_sem, *, size, parts):
    chips = size // 2
    me = lax.axis_index("head")
    core = me % 2
    z = me // 2
    partner = me + 1 - 2 * core
    step = 1 - 2 * core
    ahead = ((z + chips + step) % chips) * 2 + core
    behind = ((z + chips - step) % chips) * 2 + core
    far = ((z + 2) % chips) * 2 + core
    rows = x_ref.shape[0] // parts

    def remote(src, slot, part, sem, device):
        piece = pl.ds(part * rows, rows)
        return pltpu.make_async_remote_copy(
            src.at[piece], out_ref.at[slot, piece], send_sem.at[sem * parts + part],
            recv_sem.at[slot * parts + part], device_id={"head": device}, device_id_type=MESH_ID,
        )

    barrier = pltpu.get_barrier_semaphore()
    for device in (ahead, behind, partner):
        pl.semaphore_signal(barrier, 1, device_id={"head": device}, device_id_type=MESH_ID)
    pl.semaphore_wait(barrier, 3)

    sent = []
    for part in range(parts):
        for sem, device in ((0, ahead), (1, behind), (2, partner)):
            copy = remote(x_ref, me, part, sem, device)
            copy.start()
            sent.append(copy)
    local = pltpu.make_async_copy(x_ref, out_ref.at[me], local_sem)
    local.start()
    for part in range(parts):
        remote(x_ref, behind, part, 0, behind).wait_recv()
        for sem, device in ((3, ahead), (4, partner)):
            copy = remote(out_ref.at[behind], behind, part, sem, device)
            copy.start()
            sent.append(copy)
    for part in range(parts):
        remote(x_ref, ahead, part, 0, ahead).wait_recv()
        copy = remote(out_ref.at[ahead], ahead, part, 5, partner)
        copy.start()
        sent.append(copy)
    for part in range(parts):
        remote(x_ref, far, part, 0, behind).wait_recv()
        copy = remote(out_ref.at[far], far, part, 6, partner)
        copy.start()
        sent.append(copy)
    for j in range(chips):
        for part in range(parts):
            remote(x_ref, j * 2 + 1 - core, part, 0, partner).wait_recv()
    local.wait()
    for copy in sent:
        copy.wait_send()


def head_gather(x, size):
    return pl.pallas_call(
        functools.partial(head_gather_body, size=size, parts=GATHER_PARTS),
        out_shape=jax.ShapeDtypeStruct((size,) + x.shape, x.dtype),
        in_specs=[pl.BlockSpec(memory_space=pltpu.VMEM)],
        out_specs=pl.BlockSpec(memory_space=pl.ANY),
        scratch_shapes=[
            pltpu.SemaphoreType.DMA(((size - 1) * GATHER_PARTS,)),
            pltpu.SemaphoreType.DMA((size * GATHER_PARTS,)),
            pltpu.SemaphoreType.DMA,
        ],
        compiler_params=pltpu.CompilerParams(collective_id=0, has_side_effects=True),
    )(x)


def expert_half(slot_rows, gate_half, up_half, down_half):
    contract_rows = (((1,), (1,)), ((), ()))
    gate_t = lax.dot_general(
        gate_half, slot_rows, contract_rows, preferred_element_type=jnp.float32
    )
    up_t = lax.dot_general(up_half, slot_rows, contract_rows, preferred_element_type=jnp.float32)
    hidden = (jax.nn.silu(gate_t) * up_t).astype(jnp.bfloat16)
    product = lax.dot_general(
        hidden, down_half, (((0,), (0,)), ((), ())), preferred_element_type=jnp.float32
    )
    return product.astype(jnp.bfloat16)


def shards(
    table_cells,
    w_query,
    w_key,
    w_value,
    w_out,
    norm_gain,
    w_gate,
    w_up,
    w_down,
    lengths,
    expert_of_cell,
    slot_of_cell,
):
    cell_count, tables, model_width = table_cells.shape
    head_width = w_query.shape[1]
    head_count = head_width // DH
    score_scale = 1.0 / math.sqrt(DH)
    cells_flat = table_cells.reshape(cell_count * tables, model_width)
    head_size = lax.axis_size("head")
    flat_rows = head_gather(cells_flat, head_size).reshape(
        head_size * cells_flat.shape[0], model_width
    )
    row_cells = flat_rows.shape[0] // tables
    q_all = (
        jnp.dot(flat_rows, w_query, preferred_element_type=jnp.float32)
        .astype(jnp.bfloat16)
        .reshape(row_cells, tables * head_width)
    )
    kv_weight = jnp.concatenate([w_key, w_value], axis=1)
    kv_rows = (
        jnp.dot(flat_rows, kv_weight, preferred_element_type=jnp.float32)
        .astype(jnp.bfloat16)
        .reshape(row_cells, tables * 2 * head_width)
    )
    kv_all = lax.all_gather(kv_rows, "expert", axis=0, tiled=True)
    offset = lax.axis_index("expert") * row_cells
    scalars = jnp.concatenate(
        [lengths.astype(jnp.int32), jnp.reshape(offset, (1,)).astype(jnp.int32)]
    )
    attended = flash_attention(scalars, q_all, kv_all, head_count, score_scale)
    head_size = lax.axis_size("head")
    me_head = lax.axis_index("head")
    w_parts = [w_out]
    for shift in range(1, head_size):
        w_parts.append(
            lax.ppermute(
                w_out, "head", [(index, (index + shift) % head_size) for index in range(head_size)]
            )
        )
    w_rel = jnp.concatenate(w_parts, axis=0)
    by_owner = lax.all_to_all(
        attended.reshape(head_size, cell_count, tables, head_width), "head", 0, 0, tiled=True
    )
    groups_rel = (me_head - jnp.arange(head_size)) % head_size
    rel = jnp.take(by_owner, groups_rel, axis=0).transpose(1, 2, 0, 3)
    summed = jnp.dot(
        rel.reshape(cell_count * tables, head_size * head_width),
        w_rel,
        preferred_element_type=jnp.float32,
    )
    residual = cells_flat.astype(jnp.float32) + summed
    mean_square = jnp.mean(residual * residual, axis=-1, keepdims=True)
    normed = (residual * lax.rsqrt(mean_square + 1e-06) * norm_gain.astype(jnp.float32)).astype(
        jnp.bfloat16
    )
    rows_dev = cell_count * tables
    normed_rows = normed.reshape(rows_dev, model_width)
    expert_count = lax.axis_size("expert") * lax.axis_size("head") // 2
    slot_cap = 2 * max(1, rows_dev // expert_count)
    target = expert_of_cell.reshape(rows_dev) * slot_cap + slot_of_cell.reshape(rows_dev)
    slot_table = (
        jnp.arange(expert_count * slot_cap, dtype=jnp.int32)[:, None] == target[None, :]
    ).astype(jnp.bfloat16)
    send_rows = jnp.dot(slot_table, normed_rows, preferred_element_type=jnp.float32).astype(
        jnp.bfloat16
    )
    gate_half = w_gate[0]
    up_half = w_up[0]
    down_half = w_down[0]
    pieces = 2
    received = lax.all_to_all(send_rows, ("expert", "head"), 0, 0, tiled=True)
    swap = [(index, index ^ 1) for index in range(lax.axis_size("head"))]
    from_partner = lax.ppermute(received, "head", swap)
    both = jnp.concatenate([received, from_partner], axis=0)
    half_out = expert_half(both, gate_half, up_half, down_half)
    mine = half_out[: received.shape[0]]
    theirs = lax.ppermute(half_out[received.shape[0] :], "head", swap)
    summed_halves = (mine.astype(jnp.float32) + theirs.astype(jnp.float32)).astype(jnp.bfloat16)
    combined = lax.all_to_all(summed_halves, ("expert", "head"), 0, 0, tiled=True)
    expert_out = lax.dot_general(
        slot_table, combined, (((0,), (0,)), ((), ())), preferred_element_type=jnp.float32
    )
    updated = (residual.reshape(rows_dev, model_width) + expert_out).astype(jnp.bfloat16)
    return updated.reshape(cell_count, tables, model_width)


def solution(mesh):
    placed = (
        P(("expert", "head"), None, None),
        P(None, "head"),
        P(None, "head"),
        P(None, "head"),
        P("head", None),
        P(),
        P(("expert", "head"), None, None),
        P(("expert", "head"), None, None),
        P(("expert", "head"), None, None),
        P(),
        P(("expert", "head"), None),
        P(("expert", "head"), None),
    )
    return jax.shard_map(
        shards,
        mesh=mesh,
        in_specs=placed,
        out_specs=P(("expert", "head"), None, None),
        check_vma=False,
    )
```

```python
import functools
import math

import jax
import jax.numpy as jnp
from jax import lax
from jax.experimental import pallas as pl
from jax.experimental.pallas import tpu as pltpu

from jax.sharding import PartitionSpec as P

DH = 128
KEY_BLOCK = 4096


def flash_body(scalars, q_ref, k_ref, v_ref, o_ref, m_ref, l_ref, acc_ref, *, scale, key_block):
    s = pl.program_id(0)
    j = pl.program_id(2)
    last = pl.num_programs(2) - 1
    length = scalars[s]
    start = j * key_block

    @pl.when(j == 0)
    def _():
        m_ref[...] = jnp.full(m_ref.shape, -1e30, jnp.float32)
        l_ref[...] = jnp.zeros(l_ref.shape, jnp.float32)
        acc_ref[...] = jnp.zeros(acc_ref.shape, jnp.float32)

    def update(masked):
        q = q_ref[...]
        k = k_ref[...]
        scores = lax.dot_general(
            q, k, (((1,), (1,)), ((), ())), preferred_element_type=jnp.float32
        ) * scale
        if masked:
            cols = start + lax.broadcasted_iota(jnp.int32, scores.shape, 1)
            scores = jnp.where(cols < length, scores, -jnp.inf)
        m_prev = m_ref[...]
        m_new = jnp.maximum(m_prev, jnp.max(scores, axis=1, keepdims=True))
        alpha = jnp.exp(m_prev - m_new)
        p = jnp.exp(scores - m_new[:, :1])
        l_ref[...] = alpha * l_ref[...] + jnp.sum(p, axis=1, keepdims=True)
        acc_ref[...] = acc_ref[...] * alpha + jnp.dot(
            p.astype(jnp.bfloat16), v_ref[...], preferred_element_type=jnp.float32
        )
        m_ref[...] = m_new

    @pl.when(start + key_block <= length)
    def _():
        update(False)

    @pl.when(jnp.logical_and(start < length, start + key_block > length))
    def _():
        update(True)

    @pl.when(j == last)
    def _():
        rows = scalars[2] + lax.broadcasted_iota(jnp.int32, acc_ref.shape, 0)
        out = acc_ref[...] / l_ref[...]
        o_ref[...] = jnp.where(rows < length, out, 0.0).astype(o_ref.dtype)


def flash_attention(scalars, q_all, kv_all, heads, scale):
    rows = q_all.shape[0]
    keys = kv_all.shape[0]
    tables = scalars.shape[0] - 1
    key_block = KEY_BLOCK
    nk = keys // key_block

    def clamp(j, sc, s):
        return jnp.minimum(j, (sc[s] - 1) // key_block)

    grid_spec = pltpu.PrefetchScalarGridSpec(
        num_scalar_prefetch=1,
        grid=(tables, heads, nk),
        in_specs=[
            pl.BlockSpec((rows, DH), lambda s, h, j, sc: (0, s * heads + h)),
            pl.BlockSpec((key_block, DH), lambda s, h, j, sc: (clamp(j, sc, s), s * 2 * heads + h)),
            pl.BlockSpec(
                (key_block, DH), lambda s, h, j, sc: (clamp(j, sc, s), s * 2 * heads + heads + h)
            ),
        ],
        out_specs=pl.BlockSpec((rows, DH), lambda s, h, j, sc: (0, s * heads + h)),
        scratch_shapes=[
            pltpu.VMEM((rows, DH), jnp.float32),
            pltpu.VMEM((rows, DH), jnp.float32),
            pltpu.VMEM((rows, DH), jnp.float32),
        ],
    )
    flops = 4 * tables * heads * rows * keys * DH
    return pl.pallas_call(
        functools.partial(flash_body, scale=scale, key_block=key_block),
        grid_spec=grid_spec,
        out_shape=jax.ShapeDtypeStruct((rows, tables * heads * DH), jnp.bfloat16),
        compiler_params=pltpu.CompilerParams(
            dimension_semantics=("arbitrary", "arbitrary", "arbitrary")
        ),
        cost_estimate=pl.CostEstimate(
            flops=flops,
            transcendentals=tables * heads * rows * keys,
            bytes_accessed=2 * (q_all.size * 2 + kv_all.size),
        ),
    )(scalars, q_all, kv_all, kv_all)


MESH_ID = pl.DeviceIdType.MESH
GATHER_PARTS = 2


def head_gather_body(x_ref, out_ref, send_sem, recv_sem, local_sem, *, size, parts):
    chips = size // 2
    me = lax.axis_index("head")
    core = me % 2
    z = me // 2
    partner = me + 1 - 2 * core
    step = 1 - 2 * core
    ahead = ((z + chips + step) % chips) * 2 + core
    behind = ((z + chips - step) % chips) * 2 + core
    far = ((z + 2) % chips) * 2 + core
    rows = x_ref.shape[0] // parts

    def remote(src, slot, part, sem, device):
        piece = pl.ds(part * rows, rows)
        return pltpu.make_async_remote_copy(
            src.at[piece], out_ref.at[slot, piece], send_sem.at[sem * parts + part],
            recv_sem.at[slot * parts + part], device_id={"head": device}, device_id_type=MESH_ID,
        )

    barrier = pltpu.get_barrier_semaphore()
    for device in (ahead, behind, partner):
        pl.semaphore_signal(barrier, 1, device_id={"head": device}, device_id_type=MESH_ID)
    pl.semaphore_wait(barrier, 3)

    local = pltpu.make_async_copy(x_ref, out_ref.at[me], local_sem)
    local.start()
    sent = []
    for sem, device in ((0, ahead), (1, behind), (2, partner)):
        for part in range(parts):
            copy = remote(x_ref, me, part, sem, device)
            copy.start()
            sent.append(copy)
    for part in range(parts):
        remote(x_ref, behind, part, 0, behind).wait_recv()
        for sem, device in ((3, ahead), (4, partner)):
            copy = remote(out_ref.at[behind], behind, part, sem, device)
            copy.start()
            sent.append(copy)
    for part in range(parts):
        remote(x_ref, ahead, part, 0, ahead).wait_recv()
        copy = remote(out_ref.at[ahead], ahead, part, 5, partner)
        copy.start()
        sent.append(copy)
    for part in range(parts):
        remote(x_ref, far, part, 0, behind).wait_recv()
        copy = remote(out_ref.at[far], far, part, 6, partner)
        copy.start()
        sent.append(copy)
    for j in range(chips):
        for part in range(parts):
            remote(x_ref, j * 2 + 1 - core, part, 0, partner).wait_recv()
    local.wait()
    for copy in sent:
        copy.wait_send()


def head_gather(x, size):
    return pl.pallas_call(
        functools.partial(head_gather_body, size=size, parts=GATHER_PARTS),
        out_shape=jax.ShapeDtypeStruct((size,) + x.shape, x.dtype),
        in_specs=[pl.BlockSpec(memory_space=pltpu.VMEM)],
        out_specs=pl.BlockSpec(memory_space=pl.ANY),
        scratch_shapes=[
            pltpu.SemaphoreType.DMA(((size - 1) * GATHER_PARTS,)),
            pltpu.SemaphoreType.DMA((size * GATHER_PARTS,)),
            pltpu.SemaphoreType.DMA,
        ],
        compiler_params=pltpu.CompilerParams(collective_id=0, has_side_effects=True),
    )(x)


def expert_half(slot_rows, gate_half, up_half, down_half):
    contract_rows = (((1,), (1,)), ((), ()))
    gate_t = lax.dot_general(
        gate_half, slot_rows, contract_rows, preferred_element_type=jnp.float32
    )
    up_t = lax.dot_general(up_half, slot_rows, contract_rows, preferred_element_type=jnp.float32)
    hidden = (jax.nn.silu(gate_t) * up_t).astype(jnp.bfloat16)
    product = lax.dot_general(
        hidden, down_half, (((0,), (0,)), ((), ())), preferred_element_type=jnp.float32
    )
    return product.astype(jnp.bfloat16)


def shards(
    table_cells,
    w_query,
    w_key,
    w_value,
    w_out,
    norm_gain,
    w_gate,
    w_up,
    w_down,
    lengths,
    expert_of_cell,
    slot_of_cell,
):
    cell_count, tables, model_width = table_cells.shape
    head_width = w_query.shape[1]
    head_count = head_width // DH
    score_scale = 1.0 / math.sqrt(DH)
    cells_flat = table_cells.reshape(cell_count * tables, model_width)
    head_size = lax.axis_size("head")
    flat_rows = head_gather(cells_flat, head_size).reshape(
        head_size * cells_flat.shape[0], model_width
    )
    row_cells = flat_rows.shape[0] // tables
    q_all = (
        jnp.dot(flat_rows, w_query, preferred_element_type=jnp.float32)
        .astype(jnp.bfloat16)
        .reshape(row_cells, tables * head_width)
    )
    kv_weight = jnp.concatenate([w_key, w_value], axis=1)
    kv_rows = (
        jnp.dot(flat_rows, kv_weight, preferred_element_type=jnp.float32)
        .astype(jnp.bfloat16)
        .reshape(row_cells, tables * 2 * head_width)
    )
    kv_all = lax.all_gather(kv_rows, "expert", axis=0, tiled=True)
    offset = lax.axis_index("expert") * row_cells
    scalars = jnp.concatenate(
        [lengths.astype(jnp.int32), jnp.reshape(offset, (1,)).astype(jnp.int32)]
    )
    attended = flash_attention(scalars, q_all, kv_all, head_count, score_scale)
    head_size = lax.axis_size("head")
    me_head = lax.axis_index("head")
    w_parts = [w_out]
    for shift in range(1, head_size):
        w_parts.append(
            lax.ppermute(
                w_out, "head", [(index, (index + shift) % head_size) for index in range(head_size)]
            )
        )
    w_rel = jnp.concatenate(w_parts, axis=0)
    by_owner = lax.all_to_all(
        attended.reshape(head_size, cell_count, tables, head_width), "head", 0, 0, tiled=True
    )
    groups_rel = (me_head - jnp.arange(head_size)) % head_size
    rel = jnp.take(by_owner, groups_rel, axis=0).transpose(1, 2, 0, 3)
    summed = jnp.dot(
        rel.reshape(cell_count * tables, head_size * head_width),
        w_rel,
        preferred_element_type=jnp.float32,
    )
    residual = cells_flat.astype(jnp.float32) + summed
    mean_square = jnp.mean(residual * residual, axis=-1, keepdims=True)
    normed = (residual * lax.rsqrt(mean_square + 1e-06) * norm_gain.astype(jnp.float32)).astype(
        jnp.bfloat16
    )
    rows_dev = cell_count * tables
    normed_rows = normed.reshape(rows_dev, model_width)
    expert_count = lax.axis_size("expert") * lax.axis_size("head") // 2
    slot_cap = 2 * max(1, rows_dev // expert_count)
    target = expert_of_cell.reshape(rows_dev) * slot_cap + slot_of_cell.reshape(rows_dev)
    slot_table = (
        jnp.arange(expert_count * slot_cap, dtype=jnp.int32)[:, None] == target[None, :]
    ).astype(jnp.bfloat16)
    send_rows = jnp.dot(slot_table, normed_rows, preferred_element_type=jnp.float32).astype(
        jnp.bfloat16
    )
    gate_half = w_gate[0]
    up_half = w_up[0]
    down_half = w_down[0]
    pieces = 2
    received = lax.all_to_all(send_rows, ("expert", "head"), 0, 0, tiled=True)
    swap = [(index, index ^ 1) for index in range(lax.axis_size("head"))]
    from_partner = lax.ppermute(received, "head", swap)
    both = jnp.concatenate([received, from_partner], axis=0)
    half_out = expert_half(both, gate_half, up_half, down_half)
    mine = half_out[: received.shape[0]]
    theirs = lax.ppermute(half_out[received.shape[0] :], "head", swap)
    summed_halves = (mine.astype(jnp.float32) + theirs.astype(jnp.float32)).astype(jnp.bfloat16)
    combined = lax.all_to_all(summed_halves, ("expert", "head"), 0, 0, tiled=True)
    expert_out = lax.dot_general(
        slot_table, combined, (((0,), (0,)), ((), ())), preferred_element_type=jnp.float32
    )
    updated = (residual.reshape(rows_dev, model_width) + expert_out).astype(jnp.bfloat16)
    return updated.reshape(cell_count, tables, model_width)


def solution(mesh):
    placed = (
        P(("expert", "head"), None, None),
        P(None, "head"),
        P(None, "head"),
        P(None, "head"),
        P("head", None),
        P(),
        P(("expert", "head"), None, None),
        P(("expert", "head"), None, None),
        P(("expert", "head"), None, None),
        P(),
        P(("expert", "head"), None),
        P(("expert", "head"), None),
    )
    return jax.shard_map(
        shards,
        mesh=mesh,
        in_specs=placed,
        out_specs=P(("expert", "head"), None, None),
        check_vma=False,
    )
```
